128 devices in a mesh: pb: 64 (over z, y, x), ka: 2 (over core).
Axes of the slice: x: 4, y: 4, z: 4, core: 2. Of those that a mesh axis runs over, the one named last changes fastest.
Arguments:
- query_tokens: bfloat16 [65536, 768], P(('pb', 'ka')), may hold values from -272 to 272
- source_tokens: bfloat16 [3, 16384, 768], P(None, ('pb', 'ka')), may hold values from -6 to 6
- w_query: bfloat16 [768, 768], replicated, may hold values from -0.21875 to 0.21875
- w_keyval: bfloat16 [768, 1536], replicated, may hold values from -0.21875 to 0.21875
- w_out: bfloat16 [768, 768], replicated, may hold values from -0.21875 to 0.21875
- slab_map: int32 [3, 128], replicated, may hold values from 0 to 127, as said below
- neighbours: int32 [512, 2, 6], P(('pb', 'ka')), may hold values from 0 to 383, as said below
- counts: int32 [512, 2], P(('pb', 'ka')), may hold values from 1 to 6, as said below
Outputs:
- output: bfloat16 [65536, 768], P(('pb', 'ka'))
The draws below stay inside these ranges and needn't reach their ends.
Inputs may be any that keep to these rules, and one draw needn't show every extreme that they name: Each row slab_map[c] is a permutation of the key blocks. neighbours[q, a, j] = c * 128 + b names contrast c and key block b whose stored block s has (s) % 2 == a; a query slab is 8 query blocks in a row; over all entries (live or not) of one query slab and one slab a, the named blocks are distinct and at most 1 of them have the same s // 2, a bound reached in every draw. Only the first counts[q, a] entries of neighbours[q, a] are listed.
All inputs are finite; a program needn't handle non-finite values.
Results may differ from the reference program's by a relative error of at most 0.024.
The reference program's roundings to bfloat16 on the way (of `queries`, `keyval`, `weights` and `attended`) count: a program that leaves them out, or rounds other values in their place, can miss the bound.
Values may be sent and summed in bfloat16 or wider, within the bound.
No kernel may reach another device: no remote copies, remote signals or barrier semaphores. Data moves between devices by JAX's collectives and lax.ppermute only.
A program may use at most 192 MiB of HBM per device.

```python
import jax
import jax.numpy as jnp
from jax import lax

D = 768
HEADS = 12
HEAD_DIM = 64
BLK = 128
SOURCES = 3
QB_DEV = 4
KB_DEV = 1
CAP = 6
QBLOCKS = 512
KBLOCKS = 128
TQ = 65536
TK = 16384
N_PB = 64
N_KA = 2


def layout_tables(key):
    tables = [jax.random.permutation(jax.random.fold_in(key, 11 + source), KBLOCKS) for source in range(SOURCES)]
    perms = jnp.stack(tables).astype(jnp.int32)
    inverse = jnp.argsort(perms, axis=1).astype(jnp.int32)
    per_owner = SOURCES * KB_DEV
    slab_blocks = QB_DEV * N_KA
    requests = slab_blocks * CAP
    pair_keys = jax.random.split(jax.random.fold_in(key, 23), N_PB * N_KA)

    def choose(subkey):
        owner_perm = jax.random.permutation(jax.random.fold_in(subkey, 1), N_PB).astype(jnp.int32)
        block_keys = jax.random.split(jax.random.fold_in(subkey, 2), N_PB)
        block_perms = jax.vmap(lambda one: jax.random.permutation(one, per_owner))(block_keys).astype(jnp.int32)
        order = jnp.arange(requests, dtype=jnp.int32)
        owner = owner_perm[order % N_PB]
        local = block_perms[owner, order // N_PB]
        return (owner, local)
    owners, locals_ = jax.vmap(choose)(pair_keys)
    owners = owners.reshape(N_PB, N_KA, requests)
    locals_ = locals_.reshape(N_PB, N_KA, requests)
    slab_index = jnp.arange(N_KA, dtype=jnp.int32)[None, :, None]
    contrast = locals_ // KB_DEV
    stored = (owners * N_KA + slab_index) * KB_DEV + locals_ % KB_DEV
    logical = inverse[contrast, stored]
    listed = (contrast * KBLOCKS + logical).astype(jnp.int32)
    listed = listed.reshape(N_PB, N_KA, slab_blocks, CAP).transpose(0, 2, 1, 3).reshape(QBLOCKS, N_KA, CAP)
    hottest = jax.random.randint(jax.random.fold_in(key, 31), (N_PB,), 0, N_KA)
    query_slab = jnp.arange(QBLOCKS, dtype=jnp.int32) // (QB_DEV * N_KA)
    baseline = jax.random.randint(jax.random.fold_in(key, 37), (QBLOCKS, N_KA), 1, CAP // 2 + 1)
    slab_ids = jnp.arange(N_KA, dtype=jnp.int32)[None, :]
    live_counts = jnp.where(slab_ids == hottest[query_slab][:, None], CAP, baseline).astype(jnp.int32)
    return (perms, listed.astype(jnp.int32), live_counts)


def draw_slab_map(key, part):
    return layout_tables(key)[0]


def draw_neighbours(key, part):
    return layout_tables(key)[1]


def draw_counts(key, part):
    return layout_tables(key)[2]


def draw_query_tokens(key, part):
    values = jnp.clip(jax.random.normal(jax.random.fold_in(key, 41), (TQ, D), jnp.float32), -4.0, 4.0)
    return values.astype(jnp.bfloat16)


def level_of(stream_key, extent, cuts, smallest, high):
    factor_of = 1.0
    for dim, blocks in cuts:
        steps = jax.random.uniform(jax.random.fold_in(jax.random.fold_in(stream_key, 6), dim), (blocks,), jnp.float32, smallest / len(cuts), high / len(cuts))
        factor_of = factor_of * jnp.repeat(jnp.exp(steps), extent[dim] // blocks).reshape((-1,) + (1,) * (len(extent) - 1 - dim))
    return factor_of


def centred(own_key, dims, scale, reach, shards=(), kind=jnp.bfloat16):
    values = scale * jax.random.normal(own_key, dims, jnp.float32)
    if shards:
        values = values * level_of(own_key, dims, shards, -0.22, 0.18)
    return jnp.clip(values, -reach, reach).astype(kind)


def setup_inputs(seed: int = 0) -> dict:
    splits = jax.random.split(jax.random.key(seed), 9)
    query_tokens = draw_query_tokens(jax.random.fold_in(splits[8], 71), 0)
    source_tokens = centred(splits[1], (SOURCES, TK, D), 1.0, 6.0, ((1, 128),))
    w_query = centred(splits[2], (D, D), D ** -0.5, 0.21875)
    w_keyval = centred(splits[3], (D, 2 * D), D ** -0.5, 0.21875)
    w_out = centred(splits[4], (D, D), D ** -0.5, 0.21875)
    slab_map = draw_slab_map(jax.random.fold_in(splits[8], 71), 0)
    neighbours = draw_neighbours(jax.random.fold_in(splits[8], 71), 0)
    counts = draw_counts(jax.random.fold_in(splits[8], 71), 0)
    return dict(query_tokens=query_tokens, source_tokens=source_tokens, w_query=w_query, w_keyval=w_keyval, w_out=w_out, slab_map=slab_map, neighbours=neighbours, counts=counts)


def reference(query_tokens, source_tokens, w_query, w_keyval, w_out, slab_map, neighbours, counts):
    queries = jnp.dot(query_tokens, w_query, preferred_element_type=jnp.float32).astype(jnp.bfloat16)
    flat_source = source_tokens.reshape(SOURCES * TK, D)
    keyval = jnp.dot(flat_source, w_keyval, preferred_element_type=jnp.float32).astype(jnp.bfloat16)
    keyval_blocks = keyval.reshape(SOURCES * KBLOCKS, BLK, 2 * D)
    entries = neighbours.reshape(QBLOCKS, N_KA * CAP).astype(jnp.int32)
    contrast = entries // KBLOCKS
    stored = slab_map.reshape(-1)[entries]
    block_rows = (contrast * KBLOCKS + stored).astype(jnp.int32)
    slot_ids = jnp.arange(CAP, dtype=jnp.int32)
    alive = (slot_ids[None, None, :] < counts[:, :, None]).reshape(QBLOCKS, N_KA * CAP)
    query_blocks = queries.reshape(QBLOCKS, BLK, HEADS, HEAD_DIM)
    scale = HEAD_DIM ** -0.5

    def one_block(inputs):
        query_part, picked_rows, living = inputs
        picked = keyval_blocks[picked_rows]
        key_part = picked[:, :, :D].reshape(N_KA * CAP * BLK, HEADS, HEAD_DIM)
        value_part = picked[:, :, D:].reshape(N_KA * CAP * BLK, HEADS, HEAD_DIM)
        scores = jnp.einsum("ihd,jhd->hij", query_part.astype(jnp.float32), key_part.astype(jnp.float32)) * scale
        keep = jnp.repeat(living, BLK)
        scores = jnp.where(keep[None, None, :], scores, -jnp.inf)
        peak = jnp.max(scores, axis=2, keepdims=True)
        expo = jnp.exp(scores - peak)
        totals = jnp.sum(expo, axis=2)
        weights = expo.astype(jnp.bfloat16)
        mixed = jnp.einsum("hij,jhd->ihd", weights.astype(jnp.float32), value_part.astype(jnp.float32))
        attended = mixed / jnp.transpose(totals)[:, :, None]
        return attended.reshape(BLK, D).astype(jnp.bfloat16)

    attended = lax.map(one_block, (query_blocks, block_rows, alive)).reshape(TQ, D)
    return jnp.dot(attended, w_out, preferred_element_type=jnp.float32).astype(jnp.bfloat16)
```

```python
import jax
import jax.numpy as jnp
from jax import lax
from jax.experimental import pallas as pl
from jax.experimental.pallas import tpu as pltpu
from jax.sharding import PartitionSpec as P

HEADS = 12
HEAD_DIM = 64
BLK = 128
CAP = 6
WIDTH = HEADS * HEAD_DIM
PARTS = 3
CUT = WIDTH // PARTS
SIDE = 4
PAIRS = HEADS // 2
BF = jnp.bfloat16
F32 = jnp.float32
I32 = jnp.int32
STRIDE = (SIDE * SIDE, SIDE, 1)
ROUTES = ((2, 0, 1), (1, 2, 0), (0, 1, 2))
LOG2E = 1.4426950408889634


ANY = pl.BlockSpec(memory_space=pl.ANY)
SMEM = pl.BlockSpec(memory_space=pltpu.SMEM)
VMEM = pl.BlockSpec(memory_space=pltpu.VMEM)


def shift(value, axis, step):
    stride = STRIDE[axis]
    pairs = []
    for source in range(SIDE**3):
        at = source // stride % SIDE
        pairs.append((source, source + ((at + step) % SIDE - at) * stride))
    return lax.ppermute(value, "pb", pairs)


def swap(value):
    return lax.ppermute(value, "ka", [(0, 1), (1, 0)])


def table_kernel(blocks, me_ref, near_ref, count_ref, map_ref, out_ref):
    def clear(i, _):
        out_ref[0, i] = 0
        out_ref[1, i] = -1
        return 0

    lax.fori_loop(0, 128, clear, 0)
    key_blocks = map_ref.shape[0] // PARTS

    def fill(i, _):
        slab = i // (blocks * CAP)
        q = i // CAP % blocks
        j = i % CAP

        @pl.when(j < count_ref[q * 2 + slab])
        def _():
            entry = near_ref[(q * 2 + slab) * CAP + j]
            owner = map_ref[entry] // 2
            out_ref[0, slab * 64 + owner] = entry // key_blocks + 1
            dz = (me_ref[0] - owner // 16 + 4) % 4
            dy = (me_ref[1] - owner // 4 % 4 + 4) % 4
            dx = (me_ref[2] - owner % 4 + 4) % 4
            out_ref[1, i] = dz * 16 + dy * 4 + dx

        return 0

    lax.fori_loop(0, 2 * blocks * CAP, fill, 0)


def select_kernel(me_ref, *refs):
    tables = refs[:10]
    gathered = [refs[10 + 4 * part : 14 + 4 * part] for part in range(PARTS)]
    outs = [refs[22 + 4 * part : 26 + 4 * part] for part in range(PARTS)]
    sems = refs[34]

    def each(run):
        def body(d1, _):
            for part, (across, first, second) in enumerate(ROUTES):
                for d2 in range(SIDE):
                    at = [None, None, None]
                    at[across] = me_ref[across]
                    at[first] = (me_ref[first] - d1 + 4) % 4
                    at[second] = (me_ref[second] - d2 + 4) % 4
                    place = me_ref[3] * 64 + at[0] * 16 + at[1] * 4 + at[2]
                    for d in range(SIDE):
                        table = tables[0] if d == 0 else tables[1 + part * 3 + d - 1]
                        which = table[0, place]

                        @pl.when(which > 0)
                        def _():
                            run(
                                pltpu.make_async_copy(
                                    gathered[part][d2].at[d1, jnp.maximum(which - 1, 0)],
                                    outs[part][d].at[d2 * 4 + d1],
                                    sems.at[part, d, d2, d1],
                                )
                            )

            return 0

        lax.fori_loop(0, SIDE, body, 0)

    each(lambda copy: copy.start())
    each(lambda copy: copy.wait())


def fetch_parts(code, arrived, target, sem_of):
    away = (code // 16, code // 4 % 4, code % 4)
    for part, (across, first, second) in enumerate(ROUTES):
        for d in range(SIDE):

            @pl.when(away[across] == d)
            def _():
                pltpu.make_async_copy(
                    arrived[part][d].at[away[second] * 4 + away[first]],
                    target(part),
                    sem_of(part),
                ).start()


def hand_kernel(me_ref, code_ref, *refs):
    arrived = [refs[4 * part : 4 + 4 * part] for part in range(PARTS)]
    out = refs[12]
    sems = refs[13]
    count = out.shape[0]

    def start(i, _):
        code = code_ref[1, me_ref[3] * count + i]

        @pl.when(code >= 0)
        def _():
            fetch_parts(
                jnp.maximum(code, 0),
                arrived,
                lambda part: out.at[i, :, pl.ds(part * CUT, CUT)],
                lambda part: sems.at[i, part],
            )

        return 0

    def finish(i, _):
        @pl.when(code_ref[1, me_ref[3] * count + i] >= 0)
        def _():
            for part in range(PARTS):
                pltpu.make_async_copy(
                    arrived[part][0].at[0],
                    out.at[i, :, pl.ds(part * CUT, CUT)],
                    sems.at[i, part],
                ).wait()

        return 0

    lax.fori_loop(0, count, start, 0)
    lax.fori_loop(0, count, finish, 0)


def attend_kernel(me_ref, code_ref, count_ref, xq_ref, wq_ref, wk_ref, wvt_ref, wo_ref, *refs):
    arrived = [refs[4 * part : 4 + 4 * part] for part in range(PARTS)]
    handed = refs[12]
    out_ref = refs[13]
    item_q, item_a, item_b, item_n = refs[14:18]
    tokens, keys, values, spread, peak, total, sums, sems = refs[18:]
    blocks = xq_ref.shape[0] // BLK
    mine = me_ref[3]
    span = blocks * CAP

    def plan_block(q, begun):
        own = count_ref[q * 2 + mine]
        other = count_ref[q * 2 + 1 - mine]
        live = own + other

        def code_of(i):
            near = code_ref[1, mine * span + q * CAP + jnp.minimum(i, own - 1)]
            far = 64 + q * CAP + jnp.maximum(i - own, 0)
            return jnp.where(i < own, near, far)

        def plan_item(k, _):
            t = begun + k
            item_q[t] = q
            item_a[t] = code_of(2 * k)
            item_b[t] = code_of(jnp.minimum(2 * k + 1, live - 1))
            item_n[t] = live - 2 * k
            return 0

        items = (live + 1) // 2
        lax.fori_loop(0, items, plan_item, 0)
        return begun + items

    steps = lax.fori_loop(0, blocks, plan_block, 0)

    def fetch(t):
        slot = t % 2
        for half, codes in enumerate((item_a, item_b)):
            code = codes[t]
            rows = pl.ds(half * BLK, BLK)

            @pl.when(code < 64)
            def _():
                fetch_parts(
                    code,
                    arrived,
                    lambda part: tokens.at[slot, rows, pl.ds(part * CUT, CUT)],
                    lambda part: sems.at[slot],
                )

            @pl.when(code >= 64)
            def _():
                pltpu.make_async_copy(
                    handed.at[jnp.maximum(code - 64, 0)], tokens.at[slot, rows], sems.at[slot]
                ).start()

    fetch(0)

    def step(t, before):
        slot = t % 2
        q = item_q[t]

        @pl.when(t + 1 < steps)
        def _():
            fetch(t + 1)

        @pl.when(q != before)
        def _():
            rows = xq_ref[pl.ds(pl.multiple_of(q * BLK, BLK), BLK), :]
            queries = jnp.dot(rows, wq_ref[...], preferred_element_type=F32).astype(BF)
            low = lax.broadcasted_iota(I32, (BLK, BLK), 1) < HEAD_DIM
            zero = jnp.zeros((BLK, BLK), BF)
            for p in range(PAIRS):
                two = queries[:, p * BLK : (p + 1) * BLK]
                spread[p, :BLK, :] = jnp.where(low, two, zero)
                spread[p, BLK:, :] = jnp.where(low, zero, two)
            peak[...] = jnp.full_like(peak, -jnp.inf)
            total[...] = jnp.zeros_like(total)
            sums[...] = jnp.zeros_like(sums)

        pltpu.make_async_copy(tokens.at[slot], tokens.at[slot], sems.at[slot]).wait()
        both = tokens[slot]
        keys[...] = jnp.dot(both, wk_ref[...], preferred_element_type=F32).astype(BF)
        values[...] = lax.dot_general(
            wvt_ref[...], both, (((1,), (1,)), ((), ())), preferred_element_type=F32
        ).astype(BF)
        row = lax.broadcasted_iota(I32, (2 * BLK, 1), 0)
        bias = jnp.where(row < BLK * item_n[t], 0.0, -jnp.inf)
        for p in range(PAIRS):
            scores = lax.dot_general(
                keys[:, p * BLK : (p + 1) * BLK],
                spread[p],
                (((1,), (1,)), ((), ())),
                preferred_element_type=F32,
            )
            scores = scores * (HEAD_DIM**-0.5 * LOG2E) + bias
            old = peak[p : p + 1, :]
            new = jnp.maximum(old, jnp.max(scores, axis=0, keepdims=True))
            expo = jnp.exp2(scores - new)
            factor = jnp.exp2(old - new)
            peak[p : p + 1, :] = new
            total[p : p + 1, :] = total[p : p + 1, :] * factor + jnp.sum(
                expo, axis=0, keepdims=True
            )
            mixed = jnp.dot(
                values[p * BLK : (p + 1) * BLK, :], expo.astype(BF), preferred_element_type=F32
            )
            top = p * BLK
            mid = top + HEAD_DIM
            end = top + BLK
            sums[top:mid, :] = sums[top:mid, :] * factor[:, :BLK] + mixed[:HEAD_DIM, :BLK]
            sums[mid:end, :] = sums[mid:end, :] * factor[:, BLK:] + mixed[HEAD_DIM:, BLK:]

        @pl.when(item_n[t] <= 2)
        def _():
            done = []
            for p in range(PAIRS):
                for h in range(2):
                    top = p * BLK + h * HEAD_DIM
                    done.append(
                        sums[top : top + HEAD_DIM, :] / total[p : p + 1, h * BLK : (h + 1) * BLK]
                    )
            attended = jnp.transpose(jnp.concatenate(done, axis=0)).astype(BF)
            out_ref[pl.ds(pl.multiple_of(q * BLK, BLK), BLK), :] = jnp.dot(
                attended, wo_ref[...], preferred_element_type=F32
            ).astype(BF)

        return q

    lax.fori_loop(0, steps, step, -1)


def on_device(query_tokens, source_tokens, w_query, w_keyval, w_out, slab_map, neighbours, counts):
    blocks = neighbours.shape[0]
    place = lax.axis_index("pb").astype(I32)
    me = jnp.stack(
        [place // 16, place // 4 % 4, place % 4, lax.axis_index("ka").astype(I32)]
    )
    flat_counts = counts.reshape(-1)
    table = pl.pallas_call(
        lambda *refs: table_kernel(blocks, *refs),
        out_shape=jax.ShapeDtypeStruct((2, 128), I32),
        in_specs=[SMEM] * 4,
        out_specs=SMEM,
        name="tables",
    )(me, neighbours.reshape(-1), flat_counts, slab_map.reshape(-1))
    partner = swap(table)
    chip = table[:1] + partner[:1]

    gathered = []
    for part, (across, first, second) in enumerate(ROUTES):
        own = source_tokens[:, :, part * CUT : (part + 1) * CUT]
        line = jnp.stack([own] + [shift(own, first, d) for d in range(1, SIDE)])
        gathered.append([line] + [shift(line, second, d) for d in range(1, SIDE)])
    wanted = [
        shift(chip, across, -d) for across, _, _ in ROUTES for d in range(1, SIDE)
    ]
    slots = jax.ShapeDtypeStruct((SIDE * SIDE, BLK, CUT), BF)
    chosen = pl.pallas_call(
        select_kernel,
        out_shape=[slots] * 12,
        in_specs=[SMEM] * 11 + [ANY] * 12,
        out_specs=[ANY] * 12,
        scratch_shapes=[pltpu.SemaphoreType.DMA((PARTS, SIDE, SIDE, SIDE))],
        name="select",
    )(me, chip, *wanted, *[a for part in gathered for a in part])
    arrived = []
    for part, (across, _, _) in enumerate(ROUTES):
        arrived.append(chosen[4 * part])
        arrived += [shift(chosen[4 * part + d], across, d) for d in range(1, SIDE)]
    handed = pl.pallas_call(
        hand_kernel,
        out_shape=jax.ShapeDtypeStruct((blocks * CAP, BLK, WIDTH), BF),
        in_specs=[SMEM] * 2 + [ANY] * 12,
        out_specs=ANY,
        scratch_shapes=[pltpu.SemaphoreType.DMA((blocks * CAP, PARTS))],
        name="hand",
    )(me, partner, *arrived)
    handed = swap(handed)
    items = blocks * CAP
    return pl.pallas_call(
        attend_kernel,
        out_shape=jax.ShapeDtypeStruct(query_tokens.shape, BF),
        in_specs=[SMEM] * 3 + [VMEM] * 5 + [ANY] * 13,
        out_specs=VMEM,
        scratch_shapes=[pltpu.SMEM((items,), I32)] * 4
        + [
            pltpu.VMEM((2, 2 * BLK, WIDTH), BF),
            pltpu.VMEM((2 * BLK, WIDTH), BF),
            pltpu.VMEM((WIDTH, 2 * BLK), BF),
            pltpu.VMEM((PAIRS, 2 * BLK, BLK), BF),
            pltpu.VMEM((8, 2 * BLK), F32),
            pltpu.VMEM((8, 2 * BLK), F32),
            pltpu.VMEM((WIDTH, BLK), F32),
            pltpu.SemaphoreType.DMA((2,)),
        ],
        name="attend",
    )(
        me,
        table,
        flat_counts,
        query_tokens,
        w_query,
        w_keyval[:, :WIDTH],
        jnp.transpose(w_keyval[:, WIDTH:]),
        w_out,
        *arrived,
        handed,
    )


def solution(mesh):
    placed = (
        P(("pb", "ka"), None),
        P(None, ("pb", "ka"), None),
        P(),
        P(),
        P(),
        P(),
        P(("pb", "ka"), None, None),
        P(("pb", "ka"), None),
    )
    return jax.shard_map(
        on_device, mesh=mesh, in_specs=placed, out_specs=P(("pb", "ka"), None), check_vma=False
    )
```

```python
import jax
import jax.numpy as jnp
from jax import lax
from jax.experimental import pallas as pl
from jax.experimental.pallas import tpu as pltpu
from jax.sharding import PartitionSpec as P

HEADS = 12
HEAD_DIM = 64
BLK = 128
CAP = 6
WIDTH = HEADS * HEAD_DIM
PARTS = 3
CUT = WIDTH // PARTS
SIDE = 4
PAIRS = HEADS // 2
BF = jnp.bfloat16
F32 = jnp.float32
I32 = jnp.int32
STRIDE = (SIDE * SIDE, SIDE, 1)
ROUTES = ((2, 0, 1), (1, 2, 0), (0, 1, 2))
LOG2E = 1.4426950408889634


ANY = pl.BlockSpec(memory_space=pl.ANY)
SMEM = pl.BlockSpec(memory_space=pltpu.SMEM)
VMEM = pl.BlockSpec(memory_space=pltpu.VMEM)


def shift(value, axis, step):
    stride = STRIDE[axis]
    pairs = []
    for source in range(SIDE**3):
        at = source // stride % SIDE
        pairs.append((source, source + ((at + step) % SIDE - at) * stride))
    return lax.ppermute(value, "pb", pairs)


def swap(value):
    return lax.ppermute(value, "ka", [(0, 1), (1, 0)])


def table_kernel(blocks, me_ref, near_ref, count_ref, map_ref, out_ref):
    def clear(i, _):
        out_ref[0, i] = 0
        out_ref[1, i] = -1
        return 0

    lax.fori_loop(0, 128, clear, 0)
    key_blocks = map_ref.shape[0] // PARTS

    def fill(i, _):
        slab = i // (blocks * CAP)
        q = i // CAP % blocks
        j = i % CAP

        @pl.when(j < count_ref[q * 2 + slab])
        def _():
            entry = near_ref[(q * 2 + slab) * CAP + j]
            owner = map_ref[entry] // 2
            out_ref[0, slab * 64 + owner] = entry // key_blocks + 1
            dz = (me_ref[0] - owner // 16 + 4) % 4
            dy = (me_ref[1] - owner // 4 % 4 + 4) % 4
            dx = (me_ref[2] - owner % 4 + 4) % 4
            out_ref[1, i] = dz * 16 + dy * 4 + dx

        return 0

    lax.fori_loop(0, 2 * blocks * CAP, fill, 0)


def select_kernel(me_ref, *refs):
    tables = refs[:10]
    gathered = [refs[10 + 4 * part : 14 + 4 * part] for part in range(PARTS)]
    outs = [refs[22 + 4 * part : 26 + 4 * part] for part in range(PARTS)]
    stage, sems, out_sems = refs[34:]

    def walk(part, d, run):
        across, first, second = ROUTES[part]
        table = tables[0] if d == 0 else tables[1 + part * 3 + d - 1]

        def body(slot, _):
            at = [None, None, None]
            at[across] = me_ref[across]
            at[first] = (me_ref[first] - slot + 16) % 4
            at[second] = (me_ref[second] - slot // 4 + 4) % 4
            which = table[0, me_ref[3] * 64 + at[0] * 16 + at[1] * 4 + at[2]]

            @pl.when(which > 0)
            def _():
                run(slot, jnp.maximum(which - 1, 0))

            return 0

        lax.fori_loop(0, SIDE * SIDE, body, 0)

    for part in range(PARTS):
        for d in range(SIDE):

            def begin(slot, which):
                for d2 in range(SIDE):

                    @pl.when(slot // 4 == d2)
                    def _():
                        pltpu.make_async_copy(
                            gathered[part][d2].at[slot % 4, which],
                            stage.at[part * 4 + d, slot],
                            sems.at[part * 4 + d, slot],
                        ).start()

            walk(part, d, begin)
    for part in range(PARTS):
        for d in range(SIDE):
            n = part * 4 + d

            def finish(slot, which):
                pltpu.make_async_copy(
                    gathered[part][0].at[0, 0], stage.at[n, slot], sems.at[n, slot]
                ).wait()

            walk(part, d, finish)
            pltpu.make_async_copy(stage.at[n], outs[part][d], out_sems.at[n]).start()
    for part in range(PARTS):
        for d in range(SIDE):
            n = part * 4 + d
            pltpu.make_async_copy(stage.at[n], outs[part][d], out_sems.at[n]).wait()


def fetch_parts(code, arrived, target, sem_of):
    away = (code // 16, code // 4 % 4, code % 4)
    for part, (across, first, second) in enumerate(ROUTES):
        for d in range(SIDE):

            @pl.when(away[across] == d)
            def _():
                pltpu.make_async_copy(
                    arrived[part][d].at[away[second] * 4 + away[first]],
                    target(part),
                    sem_of(part),
                ).start()


def hand_kernel(me_ref, code_ref, *refs):
    arrived = [refs[4 * part : 4 + 4 * part] for part in range(PARTS)]
    out, stage, sems, out_sems = refs[12:]
    count = out.shape[0]

    def start(i, _):
        code = code_ref[1, me_ref[3] * count + i]

        @pl.when(code >= 0)
        def _():
            fetch_parts(
                jnp.maximum(code, 0),
                arrived,
                lambda part: stage.at[i, :, pl.ds(part * CUT, CUT)],
                lambda part: sems.at[i, part],
            )

        return 0

    def finish(i, _):
        @pl.when(code_ref[1, me_ref[3] * count + i] >= 0)
        def _():
            for part in range(PARTS):
                pltpu.make_async_copy(
                    arrived[part][0].at[0],
                    stage.at[i, :, pl.ds(part * CUT, CUT)],
                    sems.at[i, part],
                ).wait()

        pltpu.make_async_copy(stage.at[i], out.at[i], out_sems.at[i]).start()
        return 0

    def close(i, _):
        pltpu.make_async_copy(stage.at[i], out.at[i], out_sems.at[i]).wait()
        return 0

    lax.fori_loop(0, count, start, 0)
    lax.fori_loop(0, count, finish, 0)
    lax.fori_loop(0, count, close, 0)


def attend_kernel(me_ref, code_ref, count_ref, xq_ref, wq_ref, wk_ref, wvt_ref, wo_ref, *refs):
    arrived = [refs[4 * part : 4 + 4 * part] for part in range(PARTS)]
    handed = refs[12]
    out_ref = refs[13]
    item_q, item_a, item_b, item_n = refs[14:18]
    tokens, keys, values, spread, peak, total, sums, sems = refs[18:]
    blocks = xq_ref.shape[0] // BLK
    mine = me_ref[3]
    span = blocks * CAP

    def plan_block(q, begun):
        own = count_ref[q * 2 + mine]
        other = count_ref[q * 2 + 1 - mine]
        live = own + other

        def code_of(i):
            near = code_ref[1, mine * span + q * CAP + jnp.minimum(i, own - 1)]
            far = 64 + q * CAP + jnp.maximum(i - own, 0)
            return jnp.where(i < own, near, far)

        def plan_item(k, _):
            t = begun + k
            item_q[t] = q
            item_a[t] = code_of(2 * k)
            item_b[t] = code_of(jnp.minimum(2 * k + 1, live - 1))
            item_n[t] = live - 2 * k
            return 0

        items = (live + 1) // 2
        lax.fori_loop(0, items, plan_item, 0)
        return begun + items

    steps = lax.fori_loop(0, blocks, plan_block, 0)

    def fetch(t):
        slot = t % 2
        for half, codes in enumerate((item_a, item_b)):
            code = codes[t]
            rows = pl.ds(half * BLK, BLK)

            @pl.when(code < 64)
            def _():
                fetch_parts(
                    code,
                    arrived,
                    lambda part: tokens.at[slot, rows, pl.ds(part * CUT, CUT)],
                    lambda part: sems.at[slot],
                )

            @pl.when(code >= 64)
            def _():
                pltpu.make_async_copy(
                    handed.at[jnp.maximum(code - 64, 0)], tokens.at[slot, rows], sems.at[slot]
                ).start()

    fetch(0)

    def step(t, before):
        slot = t % 2
        q = item_q[t]

        @pl.when(t + 1 < steps)
        def _():
            fetch(t + 1)

        @pl.when(q != before)
        def _():
            rows = xq_ref[pl.ds(pl.multiple_of(q * BLK, BLK), BLK), :]
            queries = jnp.dot(rows, wq_ref[...], preferred_element_type=F32).astype(BF)
            low = lax.broadcasted_iota(I32, (BLK, BLK), 1) < HEAD_DIM
            zero = jnp.zeros((BLK, BLK), BF)
            for p in range(PAIRS):
                two = queries[:, p * BLK : (p + 1) * BLK]
                spread[p, :BLK, :] = jnp.where(low, two, zero)
                spread[p, BLK:, :] = jnp.where(low, zero, two)
            peak[...] = jnp.full_like(peak, -jnp.inf)
            total[...] = jnp.zeros_like(total)
            sums[...] = jnp.zeros_like(sums)

        pltpu.make_async_copy(tokens.at[slot], tokens.at[slot], sems.at[slot]).wait()
        both = tokens[slot]
        keys[...] = jnp.dot(both, wk_ref[...], preferred_element_type=F32).astype(BF)
        values[...] = lax.dot_general(
            wvt_ref[...], both, (((1,), (1,)), ((), ())), preferred_element_type=F32
        ).astype(BF)
        row = lax.broadcasted_iota(I32, (2 * BLK, 1), 0)
        bias = jnp.where(row < BLK * item_n[t], 0.0, -jnp.inf)
        for p in range(PAIRS):
            scores = lax.dot_general(
                keys[:, p * BLK : (p + 1) * BLK],
                spread[p],
                (((1,), (1,)), ((), ())),
                preferred_element_type=F32,
            )
            scores = scores * (HEAD_DIM**-0.5 * LOG2E) + bias
            old = peak[p : p + 1, :]
            new = jnp.maximum(old, jnp.max(scores, axis=0, keepdims=True))
            expo = jnp.exp2(scores - new)
            factor = jnp.exp2(old - new)
            peak[p : p + 1, :] = new
            total[p : p + 1, :] = total[p : p + 1, :] * factor + jnp.sum(
                expo, axis=0, keepdims=True
            )
            mixed = jnp.dot(
                values[p * BLK : (p + 1) * BLK, :], expo.astype(BF), preferred_element_type=F32
            )
            top = p * BLK
            mid = top + HEAD_DIM
            end = top + BLK
            sums[top:mid, :] = sums[top:mid, :] * factor[:, :BLK] + mixed[:HEAD_DIM, :BLK]
            sums[mid:end, :] = sums[mid:end, :] * factor[:, BLK:] + mixed[HEAD_DIM:, BLK:]

        @pl.when(item_n[t] <= 2)
        def _():
            done = []
            for p in range(PAIRS):
                for h in range(2):
                    top = p * BLK + h * HEAD_DIM
                    done.append(
                        sums[top : top + HEAD_DIM, :] / total[p : p + 1, h * BLK : (h + 1) * BLK]
                    )
            attended = jnp.transpose(jnp.concatenate(done, axis=0)).astype(BF)
            out_ref[pl.ds(pl.multiple_of(q * BLK, BLK), BLK), :] = jnp.dot(
                attended, wo_ref[...], preferred_element_type=F32
            ).astype(BF)

        return q

    lax.fori_loop(0, steps, step, -1)


def on_device(query_tokens, source_tokens, w_query, w_keyval, w_out, slab_map, neighbours, counts):
    blocks = neighbours.shape[0]
    place = lax.axis_index("pb").astype(I32)
    me = jnp.stack(
        [place // 16, place // 4 % 4, place % 4, lax.axis_index("ka").astype(I32)]
    )
    flat_counts = counts.reshape(-1)
    table = pl.pallas_call(
        lambda *refs: table_kernel(blocks, *refs),
        out_shape=jax.ShapeDtypeStruct((2, 128), I32),
        in_specs=[SMEM] * 4,
        out_specs=SMEM,
        name="tables",
    )(me, neighbours.reshape(-1), flat_counts, slab_map.reshape(-1))
    partner = swap(table)
    chip = table[:1] + partner[:1]

    gathered = []
    for part, (across, first, second) in enumerate(ROUTES):
        own = source_tokens[:, :, part * CUT : (part + 1) * CUT]
        line = jnp.stack([own] + [shift(own, first, d) for d in range(1, SIDE)])
        line, chip = lax.optimization_barrier((line, chip))
        gathered.append([line] + [shift(line, second, d) for d in range(1, SIDE)])
    wanted = [
        shift(chip, across, -d) for across, _, _ in ROUTES for d in range(1, SIDE)
    ]
    slots = jax.ShapeDtypeStruct((SIDE * SIDE, BLK, CUT), BF)
    chosen = pl.pallas_call(
        select_kernel,
        out_shape=[slots] * 12,
        in_specs=[SMEM] * 11 + [ANY] * 12,
        out_specs=[ANY] * 12,
        scratch_shapes=[
            pltpu.VMEM((PARTS * SIDE, SIDE * SIDE, BLK, CUT), BF),
            pltpu.SemaphoreType.DMA((PARTS * SIDE, SIDE * SIDE)),
            pltpu.SemaphoreType.DMA((PARTS * SIDE,)),
        ],
        name="select",
    )(me, chip, *wanted, *[a for part in gathered for a in part])
    arrived = []
    for part, (across, _, _) in enumerate(ROUTES):
        arrived.append(chosen[4 * part])
        arrived += [shift(chosen[4 * part + d], across, d) for d in range(1, SIDE)]
    handed = pl.pallas_call(
        hand_kernel,
        out_shape=jax.ShapeDtypeStruct((blocks * CAP, BLK, WIDTH), BF),
        in_specs=[SMEM] * 2 + [ANY] * 12,
        out_specs=ANY,
        scratch_shapes=[
            pltpu.VMEM((blocks * CAP, BLK, WIDTH), BF),
            pltpu.SemaphoreType.DMA((blocks * CAP, PARTS)),
            pltpu.SemaphoreType.DMA((blocks * CAP,)),
        ],
        name="hand",
    )(me, partner, *arrived)
    handed = swap(handed)
    items = blocks * CAP
    return pl.pallas_call(
        attend_kernel,
        out_shape=jax.ShapeDtypeStruct(query_tokens.shape, BF),
        in_specs=[SMEM] * 3 + [VMEM] * 5 + [ANY] * 13,
        out_specs=VMEM,
        scratch_shapes=[pltpu.SMEM((items,), I32)] * 4
        + [
            pltpu.VMEM((2, 2 * BLK, WIDTH), BF),
            pltpu.VMEM((2 * BLK, WIDTH), BF),
            pltpu.VMEM((WIDTH, 2 * BLK), BF),
            pltpu.VMEM((PAIRS, 2 * BLK, BLK), BF),
            pltpu.VMEM((8, 2 * BLK), F32),
            pltpu.VMEM((8, 2 * BLK), F32),
            pltpu.VMEM((WIDTH, BLK), F32),
            pltpu.SemaphoreType.DMA((2,)),
        ],
        name="attend",
    )(
        me,
        table,
        flat_counts,
        query_tokens,
        w_query,
        w_keyval[:, :WIDTH],
        jnp.transpose(w_keyval[:, WIDTH:]),
        w_out,
        *arrived,
        handed,
    )


def solution(mesh):
    placed = (
        P(("pb", "ka"), None),
        P(None, ("pb", "ka"), None),
        P(),
        P(),
        P(),
        P(),
        P(("pb", "ka"), None, None),
        P(("pb", "ka"), None),
    )
    return jax.shard_map(
        on_device, mesh=mesh, in_specs=placed, out_specs=P(("pb", "ka"), None), check_vma=False
    )
```

```python
import jax
import jax.numpy as jnp
from jax import lax
from jax.experimental import pallas as pl
from jax.experimental.pallas import tpu as pltpu
from jax.sharding import PartitionSpec as P

HEADS = 12
HEAD_DIM = 64
BLK = 128
CAP = 6
WIDTH = HEADS * HEAD_DIM
PARTS = 3
CUT = WIDTH // PARTS
SIDE = 4
PAIRS = HEADS // 2
HALVES = 1
ROWS = BLK // HALVES
GROUP = 2 * BLK // ROWS
ITEM = GROUP * ROWS
BF = jnp.bfloat16
F32 = jnp.float32
I32 = jnp.int32
STRIDE = (SIDE * SIDE, SIDE, 1)
ROUTES = ((2, 0, 1), (1, 2, 0), (0, 1, 2))
LOG2E = 1.4426950408889634


ANY = pl.BlockSpec(memory_space=pl.ANY)
SMEM = pl.BlockSpec(memory_space=pltpu.SMEM)
VMEM = pl.BlockSpec(memory_space=pltpu.VMEM)


def shift(value, axis, step):
    stride = STRIDE[axis]
    pairs = []
    for source in range(SIDE**3):
        at = source // stride % SIDE
        pairs.append((source, source + ((at + step) % SIDE - at) * stride))
    return lax.ppermute(value, "pb", pairs)


def swap(value):
    return lax.ppermute(value, "ka", [(0, 1), (1, 0)])


def table_kernel(blocks, me_ref, near_ref, count_ref, map_ref, out_ref):
    def clear(i, _):
        for k in range(8):
            out_ref[0, i * 8 + k] = 0
            out_ref[1, i * 8 + k] = -1
        return 0

    lax.fori_loop(0, 16, clear, 0)
    key_blocks = map_ref.shape[0] // PARTS
    mine = me_ref[0] * 16 + me_ref[1] * 4 + me_ref[2]
    for slab in range(2):
        for q in range(blocks):
            live = count_ref[q * 2 + slab]
            for j in range(CAP):

                @pl.when(j < live)
                def _():
                    entry = near_ref[(q * 2 + slab) * CAP + j]
                    owner = lax.shift_right_logical(map_ref[entry], 1)
                    one = (entry >= key_blocks).astype(I32)
                    two = (entry >= 2 * key_blocks).astype(I32)
                    out_ref[0, slab * 64 + owner] = 1 + one + two
                    away = (mine & 48) + 64 - (owner & 48) & 48
                    away = away | ((mine & 12) + 16 - (owner & 12) & 12)
                    away = away | ((mine & 3) + 4 - (owner & 3) & 3)
                    out_ref[1, (slab * blocks + q) * CAP + j] = away


def select_kernel(me_ref, *refs):
    tables = refs[:10]
    gathered = [refs[10 + 4 * part : 14 + 4 * part] for part in range(PARTS)]
    outs = [[refs[22 + half * 12 + 4 * part :][:4] for part in range(PARTS)] for half in range(HALVES)]
    sems = refs[22 + 12 * HALVES]
    for half in range(HALVES):
        for part, (across, first, second) in enumerate(ROUTES):
            for d2 in range(SIDE):
                for d1 in range(SIDE):
                    at = [None, None, None]
                    at[across] = me_ref[across]
                    at[first] = me_ref[first] + 4 - d1 & 3
                    at[second] = me_ref[second] + 4 - d2 & 3
                    place = me_ref[3] * 64 + at[0] * 16 + at[1] * 4 + at[2]
                    for d in range(SIDE):
                        table = tables[0] if d == 0 else tables[1 + part * 3 + d - 1]
                        which = jnp.maximum(table[0, place] - 1, 0)
                        pltpu.make_async_copy(
                            gathered[part][d2].at[d1, which, pl.ds(half * ROWS, ROWS)],
                            outs[half][part][d].at[d2 * 4 + d1],
                            sems.at[half * 12 + part * 4 + d],
                        ).start()
    for half in range(HALVES):
        for part in range(PARTS):
            for d in range(SIDE):
                out = outs[half][part][d]
                pltpu.make_async_copy(out, out, sems.at[half * 12 + part * 4 + d]).wait()


def fetch_parts(code, arrived, target, sem_of):
    away = (lax.shift_right_logical(code, 4), lax.shift_right_logical(code, 2) & 3, code & 3)
    for part, (across, first, second) in enumerate(ROUTES):
        for d in range(SIDE):

            @pl.when(away[across] == d)
            def _():
                pltpu.make_async_copy(
                    arrived[part][d].at[away[second] * 4 + away[first]],
                    target(part),
                    sem_of(part),
                ).start()


def hand_kernel(me_ref, code_ref, *refs):
    arrived = [refs[4 * part : 4 + 4 * part] for part in range(PARTS)]
    out, stage, sems, out_sems = refs[12:]
    count = out.shape[0]

    def start(i, _):
        code = code_ref[1, me_ref[3] * count + i]

        @pl.when(code >= 0)
        def _():
            fetch_parts(
                jnp.maximum(code, 0),
                arrived,
                lambda part: stage.at[i, :, pl.ds(part * CUT, CUT)],
                lambda part: sems.at[i, part],
            )

        return 0

    def finish(i, _):
        @pl.when(code_ref[1, me_ref[3] * count + i] >= 0)
        def _():
            for part in range(PARTS):
                pltpu.make_async_copy(
                    arrived[part][0].at[0],
                    stage.at[i, :, pl.ds(part * CUT, CUT)],
                    sems.at[i, part],
                ).wait()

        pltpu.make_async_copy(stage.at[i], out.at[i], out_sems.at[i]).start()
        return 0

    def close(i, _):
        pltpu.make_async_copy(stage.at[i], out.at[i], out_sems.at[i]).wait()
        return 0

    lax.fori_loop(0, count, start, 0)
    lax.fori_loop(0, count, finish, 0)
    lax.fori_loop(0, count, close, 0)


def attend_kernel(first, last, *refs):
    refs = list(refs)
    me_ref, code_ref, count_ref, xq_ref, wq_ref, wk_ref, wvt_ref, wo_ref = refs[:8]
    arrived = [refs[8 + 4 * part : 12 + 4 * part] for part in range(PARTS)]
    handed = refs[20]
    refs = refs[21:]
    if not first:
        before = refs[:3]
        refs = refs[3:]
    if last:
        out_ref = refs.pop(0)
        peak, total, sums = refs[-3:]
    else:
        peak, total, sums = refs[:3]
        refs = refs[3:]
    item_q, item_n, item_code, tokens, keys, values, spread, sems = refs[:8]
    blocks = xq_ref.shape[0] // BLK
    mine = me_ref[3]
    span = blocks * CAP

    def plan_block(q, begun):
        own = count_ref[q * 2 + mine]
        live = own + count_ref[q * 2 + 1 - mine]

        def plan_item(k, _):
            t = begun + k
            item_q[t] = q
            item_n[t] = live - GROUP * k
            for g in range(GROUP):
                i = jnp.where(GROUP * k + g < live, GROUP * k + g, GROUP * k)
                near = code_ref[1, mine * span + q * CAP + jnp.minimum(i, own - 1)]
                item_code[t * GROUP + g] = jnp.where(i < own, near, 64 + q * CAP + i - own)
            return 0

        items = lax.div(live + GROUP - 1, GROUP)
        lax.fori_loop(0, items, plan_item, 0)
        return begun + items

    steps = lax.fori_loop(0, blocks, plan_block, 0)

    def fetch(t):
        slot = t & 1
        for g in range(GROUP):
            code = item_code[t * GROUP + g]
            rows = pl.ds(g * ROWS, ROWS)

            @pl.when(code < 64)
            def _():
                fetch_parts(
                    code,
                    arrived,
                    lambda part: tokens.at[slot, rows, pl.ds(part * CUT, CUT)],
                    lambda part: sems.at[slot],
                )

            @pl.when(code >= 64)
            def _():
                pltpu.make_async_copy(
                    handed.at[jnp.maximum(code - 64, 0)], tokens.at[slot, rows], sems.at[slot]
                ).start()

    def landed(slot):
        pltpu.make_async_copy(tokens.at[slot], tokens.at[slot], sems.at[slot]).wait()

    def project(slot, chunk):
        part = pl.ds(chunk % 3 * CUT, CUT)
        if chunk < 3:
            keys[slot, :, part] = jnp.dot(
                tokens[slot], wk_ref[:, part], preferred_element_type=F32
            ).astype(BF)
        else:
            values[slot, part, :] = lax.dot_general(
                wvt_ref[part, :],
                tokens[slot],
                (((1,), (1,)), ((), ())),
                preferred_element_type=F32,
            ).astype(BF)

    fetch(0)
    fetch(1)
    low = lax.broadcasted_iota(I32, (BLK, BLK), 1) < HEAD_DIM
    zero = jnp.zeros((BLK, BLK), BF)
    for q in range(blocks):
        queries = jnp.dot(
            xq_ref[q * BLK : (q + 1) * BLK, :], wq_ref[...], preferred_element_type=F32
        ).astype(BF)
        for p in range(PAIRS):
            two = queries[:, p * BLK : (p + 1) * BLK]
            spread[q, p, :BLK, :] = jnp.where(low, two, zero)
            spread[q, p, BLK:, :] = jnp.where(low, zero, two)
    if first:
        peak[...] = jnp.full_like(peak, -jnp.inf)
        total[...] = jnp.zeros_like(total)
        sums[...] = jnp.zeros_like(sums)
    else:
        for mine_ref, old_ref in zip((peak, total, sums), before):
            mine_ref[...] = old_ref[...]
    landed(0)
    for chunk in range(6):
        project(0, chunk)

    def step(t, _):
        slot = t & 1
        q = item_q[t]
        live = item_n[t]

        @pl.when(t + 2 < steps)
        def _():
            fetch(t + 2)

        for g in range(1, GROUP):

            @pl.when(live <= g)
            def _():
                values[slot, :, pl.ds(g * ROWS, ROWS)] = jnp.zeros((WIDTH, ROWS), BF)

        @pl.when(t + 1 < steps)
        def _():
            landed(1 - slot)

        scale = HEAD_DIM**-0.5 * LOG2E

        def score(p):
            return lax.dot_general(
                keys[slot, :, p * BLK : (p + 1) * BLK],
                spread[q, p],
                (((1,), (1,)), ((), ())),
                preferred_element_type=F32,
            )

        ahead = score(0)
        waiting = None
        for p in range(PAIRS + 1):
            scores = ahead
            if p + 1 < PAIRS:
                ahead = score(p + 1)
            if p % 2 == 0 and p < PAIRS:
                project(1 - slot, p // 2)
                project(1 - slot, 3 + p // 2)
            if waiting is not None:
                weights, factor = waiting
                top = (p - 1) * BLK
                mid = top + HEAD_DIM
                end = top + BLK
                mixed = jnp.dot(values[slot, top:end, :], weights, preferred_element_type=F32)
                sums[q, top:mid, :] = (
                    sums[q, top:mid, :] * factor[:, :BLK] + mixed[:HEAD_DIM, :BLK]
                )
                sums[q, mid:end, :] = (
                    sums[q, mid:end, :] * factor[:, BLK:] + mixed[HEAD_DIM:, BLK:]
                )
            if p < PAIRS:
                old = peak[q, p : p + 1, :]
                new = jnp.maximum(old, jnp.max(scores, axis=0, keepdims=True))
                expo = jnp.exp2((scores - new) * scale)
                factor = jnp.exp2((old - new) * scale)
                peak[q, p : p + 1, :] = new
                add = total[q, p : p + 1, :] * factor
                for g in range(GROUP):
                    some = jnp.sum(expo[g * ROWS : (g + 1) * ROWS], axis=0, keepdims=True)
                    add = add + (some if g == 0 else jnp.where(g < live, some, 0.0))
                total[q, p : p + 1, :] = add
                waiting = (expo.astype(BF), factor)
        return 0

    lax.fori_loop(0, steps, step, 0)
    if last:
        for q in range(blocks):
            done = []
            for p in range(PAIRS):
                for h in range(2):
                    top = p * BLK + h * HEAD_DIM
                    done.append(
                        sums[q, top : top + HEAD_DIM, :]
                        / total[q, p : p + 1, h * BLK : (h + 1) * BLK]
                    )
            attended = jnp.transpose(jnp.concatenate(done, axis=0)).astype(BF)
            out_ref[q * BLK : (q + 1) * BLK, :] = jnp.dot(
                attended, wo_ref[...], preferred_element_type=F32
            ).astype(BF)


def on_device(query_tokens, source_tokens, w_query, w_keyval, w_out, slab_map, neighbours, counts):
    blocks = neighbours.shape[0]
    place = lax.axis_index("pb").astype(I32)
    me = jnp.stack(
        [place // 16, place // 4 % 4, place % 4, lax.axis_index("ka").astype(I32)]
    )
    flat_counts = counts.reshape(-1)
    lines = []
    for part, (_, axis, _) in enumerate(ROUTES):
        own = source_tokens[:, :, part * CUT : (part + 1) * CUT]
        lines.append([own] + [shift(own, axis, d) for d in range(1, SIDE)])
    near, _ = lax.optimization_barrier((neighbours.reshape(-1), lines[0][1]))
    table = pl.pallas_call(
        lambda *refs: table_kernel(blocks, *refs),
        out_shape=jax.ShapeDtypeStruct((2, 128), I32),
        in_specs=[SMEM] * 4,
        out_specs=SMEM,
        name="tables",
    )(me, near, flat_counts, slab_map.reshape(-1))
    partner = swap(table)
    chip = table[:1] + partner[:1]

    gathered = []
    for part, (_, _, axis) in enumerate(ROUTES):
        line, chip = lax.optimization_barrier((jnp.stack(lines[part]), chip))
        gathered += [line] + [shift(line, axis, d) for d in range(1, SIDE)]
    wanted = [shift(chip, across, -d) for across, _, _ in ROUTES for d in range(1, SIDE)]
    slots = jax.ShapeDtypeStruct((SIDE * SIDE, ROWS, CUT), BF)
    chosen = pl.pallas_call(
        select_kernel,
        out_shape=[slots] * (12 * HALVES),
        in_specs=[SMEM] * 11 + [VMEM] * 12,
        out_specs=[ANY] * (12 * HALVES),
        scratch_shapes=[pltpu.SemaphoreType.DMA((12 * HALVES,))],
        name="select",
    )(me, chip, *wanted, *gathered)
    everything = []
    for half in range(HALVES):
        arrived = []
        for part, (across, _, _) in enumerate(ROUTES):
            ours = chosen[half * 12 + 4 * part :][:4]
            arrived += [ours[0]] + [shift(ours[d], across, d) for d in range(1, SIDE)]
        everything.append(arrived)
    state = [
        jax.ShapeDtypeStruct((blocks, 8, 2 * BLK), F32),
        jax.ShapeDtypeStruct((blocks, 8, 2 * BLK), F32),
        jax.ShapeDtypeStruct((blocks, WIDTH, BLK), F32),
    ]
    carried = []
    for half, arrived in enumerate(everything):
        handed = pl.pallas_call(
            hand_kernel,
            out_shape=jax.ShapeDtypeStruct((blocks * CAP, ROWS, WIDTH), BF),
            in_specs=[SMEM] * 2 + [ANY] * 12,
            out_specs=ANY,
            scratch_shapes=[
                pltpu.VMEM((blocks * CAP, ROWS, WIDTH), BF),
                pltpu.SemaphoreType.DMA((blocks * CAP, PARTS)),
                pltpu.SemaphoreType.DMA((blocks * CAP,)),
            ],
            name="hand",
        )(me, partner, *arrived)
        handed = swap(handed)
        first = half == 0
        last = half == HALVES - 1
        items = blocks * -(-2 * CAP // GROUP)
        carried = pl.pallas_call(
            lambda *refs: attend_kernel(first, last, *refs),
            out_shape=jax.ShapeDtypeStruct(query_tokens.shape, BF) if last else state,
            in_specs=[SMEM] * 3 + [VMEM] * 5 + [ANY] * 13 + [VMEM] * len(carried),
            out_specs=VMEM if last else [VMEM] * 3,
            scratch_shapes=[
                pltpu.SMEM((items,), I32),
                pltpu.SMEM((items,), I32),
                pltpu.SMEM((items * GROUP,), I32),
                pltpu.VMEM((2, ITEM, WIDTH), BF),
                pltpu.VMEM((2, ITEM, WIDTH), BF),
                pltpu.VMEM((2, WIDTH, ITEM), BF),
                pltpu.VMEM((blocks, PAIRS, 2 * BLK, BLK), BF),
                pltpu.SemaphoreType.DMA((2,)),
            ]
            + ([pltpu.VMEM(s.shape, s.dtype) for s in state] if last else []),
            name="attend",
        )(
            me,
            table,
            flat_counts,
            query_tokens,
            w_query,
            w_keyval[:, :WIDTH],
            jnp.transpose(w_keyval[:, WIDTH:]),
            w_out,
            *arrived,
            handed,
            *carried,
        )
    return carried


def solution(mesh):
    placed = (
        P(("pb", "ka"), None),
        P(None, ("pb", "ka"), None),
        P(),
        P(),
        P(),
        P(),
        P(("pb", "ka"), None, None),
        P(("pb", "ka"), None),
    )
    return jax.shard_map(
        on_device, mesh=mesh, in_specs=placed, out_specs=P(("pb", "ka"), None), check_vma=False
    )
```

```python
import jax
import jax.numpy as jnp
from jax import lax
from jax.experimental import pallas as pl
from jax.experimental.pallas import tpu as pltpu
from jax.sharding import PartitionSpec as P

HEADS = 12
HEAD_DIM = 64
BLK = 128
CAP = 6
WIDTH = HEADS * HEAD_DIM
PARTS = 3
CUT = WIDTH // PARTS
SIDE = 4
PAIRS = HEADS // 2
HALVES = 1
SELECT_VMEM = 4 << 20
ROWS = BLK // HALVES
GROUP = 2 * BLK // ROWS
ITEM = GROUP * ROWS
BF = jnp.bfloat16
F32 = jnp.float32
I32 = jnp.int32
STRIDE = (SIDE * SIDE, SIDE, 1)
ROUTES = ((2, 0, 1), (1, 2, 0), (0, 1, 2))
LOG2E = 1.4426950408889634


ANY = pl.BlockSpec(memory_space=pl.ANY)
SMEM = pl.BlockSpec(memory_space=pltpu.SMEM)
VMEM = pl.BlockSpec(memory_space=pltpu.VMEM)


def shift(value, axis, step):
    stride = STRIDE[axis]
    pairs = []
    for source in range(SIDE**3):
        at = source // stride % SIDE
        pairs.append((source, source + ((at + step) % SIDE - at) * stride))
    return lax.ppermute(value, "pb", pairs)


def swap(value):
    return lax.ppermute(value, "ka", [(0, 1), (1, 0)])


def table_kernel(blocks, me_ref, near_ref, count_ref, map_ref, out_ref):
    def clear(i, _):
        for k in range(8):
            out_ref[0, i * 8 + k] = 0
            out_ref[1, i * 8 + k] = -1
        return 0

    lax.fori_loop(0, 16, clear, 0)
    key_blocks = map_ref.shape[0] // PARTS
    mine = me_ref[0] * 16 + me_ref[1] * 4 + me_ref[2]
    for slab in range(2):
        for q in range(blocks):
            live = count_ref[q * 2 + slab]
            for j in range(CAP):

                @pl.when(j < live)
                def _():
                    entry = near_ref[(q * 2 + slab) * CAP + j]
                    owner = lax.shift_right_logical(map_ref[entry], 1)
                    one = (entry >= key_blocks).astype(I32)
                    two = (entry >= 2 * key_blocks).astype(I32)
                    out_ref[0, slab * 64 + owner] = 1 + one + two
                    away = (mine & 48) + 64 - (owner & 48) & 48
                    away = away | ((mine & 12) + 16 - (owner & 12) & 12)
                    away = away | ((mine & 3) + 4 - (owner & 3) & 3)
                    out_ref[1, (slab * blocks + q) * CAP + j] = away


def select_kernel(part, me_ref, table_ref, *refs):
    across, first, second = ROUTES[part]
    gathered = refs[:SIDE]
    outs = [refs[SIDE * (half + 1) :][:SIDE] for half in range(HALVES)]
    sems = refs[-1]
    for half in range(HALVES):
        for d2 in range(SIDE):
            for d1 in range(SIDE):
                at = [None, None, None]
                at[across] = me_ref[across]
                at[first] = me_ref[first] + 4 - d1 & 3
                at[second] = me_ref[second] + 4 - d2 & 3
                place = me_ref[3] * 64 + at[0] * 16 + at[1] * 4 + at[2]
                for d in range(SIDE):
                    row = 0 if d == 0 else 1 + part * 3 + d - 1
                    which = jnp.maximum(table_ref[row, place] - 1, 0)
                    begin = pl.multiple_of(which * BLK + half * ROWS, ROWS)
                    pltpu.make_async_copy(
                        gathered[d2].at[d1, pl.ds(begin, ROWS)],
                        outs[half][d].at[d2 * 4 + d1],
                        sems.at[half * SIDE + d],
                    ).start()
    for half in range(HALVES):
        for d in range(SIDE):
            out = outs[half][d]
            pltpu.make_async_copy(out, out, sems.at[half * SIDE + d]).wait()


def fetch_parts(code, arrived, target, sem_of):
    away = (lax.shift_right_logical(code, 4), lax.shift_right_logical(code, 2) & 3, code & 3)
    for part, (across, first, second) in enumerate(ROUTES):
        for d in range(SIDE):

            @pl.when(away[across] == d)
            def _():
                pltpu.make_async_copy(
                    arrived[part][d].at[away[second] * 4 + away[first]],
                    target(part),
                    sem_of(part),
                ).start()


def hand_kernel(me_ref, code_ref, *refs):
    arrived = [refs[4 * part : 4 + 4 * part] for part in range(PARTS)]
    out, stage, sems, out_sems = refs[12:]
    count = out.shape[0]

    def start(i, _):
        code = code_ref[1, me_ref[3] * count + i]

        @pl.when(code >= 0)
        def _():
            fetch_parts(
                jnp.maximum(code, 0),
                arrived,
                lambda part: stage.at[i, :, pl.ds(part * CUT, CUT)],
                lambda part: sems.at[i, part],
            )

        return 0

    def finish(i, _):
        @pl.when(code_ref[1, me_ref[3] * count + i] >= 0)
        def _():
            for part in range(PARTS):
                pltpu.make_async_copy(
                    arrived[part][0].at[0],
                    stage.at[i, :, pl.ds(part * CUT, CUT)],
                    sems.at[i, part],
                ).wait()

        pltpu.make_async_copy(stage.at[i], out.at[i], out_sems.at[i]).start()
        return 0

    def close(i, _):
        pltpu.make_async_copy(stage.at[i], out.at[i], out_sems.at[i]).wait()
        return 0

    lax.fori_loop(0, count, start, 0)
    lax.fori_loop(0, count, finish, 0)
    lax.fori_loop(0, count, close, 0)


def attend_kernel(first, last, *refs):
    refs = list(refs)
    me_ref, code_ref, count_ref, xq_ref, wq_ref, wk_ref, wvt_ref, wo_ref = refs[:8]
    arrived = [refs[8 + 4 * part : 12 + 4 * part] for part in range(PARTS)]
    handed = refs[20]
    refs = refs[21:]
    if not first:
        before = refs[:3]
        refs = refs[3:]
    if last:
        out_ref = refs.pop(0)
        peak, total, sums = refs[-3:]
    else:
        peak, total, sums = refs[:3]
        refs = refs[3:]
    item_q, item_n, item_code, tokens, keys, values, spread, sems = refs[:8]
    blocks = xq_ref.shape[0] // BLK
    mine = me_ref[3]
    span = blocks * CAP

    def plan_block(q, begun):
        own = count_ref[q * 2 + mine]
        live = own + count_ref[q * 2 + 1 - mine]

        def plan_item(k, _):
            t = begun + k
            item_q[t] = q
            item_n[t] = live - GROUP * k
            for g in range(GROUP):
                i = jnp.where(GROUP * k + g < live, GROUP * k + g, GROUP * k)
                near = code_ref[1, mine * span + q * CAP + jnp.minimum(i, own - 1)]
                item_code[t * GROUP + g] = jnp.where(i < own, near, 64 + q * CAP + i - own)
            return 0

        items = lax.div(live + GROUP - 1, GROUP)
        lax.fori_loop(0, items, plan_item, 0)
        return begun + items

    steps = lax.fori_loop(0, blocks, plan_block, 0)

    def fetch(t):
        slot = t & 1
        for g in range(GROUP):
            code = item_code[t * GROUP + g]
            rows = pl.ds(g * ROWS, ROWS)

            @pl.when(code < 64)
            def _():
                fetch_parts(
                    code,
                    arrived,
                    lambda part: tokens.at[slot, rows, pl.ds(part * CUT, CUT)],
                    lambda part: sems.at[slot],
                )

            @pl.when(code >= 64)
            def _():
                pltpu.make_async_copy(
                    handed.at[jnp.maximum(code - 64, 0)], tokens.at[slot, rows], sems.at[slot]
                ).start()

    def landed(slot):
        pltpu.make_async_copy(tokens.at[slot], tokens.at[slot], sems.at[slot]).wait()

    def project(slot, chunk):
        part = pl.ds(chunk % 3 * CUT, CUT)
        if chunk < 3:
            keys[slot, :, part] = jnp.dot(
                tokens[slot], wk_ref[:, part], preferred_element_type=F32
            ).astype(BF)
        else:
            values[slot, part, :] = lax.dot_general(
                wvt_ref[part, :],
                tokens[slot],
                (((1,), (1,)), ((), ())),
                preferred_element_type=F32,
            ).astype(BF)

    fetch(0)
    fetch(1)
    low = lax.broadcasted_iota(I32, (BLK, BLK), 1) < HEAD_DIM
    zero = jnp.zeros((BLK, BLK), BF)
    for q in range(blocks):
        queries = jnp.dot(
            xq_ref[q * BLK : (q + 1) * BLK, :], wq_ref[...], preferred_element_type=F32
        ).astype(BF)
        for p in range(PAIRS):
            two = queries[:, p * BLK : (p + 1) * BLK]
            spread[q, p, :BLK, :] = jnp.where(low, two, zero)
            spread[q, p, BLK:, :] = jnp.where(low, zero, two)
    if first:
        peak[...] = jnp.full_like(peak, -jnp.inf)
        total[...] = jnp.zeros_like(total)
        sums[...] = jnp.zeros_like(sums)
    else:
        for mine_ref, old_ref in zip((peak, total, sums), before):
            mine_ref[...] = old_ref[...]
    landed(0)
    for chunk in range(6):
        project(0, chunk)

    def step(t, _):
        slot = t & 1
        q = item_q[t]
        live = item_n[t]

        @pl.when(t + 2 < steps)
        def _():
            fetch(t + 2)

        for g in range(1, GROUP):

            @pl.when(live <= g)
            def _():
                values[slot, :, pl.ds(g * ROWS, ROWS)] = jnp.zeros((WIDTH, ROWS), BF)

        @pl.when(t + 1 < steps)
        def _():
            landed(1 - slot)

        scale = HEAD_DIM**-0.5 * LOG2E

        def score(p):
            return lax.dot_general(
                keys[slot, :, p * BLK : (p + 1) * BLK],
                spread[q, p],
                (((1,), (1,)), ((), ())),
                preferred_element_type=F32,
            )

        ahead = score(0)
        waiting = None
        for p in range(PAIRS + 1):
            scores = ahead
            if p + 1 < PAIRS:
                ahead = score(p + 1)
            if p % 2 == 0 and p < PAIRS:
                project(1 - slot, p // 2)
                project(1 - slot, 3 + p // 2)
            if waiting is not None:
                weights, factor = waiting
                top = (p - 1) * BLK
                mid = top + HEAD_DIM
                end = top + BLK
                mixed = jnp.dot(values[slot, top:end, :], weights, preferred_element_type=F32)
                sums[q, top:mid, :] = (
                    sums[q, top:mid, :] * factor[:, :BLK] + mixed[:HEAD_DIM, :BLK]
                )
                sums[q, mid:end, :] = (
                    sums[q, mid:end, :] * factor[:, BLK:] + mixed[HEAD_DIM:, BLK:]
                )
            if p < PAIRS:
                old = peak[q, p : p + 1, :]
                new = jnp.maximum(old, jnp.max(scores, axis=0, keepdims=True))
                expo = jnp.exp2((scores - new) * scale)
                factor = jnp.exp2((old - new) * scale)
                peak[q, p : p + 1, :] = new
                add = total[q, p : p + 1, :] * factor
                for g in range(GROUP):
                    some = jnp.sum(expo[g * ROWS : (g + 1) * ROWS], axis=0, keepdims=True)
                    add = add + (some if g == 0 else jnp.where(g < live, some, 0.0))
                total[q, p : p + 1, :] = add
                waiting = (expo.astype(BF), factor)
        return 0

    lax.fori_loop(0, steps, step, 0)
    if last:
        for q in range(blocks):
            done = []
            for p in range(PAIRS):
                for h in range(2):
                    top = p * BLK + h * HEAD_DIM
                    done.append(
                        sums[q, top : top + HEAD_DIM, :]
                        / total[q, p : p + 1, h * BLK : (h + 1) * BLK]
                    )
            attended = jnp.transpose(jnp.concatenate(done, axis=0)).astype(BF)
            out_ref[q * BLK : (q + 1) * BLK, :] = jnp.dot(
                attended, wo_ref[...], preferred_element_type=F32
            ).astype(BF)


def on_device(query_tokens, source_tokens, w_query, w_keyval, w_out, slab_map, neighbours, counts):
    blocks = neighbours.shape[0]
    place = lax.axis_index("pb").astype(I32)
    me = jnp.stack(
        [place // 16, place // 4 % 4, place % 4, lax.axis_index("ka").astype(I32)]
    )
    flat_counts = counts.reshape(-1)
    table = pl.pallas_call(
        lambda *refs: table_kernel(blocks, *refs),
        out_shape=jax.ShapeDtypeStruct((2, 128), I32),
        in_specs=[SMEM] * 4,
        out_specs=SMEM,
        name="tables",
    )(me, neighbours.reshape(-1), flat_counts, slab_map.reshape(-1))
    note = jnp.pad(table[:1].astype(BF), ((0, 15), (0, CUT - 128)))
    tall = PARTS * BLK
    heard = []
    lines = []
    hold = None
    for part, (_, axis, _) in enumerate(ROUTES):
        own = source_tokens[:, :, part * CUT : (part + 1) * CUT].reshape(tall, CUT)
        own = jnp.concatenate([own, note])
        if part == 2:
            own, lines[0] = lax.optimization_barrier((own, lines[0]))
        told = [own] + [shift(own, axis, d) for d in range(1, SIDE)]
        heard.append([t[tall, :128].astype(I32) for t in told])
        lines.append(jnp.stack(told))
    source = {first: part for part, (_, first, _) in enumerate(ROUTES)}
    rows = [table[0]]
    for across, _, _ in ROUTES:
        rows += [heard[source[across]][SIDE - d] for d in range(1, SIDE)]
    wishes = jnp.stack(rows + [table[1]])
    partner = swap(wishes)
    wishes = wishes + partner
    partner = partner[9:]

    everything = [[] for _ in range(HALVES)]
    for part, (across, _, axis) in enumerate(ROUTES):
        gathered = [lines[part]] + [shift(lines[part], axis, d) for d in range(1, SIDE)]
        chosen = pl.pallas_call(
            lambda *refs: select_kernel(part, *refs),
            out_shape=[jax.ShapeDtypeStruct((SIDE * SIDE, ROWS, CUT), BF)] * (SIDE * HALVES),
            in_specs=[SMEM] * 2 + [VMEM] * SIDE,
            out_specs=[ANY] * (SIDE * HALVES),
            scratch_shapes=[pltpu.SemaphoreType.DMA((SIDE * HALVES,))],
            compiler_params=pltpu.CompilerParams(vmem_limit_bytes=SELECT_VMEM),
            name="select",
        )(me, wishes, *gathered)
        for half in range(HALVES):
            ours = chosen[half * SIDE :][:SIDE]
            everything[half] += [ours[0]] + [shift(ours[d], across, d) for d in range(1, SIDE)]
    state = [
        jax.ShapeDtypeStruct((blocks, 8, 2 * BLK), F32),
        jax.ShapeDtypeStruct((blocks, 8, 2 * BLK), F32),
        jax.ShapeDtypeStruct((blocks, WIDTH, BLK), F32),
    ]
    carried = []
    for half, arrived in enumerate(everything):
        handed = pl.pallas_call(
            hand_kernel,
            out_shape=jax.ShapeDtypeStruct((blocks * CAP, ROWS, WIDTH), BF),
            in_specs=[SMEM] * 2 + [ANY] * 12,
            out_specs=ANY,
            scratch_shapes=[
                pltpu.VMEM((blocks * CAP, ROWS, WIDTH), BF),
                pltpu.SemaphoreType.DMA((blocks * CAP, PARTS)),
                pltpu.SemaphoreType.DMA((blocks * CAP,)),
            ],
            name="hand",
        )(me, partner, *arrived)
        handed = swap(handed)
        first = half == 0
        last = half == HALVES - 1
        items = blocks * -(-2 * CAP // GROUP)
        carried = pl.pallas_call(
            lambda *refs: attend_kernel(first, last, *refs),
            out_shape=jax.ShapeDtypeStruct(query_tokens.shape, BF) if last else state,
            in_specs=[SMEM] * 3 + [VMEM] * 5 + [ANY] * 13 + [VMEM] * len(carried),
            out_specs=VMEM if last else [VMEM] * 3,
            scratch_shapes=[
                pltpu.SMEM((items,), I32),
                pltpu.SMEM((items,), I32),
                pltpu.SMEM((items * GROUP,), I32),
                pltpu.VMEM((2, ITEM, WIDTH), BF),
                pltpu.VMEM((2, ITEM, WIDTH), BF),
                pltpu.VMEM((2, WIDTH, ITEM), BF),
                pltpu.VMEM((blocks, PAIRS, 2 * BLK, BLK), BF),
                pltpu.SemaphoreType.DMA((2,)),
            ]
            + ([pltpu.VMEM(s.shape, s.dtype) for s in state] if last else []),
            name="attend",
        )(
            me,
            table,
            flat_counts,
            query_tokens,
            w_query,
            w_keyval[:, :WIDTH],
            jnp.transpose(w_keyval[:, WIDTH:]),
            w_out,
            *arrived,
            handed,
            *carried,
        )
    return carried


def solution(mesh):
    placed = (
        P(("pb", "ka"), None),
        P(None, ("pb", "ka"), None),
        P(),
        P(),
        P(),
        P(),
        P(("pb", "ka"), None, None),
        P(("pb", "ka"), None),
    )
    return jax.shard_map(
        on_device, mesh=mesh, in_specs=placed, out_specs=P(("pb", "ka"), None), check_vma=False
    )
```

```python
import jax
import jax.numpy as jnp
from jax import lax
from jax.experimental import pallas as pl
from jax.experimental.pallas import tpu as pltpu
from jax.sharding import PartitionSpec as P

HEADS = 12
HEAD_DIM = 64
BLK = 128
CAP = 6
WIDTH = HEADS * HEAD_DIM
PARTS = 3
CUT = WIDTH // PARTS
SIDE = 4
PAIRS = HEADS // 2
HALVES = 1
SELECT_VMEM = 8 << 20
ROWS = BLK // HALVES
GROUP = 2 * BLK // ROWS
ITEM = GROUP * ROWS
BF = jnp.bfloat16
F32 = jnp.float32
I32 = jnp.int32
STRIDE = (SIDE * SIDE, SIDE, 1)
ROUTES = ((2, 0, 1), (1, 2, 0), (0, 1, 2))
LOG2E = 1.4426950408889634


SMEM = pl.BlockSpec(memory_space=pltpu.SMEM)
VMEM = pl.BlockSpec(memory_space=pltpu.VMEM)
HBM = pl.BlockSpec(memory_space=pltpu.HBM)


def shift(value, axis, step):
    stride = STRIDE[axis]
    pairs = []
    for source in range(SIDE**3):
        at = source // stride % SIDE
        pairs.append((source, source + ((at + step) % SIDE - at) * stride))
    return lax.ppermute(value, "pb", pairs)


def swap(value):
    return lax.ppermute(value, "ka", [(0, 1), (1, 0)])


def table_kernel(blocks, me_ref, near_ref, count_ref, map_ref, out_ref):
    def clear(i, _):
        for k in range(8):
            out_ref[0, i * 8 + k] = 0
            out_ref[1, i * 8 + k] = -1
        return 0

    lax.fori_loop(0, 16, clear, 0)
    key_blocks = map_ref.shape[0] // PARTS
    mine = me_ref[0] * 16 + me_ref[1] * 4 + me_ref[2]
    for slab in range(2):
        for q in range(blocks):
            live = count_ref[q * 2 + slab]
            for j in range(CAP):

                @pl.when(j < live)
                def _():
                    entry = near_ref[(q * 2 + slab) * CAP + j]
                    owner = lax.shift_right_logical(map_ref[entry], 1)
                    one = (entry >= key_blocks).astype(I32)
                    two = (entry >= 2 * key_blocks).astype(I32)
                    out_ref[0, slab * 64 + owner] = 1 + one + two
                    away = (mine & 48) + 64 - (owner & 48) & 48
                    away = away | ((mine & 12) + 16 - (owner & 12) & 12)
                    away = away | ((mine & 3) + 4 - (owner & 3) & 3)
                    out_ref[1, (slab * blocks + q) * CAP + j] = away


def select_kernel(part, me_ref, table_ref, *refs):
    across, first, second = ROUTES[part]
    gathered = refs[:SIDE]
    outs = [refs[SIDE * (half + 1) :][:SIDE] for half in range(HALVES)]

    def body(d1, _):
        for d2 in range(SIDE):
            at = [None, None, None]
            at[across] = me_ref[across]
            at[first] = me_ref[first] + 4 - d1 & 3
            at[second] = me_ref[second] + 4 - d2 & 3
            place = me_ref[3] * 64 + at[0] * 16 + at[1] * 4 + at[2]
            for d in range(SIDE):
                row = 0 if d == 0 else 1 + part * 3 + d - 1
                which = jnp.maximum(table_ref[row, place] - 1, 0)
                for half in range(HALVES):
                    begin = pl.multiple_of(which * BLK + half * ROWS, ROWS)
                    outs[half][d][d2 * 4 + d1] = gathered[d2][d1, pl.ds(begin, ROWS), :]
        return 0

    lax.fori_loop(0, SIDE, body, 0)


def fetch_parts(code, arrived, target, sem_of):
    away = (lax.shift_right_logical(code, 4), lax.shift_right_logical(code, 2) & 3, code & 3)
    for part, (across, first, second) in enumerate(ROUTES):
        for d in range(SIDE):

            @pl.when(away[across] == d)
            def _():
                pltpu.make_async_copy(
                    arrived[part][d].at[away[second] * 4 + away[first]],
                    target(part),
                    sem_of(part),
                ).start()


def hand_kernel(me_ref, code_ref, *refs):
    arrived = [refs[4 * part : 4 + 4 * part] for part in range(PARTS)]
    out, sems = refs[12:]
    count = out.shape[0]

    def start(i, _):
        code = code_ref[1, me_ref[3] * count + i]

        @pl.when(code >= 0)
        def _():
            fetch_parts(
                jnp.maximum(code, 0),
                arrived,
                lambda part: out.at[i, :, pl.ds(part * CUT, CUT)],
                lambda part: sems.at[i],
            )

        return 0

    def finish(i, _):
        @pl.when(code_ref[1, me_ref[3] * count + i] >= 0)
        def _():
            pltpu.make_async_copy(out.at[i], out.at[i], sems.at[i]).wait()

        return 0

    lax.fori_loop(0, count, start, 0)
    lax.fori_loop(0, count, finish, 0)


def attend_kernel(first, last, *refs):
    refs = list(refs)
    me_ref, code_ref, count_ref, xq_ref, wq_ref, wk_ref, wvt_ref, wo_ref = refs[:8]
    arrived = [refs[8 + 4 * part : 12 + 4 * part] for part in range(PARTS)]
    handed = refs[20]
    refs = refs[21:]
    if not first:
        before = refs[:3]
        refs = refs[3:]
    if last:
        out_ref = refs.pop(0)
        peak, total, sums = refs[-3:]
    else:
        peak, total, sums = refs[:3]
        refs = refs[3:]
    item_q, item_n, item_code, tokens, keys, values, spread, sems = refs[:8]
    blocks = xq_ref.shape[0] // BLK
    mine = me_ref[3]
    span = blocks * CAP

    def plan_block(q, begun):
        own = count_ref[q * 2 + mine]
        live = own + count_ref[q * 2 + 1 - mine]

        def plan_item(k, _):
            t = begun + k
            item_q[t] = q
            item_n[t] = live - GROUP * k
            for g in range(GROUP):
                i = jnp.where(GROUP * k + g < live, GROUP * k + g, GROUP * k)
                near = code_ref[1, mine * span + q * CAP + jnp.minimum(i, own - 1)]
                item_code[t * GROUP + g] = jnp.where(i < own, near, 64 + q * CAP + i - own)
            return 0

        items = lax.div(live + GROUP - 1, GROUP)
        lax.fori_loop(0, items, plan_item, 0)
        return begun + items

    steps = lax.fori_loop(0, blocks, plan_block, 0)

    def fetch(t):
        slot = t & 1
        for g in range(GROUP):
            code = item_code[t * GROUP + g]
            rows = pl.ds(g * ROWS, ROWS)

            @pl.when(code < 64)
            def _():
                fetch_parts(
                    code,
                    arrived,
                    lambda part: tokens.at[slot, rows, pl.ds(part * CUT, CUT)],
                    lambda part: sems.at[slot],
                )

            @pl.when(code >= 64)
            def _():
                pltpu.make_async_copy(
                    handed.at[jnp.maximum(code - 64, 0)], tokens.at[slot, rows], sems.at[slot]
                ).start()

    def landed(slot):
        pltpu.make_async_copy(tokens.at[slot], tokens.at[slot], sems.at[slot]).wait()

    def project(slot, chunk):
        part = pl.ds(chunk % 3 * CUT, CUT)
        if chunk < 3:
            keys[slot, :, part] = jnp.dot(
                tokens[slot], wk_ref[:, part], preferred_element_type=F32
            ).astype(BF)
        else:
            values[slot, part, :] = lax.dot_general(
                wvt_ref[part, :],
                tokens[slot],
                (((1,), (1,)), ((), ())),
                preferred_element_type=F32,
            ).astype(BF)

    fetch(0)
    fetch(1)
    low = lax.broadcasted_iota(I32, (BLK, BLK), 1) < HEAD_DIM
    zero = jnp.zeros((BLK, BLK), BF)
    for q in range(blocks):
        queries = jnp.dot(
            xq_ref[q * BLK : (q + 1) * BLK, :], wq_ref[...], preferred_element_type=F32
        ).astype(BF)
        for p in range(PAIRS):
            two = queries[:, p * BLK : (p + 1) * BLK]
            spread[q, p, :BLK, :] = jnp.where(low, two, zero)
            spread[q, p, BLK:, :] = jnp.where(low, zero, two)
    if first:
        peak[...] = jnp.full_like(peak, -jnp.inf)
        total[...] = jnp.zeros_like(total)
        sums[...] = jnp.zeros_like(sums)
    else:
        for mine_ref, old_ref in zip((peak, total, sums), before):
            mine_ref[...] = old_ref[...]
    landed(0)
    for chunk in range(6):
        project(0, chunk)

    def step(t, _):
        slot = t & 1
        q = item_q[t]
        live = item_n[t]

        @pl.when(t + 2 < steps)
        def _():
            fetch(t + 2)

        for g in range(1, GROUP):

            @pl.when(live <= g)
            def _():
                values[slot, :, pl.ds(g * ROWS, ROWS)] = jnp.zeros((WIDTH, ROWS), BF)

        @pl.when(t + 1 < steps)
        def _():
            landed(1 - slot)

        scale = HEAD_DIM**-0.5 * LOG2E

        def score(p):
            return lax.dot_general(
                keys[slot, :, p * BLK : (p + 1) * BLK],
                spread[q, p],
                (((1,), (1,)), ((), ())),
                preferred_element_type=F32,
            )

        ahead = score(0)
        waiting = None
        for p in range(PAIRS + 1):
            scores = ahead
            if p + 1 < PAIRS:
                ahead = score(p + 1)
            if p % 2 == 0 and p < PAIRS:
                project(1 - slot, p // 2)
                project(1 - slot, 3 + p // 2)
            if waiting is not None:
                weights, factor = waiting
                top = (p - 1) * BLK
                mid = top + HEAD_DIM
                end = top + BLK
                mixed = jnp.dot(values[slot, top:end, :], weights, preferred_element_type=F32)
                sums[q, top:mid, :] = (
                    sums[q, top:mid, :] * factor[:, :BLK] + mixed[:HEAD_DIM, :BLK]
                )
                sums[q, mid:end, :] = (
                    sums[q, mid:end, :] * factor[:, BLK:] + mixed[HEAD_DIM:, BLK:]
                )
            if p < PAIRS:
                old = peak[q, p : p + 1, :]
                new = jnp.maximum(old, jnp.max(scores, axis=0, keepdims=True))
                expo = jnp.exp2((scores - new) * scale)
                factor = jnp.exp2((old - new) * scale)
                peak[q, p : p + 1, :] = new
                add = total[q, p : p + 1, :] * factor
                for g in range(GROUP):
                    some = jnp.sum(expo[g * ROWS : (g + 1) * ROWS], axis=0, keepdims=True)
                    add = add + (some if g == 0 else jnp.where(g < live, some, 0.0))
                total[q, p : p + 1, :] = add
                waiting = (expo.astype(BF), factor)
        return 0

    lax.fori_loop(0, steps, step, 0)
    if last:
        for q in range(blocks):
            done = []
            for p in range(PAIRS):
                for h in range(2):
                    top = p * BLK + h * HEAD_DIM
                    done.append(
                        sums[q, top : top + HEAD_DIM, :]
                        / total[q, p : p + 1, h * BLK : (h + 1) * BLK]
                    )
            attended = jnp.transpose(jnp.concatenate(done, axis=0)).astype(BF)
            out_ref[q * BLK : (q + 1) * BLK, :] = jnp.dot(
                attended, wo_ref[...], preferred_element_type=F32
            ).astype(BF)


def on_device(query_tokens, source_tokens, w_query, w_keyval, w_out, slab_map, neighbours, counts):
    blocks = neighbours.shape[0]
    place = lax.axis_index("pb").astype(I32)
    me = jnp.stack(
        [place // 16, place // 4 % 4, place % 4, lax.axis_index("ka").astype(I32)]
    )
    flat_counts = counts.reshape(-1)
    table = pl.pallas_call(
        lambda *refs: table_kernel(blocks, *refs),
        out_shape=jax.ShapeDtypeStruct((2, 128), I32),
        in_specs=[SMEM] * 4,
        out_specs=SMEM,
        name="tables",
    )(me, neighbours.reshape(-1), flat_counts, slab_map.reshape(-1))
    note = jnp.pad(table[:1].astype(BF), ((0, 15), (0, CUT - 128)))
    tall = PARTS * BLK
    heard = []
    lines = []
    for part, (_, axis, _) in enumerate(ROUTES):
        own = source_tokens[:, :, part * CUT : (part + 1) * CUT].reshape(tall, CUT)
        own = jnp.concatenate([own, note])
        told = [own] + [shift(own, axis, d) for d in range(1, SIDE)]
        heard.append([t[tall, :128].astype(I32) for t in told])
        lines.append(jnp.stack(told))
    source = {first: part for part, (_, first, _) in enumerate(ROUTES)}
    rows = [table[0]]
    for across, _, _ in ROUTES:
        rows += [heard[source[across]][SIDE - d] for d in range(1, SIDE)]
    wishes = jnp.stack(rows + [table[1]])
    partner = swap(wishes)
    wishes = wishes + partner
    partner = partner[9:]

    everything = [[] for _ in range(HALVES)]
    for part, (across, _, axis) in enumerate(ROUTES):
        gathered = [lines[part]] + [shift(lines[part], axis, d) for d in range(1, SIDE)]
        chosen = pl.pallas_call(
            lambda *refs: select_kernel(part, *refs),
            out_shape=[jax.ShapeDtypeStruct((SIDE * SIDE, ROWS, CUT), BF)] * (SIDE * HALVES),
            in_specs=[SMEM] * 2 + [VMEM] * SIDE,
            out_specs=[VMEM] * (SIDE * HALVES),
            compiler_params=pltpu.CompilerParams(vmem_limit_bytes=SELECT_VMEM),
            name="select",
        )(me, wishes, *gathered)
        for half in range(HALVES):
            ours = chosen[half * SIDE :][:SIDE]
            everything[half] += [ours[0]] + [shift(ours[d], across, d) for d in range(1, SIDE)]
    state = [
        jax.ShapeDtypeStruct((blocks, 8, 2 * BLK), F32),
        jax.ShapeDtypeStruct((blocks, 8, 2 * BLK), F32),
        jax.ShapeDtypeStruct((blocks, WIDTH, BLK), F32),
    ]
    carried = []
    for half, arrived in enumerate(everything):
        handed = pl.pallas_call(
            hand_kernel,
            out_shape=jax.ShapeDtypeStruct((blocks * CAP, ROWS, WIDTH), BF),
            in_specs=[SMEM] * 2 + [HBM] * 12,
            out_specs=VMEM,
            scratch_shapes=[pltpu.SemaphoreType.DMA((blocks * CAP,))],
            name="hand",
        )(me, partner, *arrived)
        handed = swap(handed)
        first = half == 0
        last = half == HALVES - 1
        items = blocks * -(-2 * CAP // GROUP)
        carried = pl.pallas_call(
            lambda *refs: attend_kernel(first, last, *refs),
            out_shape=jax.ShapeDtypeStruct(query_tokens.shape, BF) if last else state,
            in_specs=[SMEM] * 3 + [VMEM] * 5 + [HBM] * 13 + [VMEM] * len(carried),
            out_specs=VMEM if last else [VMEM] * 3,
            scratch_shapes=[
                pltpu.SMEM((items,), I32),
                pltpu.SMEM((items,), I32),
                pltpu.SMEM((items * GROUP,), I32),
                pltpu.VMEM((2, ITEM, WIDTH), BF),
                pltpu.VMEM((2, ITEM, WIDTH), BF),
                pltpu.VMEM((2, WIDTH, ITEM), BF),
                pltpu.VMEM((blocks, PAIRS, 2 * BLK, BLK), BF),
                pltpu.SemaphoreType.DMA((2,)),
            ]
            + ([pltpu.VMEM(s.shape, s.dtype) for s in state] if last else []),
            name="attend",
        )(
            me,
            table,
            flat_counts,
            query_tokens,
            w_query,
            w_keyval[:, :WIDTH],
            jnp.transpose(w_keyval[:, WIDTH:]),
            w_out,
            *arrived,
            handed,
            *carried,
        )
    return carried


def solution(mesh):
    placed = (
        P(("pb", "ka"), None),
        P(None, ("pb", "ka"), None),
        P(),
        P(),
        P(),
        P(),
        P(("pb", "ka"), None, None),
        P(("pb", "ka"), None),
    )
    return jax.shard_map(
        on_device, mesh=mesh, in_specs=placed, out_specs=P(("pb", "ka"), None), check_vma=False
    )
```

```python
import jax
import jax.numpy as jnp
from jax import lax
from jax.experimental import pallas as pl
from jax.experimental.pallas import tpu as pltpu
from jax.sharding import PartitionSpec as P


HEADS = 12
HEAD_DIM = 64
BLK = 128
CAP = 6
WIDTH = HEADS * HEAD_DIM
PARTS = 3
CUT = WIDTH // PARTS
SIDE = 4
PAIRS = HEADS // 2
HALVES = 2
SELECT_VMEM = 8 << 20
ROWS = BLK // HALVES
GROUP = 2 * BLK // ROWS
ITEM = GROUP * ROWS
BF = jnp.bfloat16
F32 = jnp.float32
I32 = jnp.int32
STRIDE = (SIDE * SIDE, SIDE, 1)
ROUTES = ((2, 0, 1), (1, 2, 0), (0, 1, 2))
LOG2E = 1.4426950408889634


SMEM = pl.BlockSpec(memory_space=pltpu.SMEM)
VMEM = pl.BlockSpec(memory_space=pltpu.VMEM)
HBM = pl.BlockSpec(memory_space=pltpu.HBM)


def shift(value, axis, step):
    stride = STRIDE[axis]
    pairs = []
    for source in range(SIDE**3):
        at = source // stride % SIDE
        pairs.append((source, source + ((at + step) % SIDE - at) * stride))
    return lax.ppermute(value, "pb", pairs)


def swap(value):
    return lax.ppermute(value, "ka", [(0, 1), (1, 0)])


def table_kernel(blocks, me_ref, near_ref, count_ref, map_ref, out_ref):
    def clear(i, _):
        for k in range(8):
            out_ref[0, i * 8 + k] = 0
            out_ref[1, i * 8 + k] = -1
        return 0

    lax.fori_loop(0, 16, clear, 0)
    key_blocks = map_ref.shape[0] // PARTS
    mine = me_ref[0] * 16 + me_ref[1] * 4 + me_ref[2]
    for slab in range(2):
        for q in range(blocks):
            live = count_ref[q * 2 + slab]
            for j in range(CAP):

                @pl.when(j < live)
                def _():
                    entry = near_ref[(q * 2 + slab) * CAP + j]
                    owner = lax.shift_right_logical(map_ref[entry], 1)
                    one = (entry >= key_blocks).astype(I32)
                    two = (entry >= 2 * key_blocks).astype(I32)
                    out_ref[0, slab * 64 + owner] = 1 + one + two
                    away = (mine & 48) + 64 - (owner & 48) & 48
                    away = away | ((mine & 12) + 16 - (owner & 12) & 12)
                    away = away | ((mine & 3) + 4 - (owner & 3) & 3)
                    out_ref[1, (slab * blocks + q) * CAP + j] = away


def select_kernel(part, me_ref, table_ref, *refs):
    across, first, second = ROUTES[part]
    gathered = refs[:SIDE]
    outs = [refs[SIDE * (half + 1) :][:SIDE] for half in range(HALVES)]

    def body(d1, _):
        for d2 in range(SIDE):
            at = [None, None, None]
            at[across] = me_ref[across]
            at[first] = me_ref[first] + 4 - d1 & 3
            at[second] = me_ref[second] + 4 - d2 & 3
            place = me_ref[3] * 64 + at[0] * 16 + at[1] * 4 + at[2]
            for d in range(SIDE):
                row = 0 if d == 0 else 1 + part * 3 + d - 1
                which = jnp.maximum(table_ref[row, place] - 1, 0)
                for half in range(HALVES):
                    begin = pl.multiple_of(which * BLK + half * ROWS, ROWS)
                    outs[half][d][d2 * 4 + d1] = gathered[d2][d1, pl.ds(begin, ROWS), :]
        return 0

    lax.fori_loop(0, SIDE, body, 0)


def fetch_parts(code, arrived, target, sem_of):
    away = (lax.shift_right_logical(code, 4), lax.shift_right_logical(code, 2) & 3, code & 3)
    for part, (across, first, second) in enumerate(ROUTES):
        for d in range(SIDE):

            @pl.when(away[across] == d)
            def _():
                pltpu.make_async_copy(
                    arrived[part][d].at[away[second] * 4 + away[first]],
                    target(part),
                    sem_of(part),
                ).start()


def hand_kernel(me_ref, code_ref, *refs):
    arrived = [refs[4 * part : 4 + 4 * part] for part in range(PARTS)]
    out, sems = refs[12:]
    count = out.shape[0]

    def start(i, _):
        code = code_ref[1, me_ref[3] * count + i]

        @pl.when(code >= 0)
        def _():
            fetch_parts(
                jnp.maximum(code, 0),
                arrived,
                lambda part: out.at[i, :, pl.ds(part * CUT, CUT)],
                lambda part: sems.at[i],
            )

        return 0

    def finish(i, _):
        @pl.when(code_ref[1, me_ref[3] * count + i] >= 0)
        def _():
            pltpu.make_async_copy(out.at[i], out.at[i], sems.at[i]).wait()

        return 0

    lax.fori_loop(0, count, start, 0)
    lax.fori_loop(0, count, finish, 0)


def attend_kernel(first, last, *refs):
    refs = list(refs)
    me_ref, code_ref, count_ref, xq_ref, wq_ref, wk_ref, wvt_ref, wo_ref = refs[:8]
    arrived = [refs[8 + 4 * part : 12 + 4 * part] for part in range(PARTS)]
    handed = refs[20]
    refs = refs[21:]
    if not first:
        before = refs[:3]
        refs = refs[3:]
    if last:
        out_ref = refs.pop(0)
        peak, total, sums = refs[-3:]
    else:
        peak, total, sums = refs[:3]
        refs = refs[3:]
    item_q, item_n, item_code, tokens, keys, values, spread, sems = refs[:8]
    blocks = xq_ref.shape[0] // BLK
    mine = me_ref[3]
    span = blocks * CAP

    def plan_block(q, begun):
        own = count_ref[q * 2 + mine]
        live = own + count_ref[q * 2 + 1 - mine]

        def plan_item(k, _):
            t = begun + k
            item_q[t] = q
            item_n[t] = live - GROUP * k
            for g in range(GROUP):
                i = jnp.where(GROUP * k + g < live, GROUP * k + g, GROUP * k)
                near = code_ref[1, mine * span + q * CAP + jnp.minimum(i, own - 1)]
                item_code[t * GROUP + g] = jnp.where(i < own, near, 64 + q * CAP + i - own)
            return 0

        items = lax.div(live + GROUP - 1, GROUP)
        lax.fori_loop(0, items, plan_item, 0)
        return begun + items

    steps = lax.fori_loop(0, blocks, plan_block, 0)

    def fetch(t):
        slot = t & 1
        for g in range(GROUP):
            code = item_code[t * GROUP + g]
            rows = pl.ds(g * ROWS, ROWS)

            @pl.when(code < 64)
            def _():
                fetch_parts(
                    code,
                    arrived,
                    lambda part: tokens.at[slot, rows, pl.ds(part * CUT, CUT)],
                    lambda part: sems.at[slot],
                )

            @pl.when(code >= 64)
            def _():
                pltpu.make_async_copy(
                    handed.at[jnp.maximum(code - 64, 0)], tokens.at[slot, rows], sems.at[slot]
                ).start()

    def landed(slot):
        pltpu.make_async_copy(tokens.at[slot], tokens.at[slot], sems.at[slot]).wait()

    def project(slot, chunk):
        part = pl.ds(chunk % 3 * CUT, CUT)
        if chunk < 3:
            keys[slot, :, part] = jnp.dot(
                tokens[slot], wk_ref[:, part], preferred_element_type=F32
            ).astype(BF)
        else:
            values[slot, part, :] = lax.dot_general(
                wvt_ref[part, :],
                tokens[slot],
                (((1,), (1,)), ((), ())),
                preferred_element_type=F32,
            ).astype(BF)

    fetch(0)
    fetch(1)
    low = lax.broadcasted_iota(I32, (BLK, BLK), 1) < HEAD_DIM
    zero = jnp.zeros((BLK, BLK), BF)
    for q in range(blocks):
        queries = jnp.dot(
            xq_ref[q * BLK : (q + 1) * BLK, :], wq_ref[...], preferred_element_type=F32
        ).astype(BF)
        for p in range(PAIRS):
            two = queries[:, p * BLK : (p + 1) * BLK]
            spread[q, p, :BLK, :] = jnp.where(low, two, zero)
            spread[q, p, BLK:, :] = jnp.where(low, zero, two)
    if first:
        peak[...] = jnp.full_like(peak, -jnp.inf)
        total[...] = jnp.zeros_like(total)
        sums[...] = jnp.zeros_like(sums)
    else:
        for mine_ref, old_ref in zip((peak, total, sums), before):
            mine_ref[...] = old_ref[...]
    landed(0)
    for chunk in range(6):
        project(0, chunk)

    def step(t, _):
        slot = t & 1
        q = item_q[t]
        live = item_n[t]

        @pl.when(t + 2 < steps)
        def _():
            fetch(t + 2)

        for g in range(1, GROUP):

            @pl.when(live <= g)
            def _():
                values[slot, :, pl.ds(g * ROWS, ROWS)] = jnp.zeros((WIDTH, ROWS), BF)

        @pl.when(t + 1 < steps)
        def _():
            landed(1 - slot)

        scale = HEAD_DIM**-0.5 * LOG2E

        def score(p):
            return lax.dot_general(
                keys[slot, :, p * BLK : (p + 1) * BLK],
                spread[q, p],
                (((1,), (1,)), ((), ())),
                preferred_element_type=F32,
            )

        ahead = score(0)
        waiting = None
        for p in range(PAIRS + 1):
            scores = ahead
            if p + 1 < PAIRS:
                ahead = score(p + 1)
            if p % 2 == 0 and p < PAIRS:
                project(1 - slot, p // 2)
                project(1 - slot, 3 + p // 2)
            if waiting is not None:
                weights, factor = waiting
                top = (p - 1) * BLK
                mid = top + HEAD_DIM
                end = top + BLK
                mixed = jnp.dot(values[slot, top:end, :], weights, preferred_element_type=F32)
                sums[q, top:mid, :] = (
                    sums[q, top:mid, :] * factor[:, :BLK] + mixed[:HEAD_DIM, :BLK]
                )
                sums[q, mid:end, :] = (
                    sums[q, mid:end, :] * factor[:, BLK:] + mixed[HEAD_DIM:, BLK:]
                )
            if p < PAIRS:
                old = peak[q, p : p + 1, :]
                new = jnp.maximum(old, jnp.max(scores, axis=0, keepdims=True))
                expo = jnp.exp2((scores - new) * scale)
                factor = jnp.exp2((old - new) * scale)
                peak[q, p : p + 1, :] = new
                add = total[q, p : p + 1, :] * factor
                for g in range(GROUP):
                    some = jnp.sum(expo[g * ROWS : (g + 1) * ROWS], axis=0, keepdims=True)
                    add = add + (some if g == 0 else jnp.where(g < live, some, 0.0))
                total[q, p : p + 1, :] = add
                waiting = (expo.astype(BF), factor)
        return 0

    lax.fori_loop(0, steps, step, 0)
    if last:
        for q in range(blocks):
            done = []
            for p in range(PAIRS):
                for h in range(2):
                    top = p * BLK + h * HEAD_DIM
                    done.append(
                        sums[q, top : top + HEAD_DIM, :]
                        / total[q, p : p + 1, h * BLK : (h + 1) * BLK]
                    )
            attended = jnp.transpose(jnp.concatenate(done, axis=0)).astype(BF)
            out_ref[q * BLK : (q + 1) * BLK, :] = jnp.dot(
                attended, wo_ref[...], preferred_element_type=F32
            ).astype(BF)


def on_device(query_tokens, source_tokens, w_query, w_keyval, w_out, slab_map, neighbours, counts):
    blocks = neighbours.shape[0]
    place = lax.axis_index("pb").astype(I32)
    me = jnp.stack(
        [place // 16, place // 4 % 4, place % 4, lax.axis_index("ka").astype(I32)]
    )
    flat_counts = counts.reshape(-1)
    table = pl.pallas_call(
        lambda *refs: table_kernel(blocks, *refs),
        out_shape=jax.ShapeDtypeStruct((2, 128), I32),
        in_specs=[SMEM] * 4,
        out_specs=SMEM,
        name="tables",
    )(me, neighbours.reshape(-1), flat_counts, slab_map.reshape(-1))
    note = jnp.pad(table[:1].astype(BF), ((0, 15), (0, CUT - 128)))
    tall = PARTS * BLK
    heard = []
    lines = []
    for part, (_, axis, _) in enumerate(ROUTES):
        own = source_tokens[:, :, part * CUT : (part + 1) * CUT].reshape(tall, CUT)
        own = jnp.concatenate([own, note])
        told = [own] + [shift(own, axis, d) for d in range(1, SIDE)]
        heard.append([t[tall, :128].astype(I32) for t in told])
        lines.append(jnp.stack(told))
    source = {first: part for part, (_, first, _) in enumerate(ROUTES)}
    rows = [table[0]]
    for across, _, _ in ROUTES:
        rows += [heard[source[across]][SIDE - d] for d in range(1, SIDE)]
    wishes = jnp.stack(rows + [table[1]])
    partner = swap(wishes)
    wishes = wishes + partner
    partner = partner[9:]

    everything = [[] for _ in range(HALVES)]
    for part, (across, _, axis) in enumerate(ROUTES):
        gathered = [lines[part]] + [shift(lines[part], axis, d) for d in range(1, SIDE)]
        chosen = pl.pallas_call(
            lambda *refs: select_kernel(part, *refs),
            out_shape=[jax.ShapeDtypeStruct((SIDE * SIDE, ROWS, CUT), BF)] * (SIDE * HALVES),
            in_specs=[SMEM] * 2 + [VMEM] * SIDE,
            out_specs=[VMEM] * (SIDE * HALVES),
            compiler_params=pltpu.CompilerParams(vmem_limit_bytes=SELECT_VMEM),
            name="select",
        )(me, wishes, *gathered)
        for half in range(HALVES):
            ours = chosen[half * SIDE :][:SIDE]
            everything[half] += [ours[0]] + [shift(ours[d], across, d) for d in range(1, SIDE)]
    state = [
        jax.ShapeDtypeStruct((blocks, 8, 2 * BLK), F32),
        jax.ShapeDtypeStruct((blocks, 8, 2 * BLK), F32),
        jax.ShapeDtypeStruct((blocks, WIDTH, BLK), F32),
    ]
    w_keys = w_keyval[:, :WIDTH]
    w_values = jnp.transpose(w_keyval[:, WIDTH:])
    carried = []
    for half, arrived in enumerate(everything):
        handed = pl.pallas_call(
            hand_kernel,
            out_shape=jax.ShapeDtypeStruct((blocks * CAP, ROWS, WIDTH), BF),
            in_specs=[SMEM] * 2 + [HBM] * 12,
            out_specs=VMEM,
            scratch_shapes=[pltpu.SemaphoreType.DMA((blocks * CAP,))],
            name="hand",
        )(me, partner, *arrived)
        handed = swap(handed)
        first = half == 0
        last = half == HALVES - 1
        items = blocks * -(-2 * CAP // GROUP)
        carried = pl.pallas_call(
            lambda *refs: attend_kernel(first, last, *refs),
            out_shape=jax.ShapeDtypeStruct(query_tokens.shape, BF) if last else state,
            in_specs=[SMEM] * 3 + [VMEM] * 5 + [HBM] * 13 + [VMEM] * len(carried),
            out_specs=VMEM if last else [VMEM] * 3,
            scratch_shapes=[
                pltpu.SMEM((items,), I32),
                pltpu.SMEM((items,), I32),
                pltpu.SMEM((items * GROUP,), I32),
                pltpu.VMEM((2, ITEM, WIDTH), BF),
                pltpu.VMEM((2, ITEM, WIDTH), BF),
                pltpu.VMEM((2, WIDTH, ITEM), BF),
                pltpu.VMEM((blocks, PAIRS, 2 * BLK, BLK), BF),
                pltpu.SemaphoreType.DMA((2,)),
            ]
            + ([pltpu.VMEM(s.shape, s.dtype) for s in state] if last else []),
            name="attend",
        )(
            me,
            table,
            flat_counts,
            query_tokens,
            w_query,
            w_keys,
            w_values,
            w_out,
            *arrived,
            handed,
            *carried,
        )
    return carried


def solution(mesh):
    placed = (
        P(("pb", "ka"), None),
        P(None, ("pb", "ka"), None),
        P(),
        P(),
        P(),
        P(),
        P(("pb", "ka"), None, None),
        P(("pb", "ka"), None),
    )

    return jax.shard_map(
        on_device, mesh=mesh, in_specs=placed, out_specs=P(("pb", "ka"), None), check_vma=False
    )
```

```python
import jax
import jax.numpy as jnp
from jax import lax
from jax.experimental import pallas as pl
from jax.experimental.pallas import tpu as pltpu
from jax.sharding import PartitionSpec as P

HEADS = 12
HEAD_DIM = 64
BLK = 128
CAP = 6
WIDTH = HEADS * HEAD_DIM
PARTS = 3
CUT = WIDTH // PARTS
SIDE = 4
PAIRS = HEADS // 2
HALVES = 1
SELECT_VMEM = 8 << 20
ROWS = BLK // HALVES
GROUP = 2 * BLK // ROWS
ITEM = GROUP * ROWS
BF = jnp.bfloat16
F32 = jnp.float32
I32 = jnp.int32
STRIDE = (SIDE * SIDE, SIDE, 1)
ROUTES = ((2, 0, 1), (1, 2, 0), (0, 1, 2))
LOG2E = 1.4426950408889634


SMEM = pl.BlockSpec(memory_space=pltpu.SMEM)
VMEM = pl.BlockSpec(memory_space=pltpu.VMEM)
HBM = pl.BlockSpec(memory_space=pltpu.HBM)


def shift(value, axis, step):
    stride = STRIDE[axis]
    pairs = []
    for source in range(SIDE**3):
        at = source // stride % SIDE
        pairs.append((source, source + ((at + step) % SIDE - at) * stride))
    return lax.ppermute(value, "pb", pairs)


def swap(value):
    return lax.ppermute(value, "ka", [(0, 1), (1, 0)])


def table_kernel(blocks, near_ref, count_ref, map_ref, out_ref):
    def clear(i, _):
        for k in range(8):
            out_ref[0, i * 8 + k] = 0
            out_ref[1, i * 8 + k] = -1
        return 0

    lax.fori_loop(0, 16, clear, 0)
    key_blocks = map_ref.shape[1]
    mine = lax.axis_index("pb")
    for slab in range(2):
        for q in range(blocks):
            live = count_ref[q, slab]
            for j in range(CAP):

                @pl.when(j < live)
                def _():
                    entry = near_ref[q, slab, j]
                    one = (entry >= key_blocks).astype(I32)
                    two = (entry >= 2 * key_blocks).astype(I32)
                    contrast = one + two
                    stored = map_ref[contrast, entry - contrast * key_blocks]
                    owner = lax.shift_right_logical(stored, 1)
                    out_ref[0, slab * 64 + owner] = 1 + contrast
                    away = (mine & 48) + 64 - (owner & 48) & 48
                    away = away | ((mine & 12) + 16 - (owner & 12) & 12)
                    away = away | ((mine & 3) + 4 - (owner & 3) & 3)
                    out_ref[1, (slab * blocks + q) * CAP + j] = away


def select_kernel(part, me_ref, table_ref, *refs):
    across, first, second = ROUTES[part]
    gathered = refs[: 2 * SIDE]
    outs = refs[2 * SIDE : 3 * SIDE]
    sem = refs[-1]

    def each(ways, run):
        for d2 in range(SIDE):
            for d1 in range(SIDE):
                at = [None, None, None]
                at[across] = me_ref[across]
                at[first] = me_ref[first] + 4 - d1 & 3
                at[second] = me_ref[second] + 4 - d2 & 3
                place = me_ref[3] * 64 + at[0] * 16 + at[1] * 4 + at[2]
                line, row = gathered[d2 * 2 + d1 // 2], d1 % 2
                for d in ways:
                    which = table_ref[0 if d == 0 else 3 * part + d, place]
                    begin = pl.multiple_of(jnp.maximum(which - 1, 0) * BLK, BLK)
                    run(line.at[row, pl.ds(begin, BLK)], outs[d].at[d2 * 4 + d1])

    def send(source, target):
        pltpu.make_async_copy(source, target, sem).start()

    def copy(source, target):
        target[...] = source[...]

    each((0,), send)
    each((1, 2, 3), copy)
    pltpu.make_async_copy(outs[0], outs[0], sem).wait()


def fetch_parts(code, arrived, target, sem_of):
    away = (lax.shift_right_logical(code, 4), lax.shift_right_logical(code, 2) & 3, code & 3)
    for part, (across, first, second) in enumerate(ROUTES):
        for d in range(SIDE):

            @pl.when(away[across] == d)
            def _():
                pltpu.make_async_copy(
                    arrived[part][d].at[away[second] * 4 + away[first]],
                    target(part),
                    sem_of(part),
                ).start()


def hand_kernel(me_ref, code_ref, *refs):
    arrived = [refs[4 * part : 4 + 4 * part] for part in range(PARTS)]
    out, sems = refs[12:]
    count = out.shape[0]

    def start(i, _):
        code = code_ref[1, me_ref[3] * count + i]

        @pl.when(code >= 0)
        def _():
            fetch_parts(
                jnp.maximum(code, 0),
                arrived,
                lambda part: out.at[i, :, pl.ds(part * CUT, CUT)],
                lambda part: sems.at[i],
            )

        return 0

    def finish(i, _):
        @pl.when(code_ref[1, me_ref[3] * count + i] >= 0)
        def _():
            pltpu.make_async_copy(out.at[i], out.at[i], sems.at[i]).wait()

        return 0

    lax.fori_loop(0, count, start, 0)
    lax.fori_loop(0, count, finish, 0)


def attend_kernel(first, last, *refs):
    refs = list(refs)
    me_ref, code_ref, count_ref, xq_ref, wq_ref, wk_ref, wvt_ref, wo_ref = refs[:8]
    arrived = [refs[8 + 4 * part : 12 + 4 * part] for part in range(PARTS)]
    handed = refs[20]
    refs = refs[21:]
    if not first:
        before = refs[:3]
        refs = refs[3:]
    if last:
        out_ref = refs.pop(0)
        peak, total, sums = refs[-3:]
    else:
        peak, total, sums = refs[:3]
        refs = refs[3:]
    item_q, item_n, item_code, tokens, keys, values, spread, sems = refs[:8]
    blocks = xq_ref.shape[0] // BLK
    mine = me_ref[3]
    span = blocks * CAP

    def plan_block(q, begun):
        own = count_ref[q, mine]
        live = own + count_ref[q, 1 - mine]

        def plan_item(k, _):
            t = begun + k
            item_q[t] = q
            item_n[t] = live - GROUP * k
            for g in range(GROUP):
                i = jnp.where(GROUP * k + g < live, GROUP * k + g, GROUP * k)
                near = code_ref[1, mine * span + q * CAP + jnp.minimum(i, own - 1)]
                item_code[t * GROUP + g] = jnp.where(i < own, near, 64 + q * CAP + i - own)
            return 0

        items = lax.div(live + GROUP - 1, GROUP)
        lax.fori_loop(0, items, plan_item, 0)
        return begun + items

    steps = lax.fori_loop(0, blocks, plan_block, 0)

    def fetch(t):
        slot = t & 1
        for g in range(GROUP):
            code = item_code[t * GROUP + g]
            rows = pl.ds(g * ROWS, ROWS)

            @pl.when(code < 64)
            def _():
                fetch_parts(
                    code,
                    arrived,
                    lambda part: tokens.at[slot, rows, pl.ds(part * CUT, CUT)],
                    lambda part: sems.at[slot],
                )

            @pl.when(code >= 64)
            def _():
                pltpu.make_async_copy(
                    handed.at[jnp.maximum(code - 64, 0)], tokens.at[slot, rows], sems.at[slot]
                ).start()

    def landed(slot):
        pltpu.make_async_copy(tokens.at[slot], tokens.at[slot], sems.at[slot]).wait()

    def project(slot, chunk):
        part = pl.ds(chunk % 3 * CUT, CUT)
        if chunk < 3:
            keys[slot, :, part] = jnp.dot(
                tokens[slot], wk_ref[:, part], preferred_element_type=F32
            ).astype(BF)
        else:
            values[slot, part, :] = lax.dot_general(
                wvt_ref[part, :],
                tokens[slot],
                (((1,), (1,)), ((), ())),
                preferred_element_type=F32,
            ).astype(BF)

    fetch(0)
    fetch(1)
    low = lax.broadcasted_iota(I32, (BLK, BLK), 1) < HEAD_DIM
    zero = jnp.zeros((BLK, BLK), BF)
    for q in range(blocks):
        queries = jnp.dot(
            xq_ref[q * BLK : (q + 1) * BLK, :], wq_ref[...], preferred_element_type=F32
        ).astype(BF)
        for p in range(PAIRS):
            two = queries[:, p * BLK : (p + 1) * BLK]
            spread[q, p, :BLK, :] = jnp.where(low, two, zero)
            spread[q, p, BLK:, :] = jnp.where(low, zero, two)
    if first:
        peak[...] = jnp.full_like(peak, -jnp.inf)
        total[...] = jnp.zeros_like(total)
        sums[...] = jnp.zeros_like(sums)
    else:
        for mine_ref, old_ref in zip((peak, total, sums), before):
            mine_ref[...] = old_ref[...]
    landed(0)
    for chunk in range(6):
        project(0, chunk)

    def step(t, _):
        slot = t & 1
        q = item_q[t]
        live = item_n[t]

        @pl.when(t + 2 < steps)
        def _():
            fetch(t + 2)

        for g in range(1, GROUP):

            @pl.when(live <= g)
            def _():
                values[slot, :, pl.ds(g * ROWS, ROWS)] = jnp.zeros((WIDTH, ROWS), BF)

        @pl.when(t + 1 < steps)
        def _():
            landed(1 - slot)

        scale = HEAD_DIM**-0.5 * LOG2E

        def score(p):
            return lax.dot_general(
                keys[slot, :, p * BLK : (p + 1) * BLK],
                spread[q, p],
                (((1,), (1,)), ((), ())),
                preferred_element_type=F32,
            )

        ahead = score(0)
        waiting = None
        for p in range(PAIRS + 1):
            scores = ahead
            if p + 1 < PAIRS:
                ahead = score(p + 1)
            if p % 2 == 0 and p < PAIRS:
                project(1 - slot, p // 2)
                project(1 - slot, 3 + p // 2)
            if waiting is not None:
                weights, factor = waiting
                top = (p - 1) * BLK
                mid = top + HEAD_DIM
                end = top + BLK
                mixed = jnp.dot(values[slot, top:end, :], weights, preferred_element_type=F32)
                sums[q, top:mid, :] = (
                    sums[q, top:mid, :] * factor[:, :BLK] + mixed[:HEAD_DIM, :BLK]
                )
                sums[q, mid:end, :] = (
                    sums[q, mid:end, :] * factor[:, BLK:] + mixed[HEAD_DIM:, BLK:]
                )
            if p < PAIRS:
                old = peak[q, p : p + 1, :]
                new = jnp.maximum(old, jnp.max(scores, axis=0, keepdims=True))
                expo = jnp.exp2((scores - new) * scale)
                factor = jnp.exp2((old - new) * scale)
                peak[q, p : p + 1, :] = new
                add = total[q, p : p + 1, :] * factor
                for g in range(GROUP):
                    some = jnp.sum(expo[g * ROWS : (g + 1) * ROWS], axis=0, keepdims=True)
                    add = add + (some if g == 0 else jnp.where(g < live, some, 0.0))
                total[q, p : p + 1, :] = add
                waiting = (expo.astype(BF), factor)
        return 0

    lax.fori_loop(0, steps, step, 0)
    if last:
        for q in range(blocks):
            done = []
            for p in range(PAIRS):
                for h in range(2):
                    top = p * BLK + h * HEAD_DIM
                    done.append(
                        sums[q, top : top + HEAD_DIM, :]
                        / total[q, p : p + 1, h * BLK : (h + 1) * BLK]
                    )
            attended = jnp.transpose(jnp.concatenate(done, axis=0)).astype(BF)
            out_ref[q * BLK : (q + 1) * BLK, :] = jnp.dot(
                attended, wo_ref[...], preferred_element_type=F32
            ).astype(BF)


def on_device(query_tokens, source_tokens, w_query, w_keyval, w_out, slab_map, neighbours, counts):
    blocks = neighbours.shape[0]
    place = lax.axis_index("pb").astype(I32)
    me = jnp.stack(
        [place // 16, place // 4 % 4, place % 4, lax.axis_index("ka").astype(I32)]
    )
    table = pl.pallas_call(
        lambda *refs: table_kernel(blocks, *refs),
        out_shape=jax.ShapeDtypeStruct((2, 128), I32),
        in_specs=[SMEM] * 3,
        out_specs=SMEM,
        name="tables",
    )(neighbours, counts, slab_map)
    note = jnp.pad(table[:1].astype(BF), ((0, 15), (0, CUT - 128)))
    tall = PARTS * BLK
    heard = []
    lines = []
    for part, (_, axis, _) in enumerate(ROUTES):
        own = source_tokens[:, :, part * CUT : (part + 1) * CUT].reshape(tall, CUT)
        own = jnp.concatenate([own, note])
        right, left = shift(own, axis, 1), shift(own, axis, -1)
        told = [own, right, shift(right, axis, 1), left]
        heard.append([t[tall, :128].astype(I32) for t in told])
        lines.append((jnp.stack(told[:2]), jnp.stack(told[2:])))
    source = {first: part for part, (_, first, _) in enumerate(ROUTES)}
    rows = [table[0]]
    for across, _, _ in ROUTES:
        rows += [heard[source[across]][SIDE - d] for d in range(1, SIDE)]
    wishes = jnp.stack(rows + [table[1]])
    partner = swap(wishes)
    wishes = wishes + partner
    partner = partner[9:]

    everything = [[] for _ in range(HALVES)]
    for part, (across, _, axis) in enumerate(ROUTES):
        right = [shift(half, axis, 1) for half in lines[part]]
        left = [shift(half, axis, -1) for half in lines[part]]
        far = [shift(right[0], axis, 1), shift(left[1], axis, -1)]
        gathered = [*lines[part], *right, *far, *left]
        chosen = pl.pallas_call(
            lambda *refs: select_kernel(part, *refs),
            out_shape=[jax.ShapeDtypeStruct((SIDE * SIDE, BLK, CUT), BF)] * SIDE,
            in_specs=[SMEM] * 2 + [VMEM] * (2 * SIDE),
            out_specs=[HBM] + [VMEM] * (SIDE - 1),
            scratch_shapes=[pltpu.SemaphoreType.DMA],
            compiler_params=pltpu.CompilerParams(vmem_limit_bytes=SELECT_VMEM),
            name="select",
        )(me, wishes, *gathered)
        for half in range(HALVES):
            ours = chosen[half * SIDE :][:SIDE]
            everything[half] += [ours[0]] + [shift(ours[d], across, d) for d in range(1, SIDE)]
    state = [
        jax.ShapeDtypeStruct((blocks, 8, 2 * BLK), F32),
        jax.ShapeDtypeStruct((blocks, 8, 2 * BLK), F32),
        jax.ShapeDtypeStruct((blocks, WIDTH, BLK), F32),
    ]
    carried = []
    for half, arrived in enumerate(everything):
        handed = pl.pallas_call(
            hand_kernel,
            out_shape=jax.ShapeDtypeStruct((blocks * CAP, ROWS, WIDTH), BF),
            in_specs=[SMEM] * 2 + [HBM] * 12,
            out_specs=VMEM,
            scratch_shapes=[pltpu.SemaphoreType.DMA((blocks * CAP,))],
            name="hand",
        )(me, partner, *arrived)
        handed = swap(handed)
        first = half == 0
        last = half == HALVES - 1
        items = blocks * -(-2 * CAP // GROUP)
        carried = pl.pallas_call(
            lambda *refs: attend_kernel(first, last, *refs),
            out_shape=jax.ShapeDtypeStruct(query_tokens.shape, BF) if last else state,
            in_specs=[SMEM] * 3 + [VMEM] * 5 + [HBM] * 13 + [VMEM] * len(carried),
            out_specs=VMEM if last else [VMEM] * 3,
            scratch_shapes=[
                pltpu.SMEM((items,), I32),
                pltpu.SMEM((items,), I32),
                pltpu.SMEM((items * GROUP,), I32),
                pltpu.VMEM((2, ITEM, WIDTH), BF),
                pltpu.VMEM((2, ITEM, WIDTH), BF),
                pltpu.VMEM((2, WIDTH, ITEM), BF),
                pltpu.VMEM((blocks, PAIRS, 2 * BLK, BLK), BF),
                pltpu.SemaphoreType.DMA((2,)),
            ]
            + ([pltpu.VMEM(s.shape, s.dtype) for s in state] if last else []),
            name="attend",
        )(
            me,
            table,
            counts,
            query_tokens,
            w_query,
            w_keyval[:, :WIDTH],
            jnp.transpose(w_keyval[:, WIDTH:]),
            w_out,
            *arrived,
            handed,
            *carried,
        )
    return carried


def solution(mesh):
    placed = (
        P(("pb", "ka"), None),
        P(None, ("pb", "ka"), None),
        P(),
        P(),
        P(),
        P(),
        P(("pb", "ka"), None, None),
        P(("pb", "ka"), None),
    )
    return jax.shard_map(
        on_device, mesh=mesh, in_specs=placed, out_specs=P(("pb", "ka"), None), check_vma=False
    )
```

```python
import jax
import jax.numpy as jnp
from jax import lax
from jax.experimental import pallas as pl
from jax.experimental.pallas import tpu as pltpu
from jax.sharding import PartitionSpec as P


HEADS = 12
HEAD_DIM = 64
BLK = 128
CAP = 6
WIDTH = HEADS * HEAD_DIM
PARTS = 3
CUT = WIDTH // PARTS
SIDE = 4
PAIRS = HEADS // 2
HALVES = 1
SELECT_VMEM = 8 << 20
ROWS = BLK // HALVES
GROUP = 2 * BLK // ROWS
ITEM = GROUP * ROWS
BF = jnp.bfloat16
F32 = jnp.float32
I32 = jnp.int32
STRIDE = (SIDE * SIDE, SIDE, 1)
ROUTES = ((2, 0, 1), (1, 2, 0), (0, 1, 2))
LOG2E = 1.4426950408889634


SMEM = pl.BlockSpec(memory_space=pltpu.SMEM)
VMEM = pl.BlockSpec(memory_space=pltpu.VMEM)
HBM = pl.BlockSpec(memory_space=pltpu.HBM)


def shift(value, axis, step):
    stride = STRIDE[axis]
    pairs = []
    for source in range(SIDE**3):
        at = source // stride % SIDE
        pairs.append((source, source + ((at + step) % SIDE - at) * stride))
    return lax.ppermute(value, "pb", pairs)


def swap(value):
    return lax.ppermute(value, "ka", [(0, 1), (1, 0)])


def table_kernel(blocks, near_ref, count_ref, map_ref, out_ref):
    def clear(i, _):
        for k in range(8):
            out_ref[0, i * 8 + k] = 0
            out_ref[1, i * 8 + k] = -1
        return 0

    lax.fori_loop(0, 16, clear, 0)
    key_blocks = map_ref.shape[1]
    mine = lax.axis_index("pb")
    for slab in range(2):
        for q in range(blocks):
            live = count_ref[q, slab]
            for j in range(CAP):

                @pl.when(j < live)
                def _():
                    entry = near_ref[q, slab, j]
                    one = (entry >= key_blocks).astype(I32)
                    two = (entry >= 2 * key_blocks).astype(I32)
                    contrast = one + two
                    stored = map_ref[contrast, entry - contrast * key_blocks]
                    owner = lax.shift_right_logical(stored, 1)
                    out_ref[0, slab * 64 + owner] = 1 + contrast
                    away = (mine & 48) + 64 - (owner & 48) & 48
                    away = away | ((mine & 12) + 16 - (owner & 12) & 12)
                    away = away | ((mine & 3) + 4 - (owner & 3) & 3)
                    out_ref[1, (slab * blocks + q) * CAP + j] = away


def walk_slots(part, me_ref, table_ref, gathered, outs):
    across, first, second = ROUTES[part]
    for d2 in range(SIDE):
        for d1 in range(SIDE):
            at = [None, None, None]
            at[across] = me_ref[across]
            at[first] = me_ref[first] + 4 - d1 & 3
            at[second] = me_ref[second] + 4 - d2 & 3
            place = me_ref[3] * 64 + at[0] * 16 + at[1] * 4 + at[2]
            line, row = gathered[d2 * 2 + d1 // 2], d1 % 2
            for d, out in outs:
                which = table_ref[0 if d == 0 else 3 * part + d, place]
                begin = pl.multiple_of(jnp.maximum(which - 1, 0) * BLK, BLK)
                out[d2 * 4 + d1] = line[row, pl.ds(begin, BLK), :]


def select_kernel(part, me_ref, table_ref, *refs):
    walk_slots(part, me_ref, table_ref, refs[:8], list(enumerate(refs[8:], 1)))


def own_kernel(me_ref, table_ref, *refs):
    for part in range(PARTS):
        walk_slots(part, me_ref, table_ref, refs[8 * part : 8 * part + 8], [(0, refs[24 + part])])


def spread_kernel(xq_ref, wq_ref, spread):
    low = lax.broadcasted_iota(I32, (BLK, BLK), 1) < HEAD_DIM
    zero = jnp.zeros((BLK, BLK), BF)
    for q in range(xq_ref.shape[0] // BLK):
        queries = jnp.dot(
            xq_ref[q * BLK : (q + 1) * BLK, :], wq_ref[...], preferred_element_type=F32
        ).astype(BF)
        for p in range(PAIRS):
            two = queries[:, p * BLK : (p + 1) * BLK]
            spread[q, p, :BLK, :] = jnp.where(low, two, zero)
            spread[q, p, BLK:, :] = jnp.where(low, zero, two)


def fetch_parts(code, arrived, target, sem_of):
    away = (lax.shift_right_logical(code, 4), lax.shift_right_logical(code, 2) & 3, code & 3)
    for part, (across, first, second) in enumerate(ROUTES):
        for d in range(SIDE):

            @pl.when(away[across] == d)
            def _():
                pltpu.make_async_copy(
                    arrived[part][d].at[away[second] * 4 + away[first]],
                    target(part),
                    sem_of(part),
                ).start()


def hand_kernel(part, me_ref, code_ref, *refs):
    arrived = refs[:SIDE]
    out, sem = refs[SIDE:]
    count = out.shape[0]
    across, first, second = ROUTES[part]
    shifts = (4, 2, 0)

    def start(i, _):
        code = jnp.maximum(code_ref[1, me_ref[3] * count + i], 0)
        away = [lax.shift_right_logical(code, shifts[axis]) & 3 for axis in range(3)]
        for d in range(SIDE):

            @pl.when(away[across] == d)
            def _():
                pltpu.make_async_copy(
                    arrived[d].at[away[second] * 4 + away[first]], out.at[i], sem
                ).start()

        return 0

    lax.fori_loop(0, count, start, 0)
    pltpu.make_async_copy(out, out, sem).wait()


def attend_kernel(first, last, *refs):
    refs = list(refs)
    me_ref, code_ref, count_ref, spread, wk_ref, wvt_ref, wo_ref = refs[:7]
    arrived = [refs[7 + 4 * part : 11 + 4 * part] for part in range(PARTS)]
    handed = refs[19:22]
    refs = refs[22:]
    if not first:
        before = refs[:3]
        refs = refs[3:]
    if last:
        out_ref = refs.pop(0)
        peak, total, sums = refs[-3:]
    else:
        peak, total, sums = refs[:3]
        refs = refs[3:]
    item_q, item_n, item_code, tokens, keys, values, sems = refs[:7]
    blocks = spread.shape[0]
    mine = me_ref[3]
    span = blocks * CAP

    def plan_block(q, begun):
        own = count_ref[q, mine]
        live = own + count_ref[q, 1 - mine]

        def plan_item(k, _):
            t = begun + k
            item_q[t] = q
            item_n[t] = live - GROUP * k
            for g in range(GROUP):
                i = jnp.where(GROUP * k + g < live, GROUP * k + g, GROUP * k)
                near = code_ref[1, mine * span + q * CAP + jnp.minimum(i, own - 1)]
                item_code[t * GROUP + g] = jnp.where(i < own, near, 64 + q * CAP + i - own)
            return 0

        items = lax.div(live + GROUP - 1, GROUP)
        lax.fori_loop(0, items, plan_item, 0)
        return begun + items

    steps = lax.fori_loop(0, blocks, plan_block, 0)

    def fetch(t):
        slot = t & 1
        for g in range(GROUP):
            code = item_code[t * GROUP + g]
            rows = pl.ds(g * ROWS, ROWS)

            @pl.when(code < 64)
            def _():
                fetch_parts(
                    code,
                    arrived,
                    lambda part: tokens.at[slot, rows, pl.ds(part * CUT, CUT)],
                    lambda part: sems.at[slot],
                )

            @pl.when(code >= 64)
            def _():
                for part in range(PARTS):
                    pltpu.make_async_copy(
                        handed[part].at[jnp.maximum(code - 64, 0)],
                        tokens.at[slot, rows, pl.ds(part * CUT, CUT)],
                        sems.at[slot],
                    ).start()

    def landed(slot):
        pltpu.make_async_copy(tokens.at[slot], tokens.at[slot], sems.at[slot]).wait()

    def project(slot, chunk):
        part = pl.ds(chunk % 3 * CUT, CUT)
        if chunk < 3:
            keys[slot, :, part] = jnp.dot(
                tokens[slot], wk_ref[:, part], preferred_element_type=F32
            ).astype(BF)
        else:
            values[slot, part, :] = lax.dot_general(
                wvt_ref[part, :],
                tokens[slot],
                (((1,), (1,)), ((), ())),
                preferred_element_type=F32,
            ).astype(BF)

    fetch(0)
    fetch(1)
    if first:
        peak[...] = jnp.full_like(peak, -jnp.inf)
        total[...] = jnp.zeros_like(total)
        sums[...] = jnp.zeros_like(sums)
    else:
        for mine_ref, old_ref in zip((peak, total, sums), before):
            mine_ref[...] = old_ref[...]
    landed(0)
    for chunk in range(6):
        project(0, chunk)

    def step(t, _):
        slot = t & 1
        q = item_q[t]
        live = item_n[t]

        @pl.when(t + 2 < steps)
        def _():
            fetch(t + 2)

        for g in range(1, GROUP):

            @pl.when(live <= g)
            def _():
                values[slot, :, pl.ds(g * ROWS, ROWS)] = jnp.zeros((WIDTH, ROWS), BF)

        @pl.when(t + 1 < steps)
        def _():
            landed(1 - slot)

        scale = HEAD_DIM**-0.5 * LOG2E

        def score(p):
            return lax.dot_general(
                keys[slot, :, p * BLK : (p + 1) * BLK],
                spread[q, p],
                (((1,), (1,)), ((), ())),
                preferred_element_type=F32,
            )

        ahead = score(0)
        waiting = None
        for p in range(PAIRS + 1):
            scores = ahead
            if p + 1 < PAIRS:
                ahead = score(p + 1)
            if p % 2 == 0 and p < PAIRS:
                project(1 - slot, p // 2)
                project(1 - slot, 3 + p // 2)
            if waiting is not None:
                weights, factor = waiting
                top = (p - 1) * BLK
                mid = top + HEAD_DIM
                end = top + BLK
                mixed = jnp.dot(values[slot, top:end, :], weights, preferred_element_type=F32)
                sums[q, top:mid, :] = (
                    sums[q, top:mid, :] * factor[:, :BLK] + mixed[:HEAD_DIM, :BLK]
                )
                sums[q, mid:end, :] = (
                    sums[q, mid:end, :] * factor[:, BLK:] + mixed[HEAD_DIM:, BLK:]
                )
            if p < PAIRS:
                old = peak[q, p : p + 1, :]
                new = jnp.maximum(old, jnp.max(scores, axis=0, keepdims=True))
                expo = jnp.exp2((scores - new) * scale)
                factor = jnp.exp2((old - new) * scale)
                peak[q, p : p + 1, :] = new
                add = total[q, p : p + 1, :] * factor
                for g in range(GROUP):
                    some = jnp.sum(expo[g * ROWS : (g + 1) * ROWS], axis=0, keepdims=True)
                    add = add + (some if g == 0 else jnp.where(g < live, some, 0.0))
                total[q, p : p + 1, :] = add
                waiting = (expo.astype(BF), factor)
        return 0

    lax.fori_loop(0, steps, step, 0)
    if last:
        for q in range(blocks):
            done = []
            for p in range(PAIRS):
                for h in range(2):
                    top = p * BLK + h * HEAD_DIM
                    done.append(
                        sums[q, top : top + HEAD_DIM, :]
                        / total[q, p : p + 1, h * BLK : (h + 1) * BLK]
                    )
            attended = jnp.transpose(jnp.concatenate(done, axis=0)).astype(BF)
            out_ref[q * BLK : (q + 1) * BLK, :] = jnp.dot(
                attended, wo_ref[...], preferred_element_type=F32
            ).astype(BF)


def on_device(query_tokens, source_tokens, w_query, w_keyval, w_out, slab_map, neighbours, counts):
    blocks = neighbours.shape[0]
    place = lax.axis_index("pb").astype(I32)
    me = jnp.stack(
        [place // 16, place // 4 % 4, place % 4, lax.axis_index("ka").astype(I32)]
    )
    table = pl.pallas_call(
        lambda *refs: table_kernel(blocks, *refs),
        out_shape=jax.ShapeDtypeStruct((2, 128), I32),
        in_specs=[SMEM] * 3,
        out_specs=SMEM,
        name="tables",
    )(neighbours, counts, slab_map)
    note = jnp.pad(table[:1].astype(BF), ((0, 15), (0, CUT - 128)))
    tall = PARTS * BLK
    heard = []
    lines = []
    for part, (_, axis, _) in enumerate(ROUTES):
        own = source_tokens[:, :, part * CUT : (part + 1) * CUT].reshape(tall, CUT)
        own = jnp.concatenate([own, note])
        right, left = shift(own, axis, 1), shift(own, axis, -1)
        told = [own, right, shift(right, axis, 1), left]
        heard.append([t[tall, :128].astype(I32) for t in told])
        lines.append((jnp.stack(told[:2]), jnp.stack(told[2:])))
    source = {first: part for part, (_, first, _) in enumerate(ROUTES)}
    rows = [table[0]]
    for across, _, _ in ROUTES:
        rows += [heard[source[across]][SIDE - d] for d in range(1, SIDE)]
    wishes = jnp.stack(rows + [table[1]])
    partner = swap(wishes)
    wishes = wishes + partner
    partner = partner[9:]

    w_keys = w_keyval[:, :WIDTH]
    w_values = jnp.transpose(w_keyval[:, WIDTH:])
    wishes, w_keys, w_values = lax.optimization_barrier((wishes, w_keys, w_values))
    slots = jax.ShapeDtypeStruct((SIDE * SIDE, BLK, CUT), BF)
    small = pltpu.CompilerParams(vmem_limit_bytes=SELECT_VMEM)
    gathered = []
    arrived = []
    for part, (across, _, axis) in enumerate(ROUTES):
        right = [shift(half, axis, 1) for half in lines[part]]
        left = [shift(half, axis, -1) for half in lines[part]]
        far = [shift(right[0], axis, 1), shift(left[1], axis, -1)]
        gathered.append([*lines[part], *right, *far, *left])
        chosen = pl.pallas_call(
            lambda *refs: select_kernel(part, *refs),
            out_shape=[slots] * (SIDE - 1),
            in_specs=[SMEM] * 2 + [VMEM] * 8,
            out_specs=[VMEM] * (SIDE - 1),
            compiler_params=small,
            name="select",
        )(me, wishes, *gathered[part])
        arrived.append([shift(chosen[d - 1], across, d) for d in range(1, SIDE)])
    own_slots = pl.pallas_call(
        own_kernel,
        out_shape=[slots] * PARTS,
        in_specs=[SMEM] * 2 + [VMEM] * 24,
        out_specs=[VMEM] * PARTS,
        compiler_params=small,
        name="own",
    )(me, wishes, *[a for part in gathered for a in part])
    spread = pl.pallas_call(
        spread_kernel,
        out_shape=jax.ShapeDtypeStruct((blocks, PAIRS, 2 * BLK, BLK), BF),
        in_specs=[VMEM] * 2,
        out_specs=VMEM,
        compiler_params=small,
        name="spread",
    )(query_tokens, w_query)
    arrived = [[own_slots[part]] + arrived[part] for part in range(PARTS)]
    items = blocks * -(-2 * CAP // GROUP)
    handed = []
    for part in range(PARTS):
        given = pl.pallas_call(
            lambda *refs: hand_kernel(part, *refs),
            out_shape=jax.ShapeDtypeStruct((blocks * CAP, BLK, CUT), BF),
            in_specs=[SMEM] * 2 + [HBM] * SIDE,
            out_specs=VMEM,
            scratch_shapes=[pltpu.SemaphoreType.DMA],
            name="hand",
        )(me, partner, *arrived[part])
        handed.append(swap(given))
    return pl.pallas_call(
        lambda *refs: attend_kernel(True, True, *refs),
        out_shape=jax.ShapeDtypeStruct(query_tokens.shape, BF),
        in_specs=[SMEM] * 3 + [VMEM] * 4 + [HBM] * 15,
        out_specs=VMEM,
        scratch_shapes=[
            pltpu.SMEM((items,), I32),
            pltpu.SMEM((items,), I32),
            pltpu.SMEM((items * GROUP,), I32),
            pltpu.VMEM((2, ITEM, WIDTH), BF),
            pltpu.VMEM((2, ITEM, WIDTH), BF),
            pltpu.VMEM((2, WIDTH, ITEM), BF),
            pltpu.SemaphoreType.DMA((2,)),
            pltpu.VMEM((blocks, 8, 2 * BLK), F32),
            pltpu.VMEM((blocks, 8, 2 * BLK), F32),
            pltpu.VMEM((blocks, WIDTH, BLK), F32),
        ],
        name="attend",
    )(
        me,
        table,
        counts,
        spread,
        w_keys,
        w_values,
        w_out,
        *[a for part in arrived for a in part],
        *handed,
    )


def solution(mesh):
    placed = (
        P(("pb", "ka"), None),
        P(None, ("pb", "ka"), None),
        P(),
        P(),
        P(),
        P(),
        P(("pb", "ka"), None, None),
        P(("pb", "ka"), None),
    )

    return jax.shard_map(
        on_device, mesh=mesh, in_specs=placed, out_specs=P(("pb", "ka"), None), check_vma=False
    )
```

```python
import jax
import jax.numpy as jnp
from jax import lax
from jax.experimental import pallas as pl
from jax.experimental.pallas import tpu as pltpu
from jax.sharding import PartitionSpec as P


HEADS = 12
HEAD_DIM = 64
BLK = 128
CAP = 6
WIDTH = HEADS * HEAD_DIM
PARTS = 3
CUT = WIDTH // PARTS
SIDE = 4
PAIRS = HEADS // 2
HALVES = 1
SELECT_VMEM = 8 << 20
ROWS = BLK // HALVES
GROUP = 2 * BLK // ROWS
ITEM = GROUP * ROWS
BF = jnp.bfloat16
F32 = jnp.float32
I32 = jnp.int32
STRIDE = (SIDE * SIDE, SIDE, 1)
ROUTES = ((2, 0, 1), (1, 2, 0), (0, 1, 2))
LOG2E = 1.4426950408889634


SMEM = pl.BlockSpec(memory_space=pltpu.SMEM)
VMEM = pl.BlockSpec(memory_space=pltpu.VMEM)
HBM = pl.BlockSpec(memory_space=pltpu.HBM)


def shift(value, axis, step):
    stride = STRIDE[axis]
    pairs = []
    for source in range(SIDE**3):
        at = source // stride % SIDE
        pairs.append((source, source + ((at + step) % SIDE - at) * stride))
    return lax.ppermute(value, "pb", pairs)


def swap(value):
    return lax.ppermute(value, "ka", [(0, 1), (1, 0)])


def table_kernel(blocks, near_ref, count_ref, map_ref, out_ref):
    def clear(i, _):
        for k in range(8):
            out_ref[0, i * 8 + k] = 0
            out_ref[1, i * 8 + k] = -1
        return 0

    lax.fori_loop(0, 16, clear, 0)
    key_blocks = map_ref.shape[1]
    mine = lax.axis_index("pb")
    for slab in range(2):
        for q in range(blocks):
            live = count_ref[q, slab]
            for j in range(CAP):

                @pl.when(j < live)
                def _():
                    entry = near_ref[q, slab, j]
                    one = (entry >= key_blocks).astype(I32)
                    two = (entry >= 2 * key_blocks).astype(I32)
                    contrast = one + two
                    stored = map_ref[contrast, entry - contrast * key_blocks]
                    owner = lax.shift_right_logical(stored, 1)
                    out_ref[0, slab * 64 + owner] = 1 + contrast
                    away = (mine & 48) + 64 - (owner & 48) & 48
                    away = away | ((mine & 12) + 16 - (owner & 12) & 12)
                    away = away | ((mine & 3) + 4 - (owner & 3) & 3)
                    out_ref[1, (slab * blocks + q) * CAP + j] = away


def walk_slots(part, me_ref, table_ref, gathered, outs):
    across, first, second = ROUTES[part]

    def body(low, _):
        for d2 in range(SIDE):
            for high in range(2):
                d1 = high * 2 + low
                at = [None, None, None]
                at[across] = me_ref[across]
                at[first] = me_ref[first] + 4 - d1 & 3
                at[second] = me_ref[second] + 4 - d2 & 3
                place = me_ref[3] * 64 + at[0] * 16 + at[1] * 4 + at[2]
                line = gathered[d2 * 2 + high]
                for d, out in outs:
                    which = table_ref[0 if d == 0 else 3 * part + d, place]
                    begin = pl.multiple_of(jnp.maximum(which - 1, 0) * BLK, BLK)
                    out[d2 * 4 + d1] = line[low, pl.ds(begin, BLK), :]
        return 0

    lax.fori_loop(0, 2, body, 0)


def select_kernel(part, me_ref, table_ref, *refs):
    walk_slots(part, me_ref, table_ref, refs[:8], list(enumerate(refs[8:], 1)))


def own_kernel(me_ref, table_ref, *refs):
    for part in range(PARTS):
        walk_slots(part, me_ref, table_ref, refs[8 * part : 8 * part + 8], [(0, refs[24 + part])])


def spread_kernel(xq_ref, wq_ref, spread):
    low = lax.broadcasted_iota(I32, (BLK, BLK), 1) < HEAD_DIM
    zero = jnp.zeros((BLK, BLK), BF)
    for q in range(xq_ref.shape[0] // BLK):
        queries = jnp.dot(
            xq_ref[q * BLK : (q + 1) * BLK, :], wq_ref[...], preferred_element_type=F32
        ).astype(BF)
        for p in range(PAIRS):
            two = queries[:, p * BLK : (p + 1) * BLK]
            spread[q, p, :BLK, :] = jnp.where(low, two, zero)
            spread[q, p, BLK:, :] = jnp.where(low, zero, two)


def fetch_parts(code, arrived, target, sem_of):
    away = (lax.shift_right_logical(code, 4), lax.shift_right_logical(code, 2) & 3, code & 3)
    for part, (across, first, second) in enumerate(ROUTES):
        for d in range(SIDE):

            @pl.when(away[across] == d)
            def _():
                pltpu.make_async_copy(
                    arrived[part][d].at[away[second] * 4 + away[first]],
                    target(part),
                    sem_of(part),
                ).start()


def hand_kernel(part, me_ref, code_ref, *refs):
    arrived = refs[:SIDE]
    out, sem = refs[SIDE:]
    count = out.shape[0]
    across, first, second = ROUTES[part]
    shifts = (4, 2, 0)

    def start(i, _):
        code = jnp.maximum(code_ref[1, me_ref[3] * count + i], 0)
        away = [lax.shift_right_logical(code, shifts[axis]) & 3 for axis in range(3)]
        for d in range(SIDE):

            @pl.when(away[across] == d)
            def _():
                pltpu.make_async_copy(
                    arrived[d].at[away[second] * 4 + away[first]], out.at[i], sem
                ).start()

        return 0

    lax.fori_loop(0, count, start, 0)
    pltpu.make_async_copy(out, out, sem).wait()


def attend_kernel(first, last, *refs):
    refs = list(refs)
    me_ref, code_ref, count_ref, spread, wk_ref, wvt_ref, wo_ref = refs[:7]
    arrived = [refs[7 + 4 * part : 11 + 4 * part] for part in range(PARTS)]
    handed = refs[19:22]
    refs = refs[22:]
    if not first:
        before = refs[:3]
        refs = refs[3:]
    if last:
        out_ref = refs.pop(0)
        peak, total, sums = refs[-3:]
    else:
        peak, total, sums = refs[:3]
        refs = refs[3:]
    item_q, item_n, item_code, tokens, keys, values, sems = refs[:7]
    blocks = spread.shape[0]
    mine = me_ref[3]
    span = blocks * CAP

    def plan_block(q, begun):
        own = count_ref[q, mine]
        live = own + count_ref[q, 1 - mine]

        def plan_item(k, _):
            t = begun + k
            item_q[t] = q
            item_n[t] = live - GROUP * k
            for g in range(GROUP):
                i = jnp.where(GROUP * k + g < live, GROUP * k + g, GROUP * k)
                near = code_ref[1, mine * span + q * CAP + jnp.minimum(i, own - 1)]
                item_code[t * GROUP + g] = jnp.where(i < own, near, 64 + q * CAP + i - own)
            return 0

        items = lax.div(live + GROUP - 1, GROUP)
        lax.fori_loop(0, items, plan_item, 0)
        return begun + items

    steps = lax.fori_loop(0, blocks, plan_block, 0)

    def fetch(t):
        slot = t & 1
        for g in range(GROUP):
            code = item_code[t * GROUP + g]
            rows = pl.ds(g * ROWS, ROWS)

            @pl.when(code < 64)
            def _():
                fetch_parts(
                    code,
                    arrived,
                    lambda part: tokens.at[slot, rows, pl.ds(part * CUT, CUT)],
                    lambda part: sems.at[slot],
                )

            @pl.when(code >= 64)
            def _():
                for part in range(PARTS):
                    pltpu.make_async_copy(
                        handed[part].at[jnp.maximum(code - 64, 0)],
                        tokens.at[slot, rows, pl.ds(part * CUT, CUT)],
                        sems.at[slot],
                    ).start()

    def landed(slot):
        pltpu.make_async_copy(tokens.at[slot], tokens.at[slot], sems.at[slot]).wait()

    def project(slot, chunk):
        part = pl.ds(chunk % 3 * CUT, CUT)
        if chunk < 3:
            keys[slot, :, part] = jnp.dot(
                tokens[slot], wk_ref[:, part], preferred_element_type=F32
            ).astype(BF)
        else:
            values[slot, part, :] = lax.dot_general(
                wvt_ref[part, :],
                tokens[slot],
                (((1,), (1,)), ((), ())),
                preferred_element_type=F32,
            ).astype(BF)

    fetch(0)
    fetch(1)
    if first:
        peak[...] = jnp.full_like(peak, -jnp.inf)
        total[...] = jnp.zeros_like(total)
        sums[...] = jnp.zeros_like(sums)
    else:
        for mine_ref, old_ref in zip((peak, total, sums), before):
            mine_ref[...] = old_ref[...]
    landed(0)
    for chunk in range(6):
        project(0, chunk)

    def step(t, _):
        slot = t & 1
        q = item_q[t]
        live = item_n[t]

        @pl.when(t + 2 < steps)
        def _():
            fetch(t + 2)

        for g in range(1, GROUP):

            @pl.when(live <= g)
            def _():
                values[slot, :, pl.ds(g * ROWS, ROWS)] = jnp.zeros((WIDTH, ROWS), BF)

        @pl.when(t + 1 < steps)
        def _():
            landed(1 - slot)

        scale = HEAD_DIM**-0.5 * LOG2E

        def score(p):
            return lax.dot_general(
                keys[slot, :, p * BLK : (p + 1) * BLK],
                spread[q, p],
                (((1,), (1,)), ((), ())),
                preferred_element_type=F32,
            )

        ahead = score(0)
        waiting = None
        for p in range(PAIRS + 1):
            scores = ahead
            if p + 1 < PAIRS:
                ahead = score(p + 1)
            if p % 2 == 0 and p < PAIRS:
                project(1 - slot, p // 2)
                project(1 - slot, 3 + p // 2)
            if waiting is not None:
                weights, factor = waiting
                top = (p - 1) * BLK
                mid = top + HEAD_DIM
                end = top + BLK
                mixed = jnp.dot(values[slot, top:end, :], weights, preferred_element_type=F32)
                sums[q, top:mid, :] = (
                    sums[q, top:mid, :] * factor[:, :BLK] + mixed[:HEAD_DIM, :BLK]
                )
                sums[q, mid:end, :] = (
                    sums[q, mid:end, :] * factor[:, BLK:] + mixed[HEAD_DIM:, BLK:]
                )
            if p < PAIRS:
                old = peak[q, p : p + 1, :]
                new = jnp.maximum(old, jnp.max(scores, axis=0, keepdims=True))
                expo = jnp.exp2((scores - new) * scale)
                factor = jnp.exp2((old - new) * scale)
                peak[q, p : p + 1, :] = new
                add = total[q, p : p + 1, :] * factor
                for g in range(GROUP):
                    some = jnp.sum(expo[g * ROWS : (g + 1) * ROWS], axis=0, keepdims=True)
                    add = add + (some if g == 0 else jnp.where(g < live, some, 0.0))
                total[q, p : p + 1, :] = add
                waiting = (expo.astype(BF), factor)
        return 0

    lax.fori_loop(0, steps, step, 0)
    if last:
        for q in range(blocks):
            done = []
            for p in range(PAIRS):
                for h in range(2):
                    top = p * BLK + h * HEAD_DIM
                    done.append(
                        sums[q, top : top + HEAD_DIM, :]
                        / total[q, p : p + 1, h * BLK : (h + 1) * BLK]
                    )
            attended = jnp.transpose(jnp.concatenate(done, axis=0)).astype(BF)
            out_ref[q * BLK : (q + 1) * BLK, :] = jnp.dot(
                attended, wo_ref[...], preferred_element_type=F32
            ).astype(BF)


def on_device(query_tokens, source_tokens, w_query, w_keyval, w_out, slab_map, neighbours, counts):
    blocks = neighbours.shape[0]
    place = lax.axis_index("pb").astype(I32)
    me = jnp.stack(
        [place // 16, place // 4 % 4, place % 4, lax.axis_index("ka").astype(I32)]
    )
    table = pl.pallas_call(
        lambda *refs: table_kernel(blocks, *refs),
        out_shape=jax.ShapeDtypeStruct((2, 128), I32),
        in_specs=[SMEM] * 3,
        out_specs=SMEM,
        name="tables",
    )(neighbours, counts, slab_map)
    note = jnp.pad(table[:1].astype(BF), ((0, 15), (0, CUT - 128)))
    tall = PARTS * BLK
    heard = []
    lines = []
    for part, (_, axis, _) in enumerate(ROUTES):
        own = source_tokens[:, :, part * CUT : (part + 1) * CUT].reshape(tall, CUT)
        own = jnp.concatenate([own, note])
        right, left = shift(own, axis, 1), shift(own, axis, -1)
        told = [own, right, shift(right, axis, 1), left]
        heard.append(told)
        lines.append((jnp.stack(told[:2]), jnp.stack(told[2:])))
    source = {first: part for part, (_, first, _) in enumerate(ROUTES)}
    told = [heard[source[across]][SIDE - d] for across, _, _ in ROUTES for d in range(1, SIDE)]
    small = pltpu.CompilerParams(vmem_limit_bytes=SELECT_VMEM)
    notes = jnp.concatenate([t[tall : tall + 1, :128] for t in told]).astype(I32)
    wishes = jnp.concatenate([table[:1], notes, table[1:]])
    partner = swap(wishes)
    wishes = wishes + partner
    partner = partner[9:11]

    w_keys = w_keyval[:, :WIDTH]
    w_values = jnp.transpose(w_keyval[:, WIDTH:])
    wishes, w_keys, w_values = lax.optimization_barrier((wishes, w_keys, w_values))
    slots = jax.ShapeDtypeStruct((SIDE * SIDE, BLK, CUT), BF)
    gathered = []
    arrived = []
    for part, (across, _, axis) in enumerate(ROUTES):
        right = [shift(half, axis, 1) for half in lines[part]]
        left = [shift(half, axis, -1) for half in lines[part]]
        far = [shift(right[0], axis, 1), shift(left[1], axis, -1)]
        gathered.append([*lines[part], *right, *far, *left])
        chosen = pl.pallas_call(
            lambda *refs: select_kernel(part, *refs),
            out_shape=[slots] * (SIDE - 1),
            in_specs=[SMEM] * 2 + [VMEM] * 8,
            out_specs=[VMEM] * (SIDE - 1),
            compiler_params=small,
            name="select",
        )(me, wishes, *gathered[part])
        arrived.append([shift(chosen[d - 1], across, d) for d in range(1, SIDE)])
    own_slots = pl.pallas_call(
        own_kernel,
        out_shape=[slots] * PARTS,
        in_specs=[SMEM] * 2 + [VMEM] * 24,
        out_specs=[VMEM] * PARTS,
        compiler_params=small,
        name="own",
    )(me, wishes, *[a for part in gathered for a in part])
    spread = pl.pallas_call(
        spread_kernel,
        out_shape=jax.ShapeDtypeStruct((blocks, PAIRS, 2 * BLK, BLK), BF),
        in_specs=[VMEM] * 2,
        out_specs=VMEM,
        compiler_params=small,
        name="spread",
    )(query_tokens, w_query)
    arrived = [[own_slots[part]] + arrived[part] for part in range(PARTS)]
    items = blocks * -(-2 * CAP // GROUP)
    handed = []
    for part in range(PARTS):
        given = pl.pallas_call(
            lambda *refs: hand_kernel(part, *refs),
            out_shape=jax.ShapeDtypeStruct((blocks * CAP, BLK, CUT), BF),
            in_specs=[SMEM] * 2 + [HBM] * SIDE,
            out_specs=VMEM,
            scratch_shapes=[pltpu.SemaphoreType.DMA],
            name="hand",
        )(me, partner, *arrived[part])
        handed.append(swap(given))
    return pl.pallas_call(
        lambda *refs: attend_kernel(True, True, *refs),
        out_shape=jax.ShapeDtypeStruct(query_tokens.shape, BF),
        in_specs=[SMEM] * 3 + [VMEM] * 4 + [HBM] * 15,
        out_specs=VMEM,
        scratch_shapes=[
            pltpu.SMEM((items,), I32),
            pltpu.SMEM((items,), I32),
            pltpu.SMEM((items * GROUP,), I32),
            pltpu.VMEM((2, ITEM, WIDTH), BF),
            pltpu.VMEM((2, ITEM, WIDTH), BF),
            pltpu.VMEM((2, WIDTH, ITEM), BF),
            pltpu.SemaphoreType.DMA((2,)),
            pltpu.VMEM((blocks, 8, 2 * BLK), F32),
            pltpu.VMEM((blocks, 8, 2 * BLK), F32),
            pltpu.VMEM((blocks, WIDTH, BLK), F32),
        ],
        name="attend",
    )(
        me,
        table,
        counts,
        spread,
        w_keys,
        w_values,
        w_out,
        *[a for part in arrived for a in part],
        *handed,
    )


def solution(mesh):
    placed = (
        P(("pb", "ka"), None),
        P(None, ("pb", "ka"), None),
        P(),
        P(),
        P(),
        P(),
        P(("pb", "ka"), None, None),
        P(("pb", "ka"), None),
    )

    return jax.shard_map(
        on_device, mesh=mesh, in_specs=placed, out_specs=P(("pb", "ka"), None), check_vma=False
    )
```

```python
import jax
import jax.numpy as jnp
from jax import lax
from jax.experimental import pallas as pl
from jax.experimental.pallas import tpu as pltpu
from jax.sharding import PartitionSpec as P


HEADS = 12
HEAD_DIM = 64
BLK = 128
CAP = 6
WIDTH = HEADS * HEAD_DIM
PARTS = 3
CUT = WIDTH // PARTS
SIDE = 4
PAIRS = HEADS // 2
HALVES = 1
SELECT_VMEM = 8 << 20
ROWS = BLK // HALVES
GROUP = 2 * BLK // ROWS
ITEM = GROUP * ROWS
BF = jnp.bfloat16
F32 = jnp.float32
I32 = jnp.int32
STRIDE = (SIDE * SIDE, SIDE, 1)
ROUTES = ((2, 0, 1), (1, 2, 0), (0, 1, 2))
LOG2E = 1.4426950408889634


SMEM = pl.BlockSpec(memory_space=pltpu.SMEM)
VMEM = pl.BlockSpec(memory_space=pltpu.VMEM)
HBM = pl.BlockSpec(memory_space=pltpu.HBM)


def shift(value, axis, step):
    stride = STRIDE[axis]
    pairs = []
    for source in range(SIDE**3):
        at = source // stride % SIDE
        pairs.append((source, source + ((at + step) % SIDE - at) * stride))
    return lax.ppermute(value, "pb", pairs)


def swap(value):
    return lax.ppermute(value, "ka", [(0, 1), (1, 0)])


def table_kernel(blocks, near_ref, count_ref, map_ref, out_ref):
    def clear(i, _):
        for k in range(8):
            out_ref[0, i * 8 + k] = 0
            out_ref[1, i * 8 + k] = -1
        return 0

    lax.fori_loop(0, 16, clear, 0)
    key_blocks = map_ref.shape[1]
    mine = lax.axis_index("pb")
    for slab in range(2):
        for q in range(blocks):
            live = count_ref[q, slab]
            for j in range(CAP):

                @pl.when(j < live)
                def _():
                    entry = near_ref[q, slab, j]
                    one = (entry >= key_blocks).astype(I32)
                    two = (entry >= 2 * key_blocks).astype(I32)
                    contrast = one + two
                    stored = map_ref[contrast, entry - contrast * key_blocks]
                    owner = lax.shift_right_logical(stored, 1)
                    out_ref[0, slab * 64 + owner] = 1 + contrast
                    away = (mine & 48) + 64 - (owner & 48) & 48
                    away = away | ((mine & 12) + 16 - (owner & 12) & 12)
                    away = away | ((mine & 3) + 4 - (owner & 3) & 3)
                    out_ref[1, (slab * blocks + q) * CAP + j] = away


def walk_slots(part, me_ref, table_ref, gathered, outs):
    across, first, second = ROUTES[part]
    for d2 in range(SIDE):
        for d1 in range(SIDE):
            at = [None, None, None]
            at[across] = me_ref[across]
            at[first] = me_ref[first] + 4 - d1 & 3
            at[second] = me_ref[second] + 4 - d2 & 3
            place = me_ref[3] * 64 + at[0] * 16 + at[1] * 4 + at[2]
            line, row = gathered[d2 * 2 + d1 // 2], d1 % 2
            for d, out in outs:
                which = table_ref[0 if d == 0 else 3 * part + d, place]
                begin = pl.multiple_of(jnp.maximum(which - 1, 0) * BLK, BLK)
                out[d2 * 4 + d1] = line[row, pl.ds(begin, BLK), :]


def note_kernel(table_ref, *refs):
    out = refs[-1]
    tall = PARTS * BLK
    source = {first: part for part, (_, first, _) in enumerate(ROUTES)}
    out[...] = jnp.zeros_like(out)
    out[0:1, :] = table_ref[0:1, :]
    for part, (across, _, _) in enumerate(ROUTES):
        for d in range(1, SIDE):
            place = source[across] * SIDE + SIDE - d
            note = refs[place // 2][place % 2, tall : tall + 16, :128]
            row = part * 3 + d
            out[row : row + 1, :] = note.astype(F32).astype(I32)[0:1, :]
    out[10:11, :] = table_ref[1:2, :]


def weight_kernel(w_ref, keys_ref, values_ref):
    keys_ref[...] = w_ref[:, :WIDTH]
    values_ref[...] = jnp.transpose(w_ref[:, WIDTH:])


def select_kernel(part, me_ref, table_ref, *refs):
    walk_slots(part, me_ref, table_ref, refs[:8], list(enumerate(refs[8:], 1)))


def own_kernel(me_ref, table_ref, *refs):
    for part in range(PARTS):
        walk_slots(part, me_ref, table_ref, refs[8 * part : 8 * part + 8], [(0, refs[24 + part])])


def spread_kernel(xq_ref, wq_ref, spread):
    low = lax.broadcasted_iota(I32, (BLK, BLK), 1) < HEAD_DIM
    zero = jnp.zeros((BLK, BLK), BF)
    for q in range(xq_ref.shape[0] // BLK):
        queries = jnp.dot(
            xq_ref[q * BLK : (q + 1) * BLK, :], wq_ref[...], preferred_element_type=F32
        ).astype(BF)
        for p in range(PAIRS):
            two = queries[:, p * BLK : (p + 1) * BLK]
            spread[q, p, :BLK, :] = jnp.where(low, two, zero)
            spread[q, p, BLK:, :] = jnp.where(low, zero, two)


def fetch_parts(code, arrived, target, sem_of):
    away = (lax.shift_right_logical(code, 4), lax.shift_right_logical(code, 2) & 3, code & 3)
    for part, (across, first, second) in enumerate(ROUTES):
        for d in range(SIDE):

            @pl.when(away[across] == d)
            def _():
                pltpu.make_async_copy(
                    arrived[part][d].at[away[second] * 4 + away[first]],
                    target(part),
                    sem_of(part),
                ).start()


def hand_kernel(part, me_ref, code_ref, *refs):
    arrived = refs[:SIDE]
    out, sem = refs[SIDE:]
    count = out.shape[0]
    across, first, second = ROUTES[part]
    shifts = (4, 2, 0)

    def start(i, _):
        code = jnp.maximum(code_ref[1, me_ref[3] * count + i], 0)
        away = [lax.shift_right_logical(code, shifts[axis]) & 3 for axis in range(3)]
        for d in range(SIDE):

            @pl.when(away[across] == d)
            def _():
                pltpu.make_async_copy(
                    arrived[d].at[away[second] * 4 + away[first]], out.at[i], sem
                ).start()

        return 0

    lax.fori_loop(0, count, start, 0)
    pltpu.make_async_copy(out, out, sem).wait()


def attend_kernel(first, last, *refs):
    refs = list(refs)
    me_ref, code_ref, count_ref, spread, wk_ref, wvt_ref, wo_ref = refs[:7]
    arrived = [refs[7 + 4 * part : 11 + 4 * part] for part in range(PARTS)]
    handed = refs[19:22]
    refs = refs[22:]
    if not first:
        before = refs[:3]
        refs = refs[3:]
    if last:
        out_ref = refs.pop(0)
        peak, total, sums = refs[-3:]
    else:
        peak, total, sums = refs[:3]
        refs = refs[3:]
    item_q, item_n, item_code, tokens, keys, values, sems = refs[:7]
    blocks = spread.shape[0]
    mine = me_ref[3]
    span = blocks * CAP

    def plan_block(q, begun):
        own = count_ref[q, mine]
        live = own + count_ref[q, 1 - mine]

        def plan_item(k, _):
            t = begun + k
            item_q[t] = q
            item_n[t] = live - GROUP * k
            for g in range(GROUP):
                i = jnp.where(GROUP * k + g < live, GROUP * k + g, GROUP * k)
                near = code_ref[1, mine * span + q * CAP + jnp.minimum(i, own - 1)]
                item_code[t * GROUP + g] = jnp.where(i < own, near, 64 + q * CAP + i - own)
            return 0

        items = lax.div(live + GROUP - 1, GROUP)
        lax.fori_loop(0, items, plan_item, 0)
        return begun + items

    steps = lax.fori_loop(0, blocks, plan_block, 0)

    def fetch(t):
        slot = t & 1
        for g in range(GROUP):
            code = item_code[t * GROUP + g]
            rows = pl.ds(g * ROWS, ROWS)

            @pl.when(code < 64)
            def _():
                fetch_parts(
                    code,
                    arrived,
                    lambda part: tokens.at[slot, rows, pl.ds(part * CUT, CUT)],
                    lambda part: sems.at[slot],
                )

            @pl.when(code >= 64)
            def _():
                for part in range(PARTS):
                    pltpu.make_async_copy(
                        handed[part].at[jnp.maximum(code - 64, 0)],
                        tokens.at[slot, rows, pl.ds(part * CUT, CUT)],
                        sems.at[slot],
                    ).start()

    def landed(slot):
        pltpu.make_async_copy(tokens.at[slot], tokens.at[slot], sems.at[slot]).wait()

    def project(slot, chunk):
        part = pl.ds(chunk % 3 * CUT, CUT)
        if chunk < 3:
            keys[slot, :, part] = jnp.dot(
                tokens[slot], wk_ref[:, part], preferred_element_type=F32
            ).astype(BF)
        else:
            values[slot, part, :] = lax.dot_general(
                wvt_ref[part, :],
                tokens[slot],
                (((1,), (1,)), ((), ())),
                preferred_element_type=F32,
            ).astype(BF)

    fetch(0)
    fetch(1)
    if first:
        peak[...] = jnp.full_like(peak, -jnp.inf)
        total[...] = jnp.zeros_like(total)
        sums[...] = jnp.zeros_like(sums)
    else:
        for mine_ref, old_ref in zip((peak, total, sums), before):
            mine_ref[...] = old_ref[...]
    landed(0)
    for chunk in range(6):
        project(0, chunk)

    def step(t, _):
        slot = t & 1
        q = item_q[t]
        live = item_n[t]

        @pl.when(t + 2 < steps)
        def _():
            fetch(t + 2)

        for g in range(1, GROUP):

            @pl.when(live <= g)
            def _():
                values[slot, :, pl.ds(g * ROWS, ROWS)] = jnp.zeros((WIDTH, ROWS), BF)

        @pl.when(t + 1 < steps)
        def _():
            landed(1 - slot)

        scale = HEAD_DIM**-0.5 * LOG2E

        def score(p):
            return lax.dot_general(
                keys[slot, :, p * BLK : (p + 1) * BLK],
                spread[q, p],
                (((1,), (1,)), ((), ())),
                preferred_element_type=F32,
            )

        ahead = score(0)
        waiting = None
        for p in range(PAIRS + 1):
            scores = ahead
            if p + 1 < PAIRS:
                ahead = score(p + 1)
            if p % 2 == 0 and p < PAIRS:
                project(1 - slot, p // 2)
                project(1 - slot, 3 + p // 2)
            if waiting is not None:
                weights, factor = waiting
                top = (p - 1) * BLK
                mid = top + HEAD_DIM
                end = top + BLK
                mixed = jnp.dot(values[slot, top:end, :], weights, preferred_element_type=F32)
                sums[q, top:mid, :] = (
                    sums[q, top:mid, :] * factor[:, :BLK] + mixed[:HEAD_DIM, :BLK]
                )
                sums[q, mid:end, :] = (
                    sums[q, mid:end, :] * factor[:, BLK:] + mixed[HEAD_DIM:, BLK:]
                )
            if p < PAIRS:
                old = peak[q, p : p + 1, :]
                new = jnp.maximum(old, jnp.max(scores, axis=0, keepdims=True))
                expo = jnp.exp2((scores - new) * scale)
                factor = jnp.exp2((old - new) * scale)
                peak[q, p : p + 1, :] = new
                add = total[q, p : p + 1, :] * factor
                for g in range(GROUP):
                    some = jnp.sum(expo[g * ROWS : (g + 1) * ROWS], axis=0, keepdims=True)
                    add = add + (some if g == 0 else jnp.where(g < live, some, 0.0))
                total[q, p : p + 1, :] = add
                waiting = (expo.astype(BF), factor)
        return 0

    lax.fori_loop(0, steps, step, 0)
    if last:
        for q in range(blocks):
            done = []
            for p in range(PAIRS):
                for h in range(2):
                    top = p * BLK + h * HEAD_DIM
                    done.append(
                        sums[q, top : top + HEAD_DIM, :]
                        / total[q, p : p + 1, h * BLK : (h + 1) * BLK]
                    )
            attended = jnp.transpose(jnp.concatenate(done, axis=0)).astype(BF)
            out_ref[q * BLK : (q + 1) * BLK, :] = jnp.dot(
                attended, wo_ref[...], preferred_element_type=F32
            ).astype(BF)


def on_device(query_tokens, source_tokens, w_query, w_keyval, w_out, slab_map, neighbours, counts):
    blocks = neighbours.shape[0]
    place = lax.axis_index("pb").astype(I32)
    me = jnp.stack(
        [place // 16, place // 4 % 4, place % 4, lax.axis_index("ka").astype(I32)]
    )
    table = pl.pallas_call(
        lambda *refs: table_kernel(blocks, *refs),
        out_shape=jax.ShapeDtypeStruct((2, 128), I32),
        in_specs=[SMEM] * 3,
        out_specs=SMEM,
        name="tables",
    )(neighbours, counts, slab_map)
    note = jnp.pad(table[:1].astype(BF), ((0, 15), (0, CUT - 128)))
    tall = PARTS * BLK
    lines = []
    for part, (_, axis, _) in enumerate(ROUTES):
        own = source_tokens[:, :, part * CUT : (part + 1) * CUT].reshape(tall, CUT)
        own = jnp.concatenate([own, note])
        right, left = shift(own, axis, 1), shift(own, axis, -1)
        told = [own, right, shift(right, axis, 1), left]
        lines.append((jnp.stack(told[:2]), jnp.stack(told[2:])))
    small = pltpu.CompilerParams(vmem_limit_bytes=SELECT_VMEM)
    wishes = pl.pallas_call(
        note_kernel,
        out_shape=jax.ShapeDtypeStruct((16, 128), I32),
        in_specs=[VMEM] * 7,
        out_specs=VMEM,
        compiler_params=small,
        name="notes",
    )(table, *[half for line in lines for half in line])
    partner = swap(wishes)
    wishes = wishes + partner
    partner = partner[9:11]

    slots = jax.ShapeDtypeStruct((SIDE * SIDE, BLK, CUT), BF)
    gathered = []
    arrived = []
    for part, (across, _, axis) in enumerate(ROUTES):
        right = [shift(half, axis, 1) for half in lines[part]]
        left = [shift(half, axis, -1) for half in lines[part]]
        far = [shift(right[0], axis, 1), shift(left[1], axis, -1)]
        gathered.append([*lines[part], *right, *far, *left])
        chosen = pl.pallas_call(
            lambda *refs: select_kernel(part, *refs),
            out_shape=[slots] * (SIDE - 1),
            in_specs=[SMEM] * 2 + [VMEM] * 8,
            out_specs=[VMEM] * (SIDE - 1),
            compiler_params=small,
            name="select",
        )(me, wishes, *gathered[part])
        arrived.append([shift(chosen[d - 1], across, d) for d in range(1, SIDE)])
    own_slots = pl.pallas_call(
        own_kernel,
        out_shape=[slots] * PARTS,
        in_specs=[SMEM] * 2 + [VMEM] * 24,
        out_specs=[VMEM] * PARTS,
        compiler_params=small,
        name="own",
    )(me, wishes, *[a for part in gathered for a in part])
    spread = pl.pallas_call(
        spread_kernel,
        out_shape=jax.ShapeDtypeStruct((blocks, PAIRS, 2 * BLK, BLK), BF),
        in_specs=[VMEM] * 2,
        out_specs=VMEM,
        compiler_params=small,
        name="spread",
    )(query_tokens, w_query)
    w_keys, w_values = pl.pallas_call(
        weight_kernel,
        out_shape=[jax.ShapeDtypeStruct((WIDTH, WIDTH), BF)] * 2,
        in_specs=[VMEM],
        out_specs=[VMEM] * 2,
        compiler_params=small,
        name="weights",
    )(w_keyval)
    arrived = [[own_slots[part]] + arrived[part] for part in range(PARTS)]
    items = blocks * -(-2 * CAP // GROUP)
    handed = []
    for part in range(PARTS):
        given = pl.pallas_call(
            lambda *refs: hand_kernel(part, *refs),
            out_shape=jax.ShapeDtypeStruct((blocks * CAP, BLK, CUT), BF),
            in_specs=[SMEM] * 2 + [HBM] * SIDE,
            out_specs=VMEM,
            scratch_shapes=[pltpu.SemaphoreType.DMA],
            name="hand",
        )(me, partner, *arrived[part])
        handed.append(swap(given))
    return pl.pallas_call(
        lambda *refs: attend_kernel(True, True, *refs),
        out_shape=jax.ShapeDtypeStruct(query_tokens.shape, BF),
        in_specs=[SMEM] * 3 + [VMEM] * 4 + [HBM] * 15,
        out_specs=VMEM,
        scratch_shapes=[
            pltpu.SMEM((items,), I32),
            pltpu.SMEM((items,), I32),
            pltpu.SMEM((items * GROUP,), I32),
            pltpu.VMEM((2, ITEM, WIDTH), BF),
            pltpu.VMEM((2, ITEM, WIDTH), BF),
            pltpu.VMEM((2, WIDTH, ITEM), BF),
            pltpu.SemaphoreType.DMA((2,)),
            pltpu.VMEM((blocks, 8, 2 * BLK), F32),
            pltpu.VMEM((blocks, 8, 2 * BLK), F32),
            pltpu.VMEM((blocks, WIDTH, BLK), F32),
        ],
        name="attend",
    )(
        me,
        table,
        counts,
        spread,
        w_keys,
        w_values,
        w_out,
        *[a for part in arrived for a in part],
        *handed,
    )


def solution(mesh):
    placed = (
        P(("pb", "ka"), None),
        P(None, ("pb", "ka"), None),
        P(),
        P(),
        P(),
        P(),
        P(("pb", "ka"), None, None),
        P(("pb", "ka"), None),
    )

    return jax.shard_map(
        on_device, mesh=mesh, in_specs=placed, out_specs=P(("pb", "ka"), None), check_vma=False
    )
```

```python
import jax
import jax.numpy as jnp
from jax import lax
from jax.experimental import pallas as pl
from jax.experimental.pallas import tpu as pltpu
from jax.sharding import PartitionSpec as P


HEADS = 12
HEAD_DIM = 64
BLK = 128
CAP = 6
WIDTH = HEADS * HEAD_DIM
PARTS = 3
CUT = WIDTH // PARTS
SIDE = 4
PAIRS = HEADS // 2
HALVES = 1
SELECT_VMEM = 8 << 20
ROWS = BLK // HALVES
GROUP = 2 * BLK // ROWS
ITEM = GROUP * ROWS
BF = jnp.bfloat16
F32 = jnp.float32
I32 = jnp.int32
STRIDE = (SIDE * SIDE, SIDE, 1)
ROUTES = ((2, 0, 1), (1, 2, 0), (0, 1, 2))
LOG2E = 1.4426950408889634


SMEM = pl.BlockSpec(memory_space=pltpu.SMEM)
VMEM = pl.BlockSpec(memory_space=pltpu.VMEM)
HBM = pl.BlockSpec(memory_space=pltpu.HBM)


def shift(value, axis, step):
    stride = STRIDE[axis]
    pairs = []
    for source in range(SIDE**3):
        at = source // stride % SIDE
        pairs.append((source, source + ((at + step) % SIDE - at) * stride))
    return lax.ppermute(value, "pb", pairs)


def swap(value):
    return lax.ppermute(value, "ka", [(0, 1), (1, 0)])


def table_kernel(blocks, near_ref, count_ref, map_ref, out_ref):
    def clear(i, _):
        for k in range(8):
            out_ref[0, i * 8 + k] = 0
            out_ref[1, i * 8 + k] = -1
        return 0

    lax.fori_loop(0, 16, clear, 0)
    key_blocks = map_ref.shape[1]
    mine = lax.axis_index("pb")
    for slab in range(2):
        for q in range(blocks):
            live = count_ref[q, slab]
            for j in range(CAP):

                @pl.when(j < live)
                def _():
                    entry = near_ref[q, slab, j]
                    one = (entry >= key_blocks).astype(I32)
                    two = (entry >= 2 * key_blocks).astype(I32)
                    contrast = one + two
                    stored = map_ref[contrast, entry - contrast * key_blocks]
                    owner = lax.shift_right_logical(stored, 1)
                    out_ref[0, slab * 64 + owner] = 1 + contrast
                    away = (mine & 48) + 64 - (owner & 48) & 48
                    away = away | ((mine & 12) + 16 - (owner & 12) & 12)
                    away = away | ((mine & 3) + 4 - (owner & 3) & 3)
                    out_ref[1, (slab * blocks + q) * CAP + j] = away


def walk_slots(part, me_ref, table_ref, gathered, outs):
    across, first, second = ROUTES[part]
    for d2 in range(SIDE):
        for d1 in range(SIDE):
            at = [None, None, None]
            at[across] = me_ref[across]
            at[first] = me_ref[first] + 4 - d1 & 3
            at[second] = me_ref[second] + 4 - d2 & 3
            place = me_ref[3] * 64 + at[0] * 16 + at[1] * 4 + at[2]
            line, row = gathered[d2 * 2 + d1 // 2], d1 % 2
            for d, out in outs:
                which = table_ref[0 if d == 0 else 3 * part + d, place]
                begin = pl.multiple_of(jnp.maximum(which - 1, 0) * BLK, BLK)
                out[d2 * 4 + d1] = line[row, pl.ds(begin, BLK), :]


def note_kernel(table_ref, *refs):
    out = refs[-1]
    tall = PARTS * BLK
    source = {first: part for part, (_, first, _) in enumerate(ROUTES)}
    out[...] = jnp.zeros_like(out)
    out[0:1, :] = table_ref[0:1, :]
    for part, (across, _, _) in enumerate(ROUTES):
        for d in range(1, SIDE):
            place = source[across] * SIDE + SIDE - d
            note = refs[place // 2][place % 2, tall : tall + 16, :128]
            row = part * 3 + d
            out[row : row + 1, :] = note.astype(F32).astype(I32)[0:1, :]
    out[10:11, :] = table_ref[1:2, :]


def weight_kernel(w_ref, keys_ref, values_ref):
    keys_ref[...] = w_ref[:, :WIDTH]
    values_ref[...] = jnp.transpose(w_ref[:, WIDTH:])


def select_kernel(me_ref, table_ref, *refs):
    for part in range(PARTS):
        outs = list(enumerate(refs[24 + 3 * part : 27 + 3 * part], 1))
        walk_slots(part, me_ref, table_ref, refs[8 * part : 8 * part + 8], outs)


def own_kernel(me_ref, table_ref, *refs):
    for part in range(PARTS):
        walk_slots(part, me_ref, table_ref, refs[8 * part : 8 * part + 8], [(0, refs[24 + part])])


def spread_kernel(xq_ref, wq_ref, spread):
    low = lax.broadcasted_iota(I32, (BLK, BLK), 1) < HEAD_DIM
    zero = jnp.zeros((BLK, BLK), BF)
    for q in range(xq_ref.shape[0] // BLK):
        queries = jnp.dot(
            xq_ref[q * BLK : (q + 1) * BLK, :], wq_ref[...], preferred_element_type=F32
        ).astype(BF)
        for p in range(PAIRS):
            two = queries[:, p * BLK : (p + 1) * BLK]
            spread[q, p, :BLK, :] = jnp.where(low, two, zero)
            spread[q, p, BLK:, :] = jnp.where(low, zero, two)


def fetch_parts(code, arrived, target, sem_of):
    away = (lax.shift_right_logical(code, 4), lax.shift_right_logical(code, 2) & 3, code & 3)
    for part, (across, first, second) in enumerate(ROUTES):
        for d in range(SIDE):

            @pl.when(away[across] == d)
            def _():
                pltpu.make_async_copy(
                    arrived[part][d].at[away[second] * 4 + away[first]],
                    target(part),
                    sem_of(part),
                ).start()


def hand_kernel(part, me_ref, code_ref, *refs):
    arrived = refs[:SIDE]
    out, sem = refs[SIDE:]
    count = out.shape[0]
    across, first, second = ROUTES[part]
    shifts = (4, 2, 0)

    def start(i, _):
        code = jnp.maximum(code_ref[1, me_ref[3] * count + i], 0)
        away = [lax.shift_right_logical(code, shifts[axis]) & 3 for axis in range(3)]
        place = away[second] * 4 + away[first]

        def bring(d):
            pltpu.make_async_copy(arrived[d].at[place], out.at[i], sem).start()
            return 0

        def either(d):
            return lambda: lax.cond(away[across] == d, lambda: bring(d), lambda: bring(d + 1))

        lax.cond(away[across] < 2, either(0), either(2))
        return 0

    lax.fori_loop(0, count, start, 0)
    pltpu.make_async_copy(out, out, sem).wait()


def attend_kernel(first, last, *refs):
    refs = list(refs)
    me_ref, code_ref, count_ref, spread, wk_ref, wvt_ref, wo_ref = refs[:7]
    arrived = [refs[7 + 4 * part : 11 + 4 * part] for part in range(PARTS)]
    handed = refs[19:22]
    refs = refs[22:]
    if not first:
        before = refs[:3]
        refs = refs[3:]
    if last:
        out_ref = refs.pop(0)
        peak, total, sums = refs[-3:]
    else:
        peak, total, sums = refs[:3]
        refs = refs[3:]
    item_q, item_n, item_code, tokens, keys, values, sems = refs[:7]
    blocks = spread.shape[0]
    mine = me_ref[3]
    span = blocks * CAP

    def plan_block(q, begun):
        own = count_ref[q, mine]
        live = own + count_ref[q, 1 - mine]

        def plan_item(k, _):
            t = begun + k
            item_q[t] = q
            item_n[t] = live - GROUP * k
            for g in range(GROUP):
                i = jnp.where(GROUP * k + g < live, GROUP * k + g, GROUP * k)
                near = code_ref[1, mine * span + q * CAP + jnp.minimum(i, own - 1)]
                item_code[t * GROUP + g] = jnp.where(i < own, near, 64 + q * CAP + i - own)
            return 0

        items = lax.div(live + GROUP - 1, GROUP)
        lax.fori_loop(0, items, plan_item, 0)
        return begun + items

    steps = lax.fori_loop(0, blocks, plan_block, 0)

    def fetch(t):
        slot = t & 1
        for g in range(GROUP):
            code = item_code[t * GROUP + g]
            rows = pl.ds(g * ROWS, ROWS)

            @pl.when(code < 64)
            def _():
                fetch_parts(
                    code,
                    arrived,
                    lambda part: tokens.at[slot, rows, pl.ds(part * CUT, CUT)],
                    lambda part: sems.at[slot],
                )

            @pl.when(code >= 64)
            def _():
                for part in range(PARTS):
                    pltpu.make_async_copy(
                        handed[part].at[jnp.maximum(code - 64, 0)],
                        tokens.at[slot, rows, pl.ds(part * CUT, CUT)],
                        sems.at[slot],
                    ).start()

    def landed(slot):
        pltpu.make_async_copy(tokens.at[slot], tokens.at[slot], sems.at[slot]).wait()

    def project(slot, chunk):
        part = pl.ds(chunk % 3 * CUT, CUT)
        if chunk < 3:
            keys[slot, :, part] = jnp.dot(
                tokens[slot], wk_ref[:, part], preferred_element_type=F32
            ).astype(BF)
        else:
            values[slot, part, :] = lax.dot_general(
                wvt_ref[part, :],
                tokens[slot],
                (((1,), (1,)), ((), ())),
                preferred_element_type=F32,
            ).astype(BF)

    fetch(0)
    fetch(1)
    if first:
        peak[...] = jnp.full_like(peak, -jnp.inf)
        total[...] = jnp.zeros_like(total)
        sums[...] = jnp.zeros_like(sums)
    else:
        for mine_ref, old_ref in zip((peak, total, sums), before):
            mine_ref[...] = old_ref[...]
    landed(0)
    for chunk in range(6):
        project(0, chunk)

    def step(t, _):
        slot = t & 1
        q = item_q[t]
        live = item_n[t]

        @pl.when(t + 2 < steps)
        def _():
            fetch(t + 2)

        for g in range(1, GROUP):

            @pl.when(live <= g)
            def _():
                values[slot, :, pl.ds(g * ROWS, ROWS)] = jnp.zeros((WIDTH, ROWS), BF)

        @pl.when(t + 1 < steps)
        def _():
            landed(1 - slot)

        scale = HEAD_DIM**-0.5 * LOG2E

        def score(p):
            return lax.dot_general(
                keys[slot, :, p * BLK : (p + 1) * BLK],
                spread[q, p],
                (((1,), (1,)), ((), ())),
                preferred_element_type=F32,
            )

        ahead = score(0)
        waiting = None
        for p in range(PAIRS + 1):
            scores = ahead
            if p + 1 < PAIRS:
                ahead = score(p + 1)
            if p % 2 == 0 and p < PAIRS:
                project(1 - slot, p // 2)
                project(1 - slot, 3 + p // 2)
            if waiting is not None:
                weights, factor = waiting
                top = (p - 1) * BLK
                mid = top + HEAD_DIM
                end = top + BLK
                mixed = jnp.dot(values[slot, top:end, :], weights, preferred_element_type=F32)
                sums[q, top:mid, :] = (
                    sums[q, top:mid, :] * factor[:, :BLK] + mixed[:HEAD_DIM, :BLK]
                )
                sums[q, mid:end, :] = (
                    sums[q, mid:end, :] * factor[:, BLK:] + mixed[HEAD_DIM:, BLK:]
                )
            if p < PAIRS:
                old = peak[q, p : p + 1, :]
                new = jnp.maximum(old, jnp.max(scores, axis=0, keepdims=True))
                expo = jnp.exp2((scores - new) * scale)
                factor = jnp.exp2((old - new) * scale)
                peak[q, p : p + 1, :] = new
                add = total[q, p : p + 1, :] * factor
                for g in range(GROUP):
                    some = jnp.sum(expo[g * ROWS : (g + 1) * ROWS], axis=0, keepdims=True)
                    add = add + (some if g == 0 else jnp.where(g < live, some, 0.0))
                total[q, p : p + 1, :] = add
                waiting = (expo.astype(BF), factor)
        return 0

    lax.fori_loop(0, steps, step, 0)
    if last:
        for q in range(blocks):
            done = []
            for p in range(PAIRS):
                for h in range(2):
                    top = p * BLK + h * HEAD_DIM
                    done.append(
                        sums[q, top : top + HEAD_DIM, :]
                        / total[q, p : p + 1, h * BLK : (h + 1) * BLK]
                    )
            attended = jnp.transpose(jnp.concatenate(done, axis=0)).astype(BF)
            out_ref[q * BLK : (q + 1) * BLK, :] = jnp.dot(
                attended, wo_ref[...], preferred_element_type=F32
            ).astype(BF)


def on_device(query_tokens, source_tokens, w_query, w_keyval, w_out, slab_map, neighbours, counts):
    blocks = neighbours.shape[0]
    place = lax.axis_index("pb").astype(I32)
    me = jnp.stack(
        [place // 16, place // 4 % 4, place % 4, lax.axis_index("ka").astype(I32)]
    )
    table = pl.pallas_call(
        lambda *refs: table_kernel(blocks, *refs),
        out_shape=jax.ShapeDtypeStruct((2, 128), I32),
        in_specs=[SMEM] * 3,
        out_specs=SMEM,
        name="tables",
    )(neighbours, counts, slab_map)
    note = jnp.pad(table[:1].astype(BF), ((0, 15), (0, CUT - 128)))
    tall = PARTS * BLK
    lines = []
    for part, (_, axis, _) in enumerate(ROUTES):
        own = source_tokens[:, :, part * CUT : (part + 1) * CUT].reshape(tall, CUT)
        own = jnp.concatenate([own, note])
        right, left = shift(own, axis, 1), shift(own, axis, -1)
        told = [own, right, shift(right, axis, 1), left]
        lines.append((jnp.stack(told[:2]), jnp.stack(told[2:])))
    small = pltpu.CompilerParams(vmem_limit_bytes=SELECT_VMEM)
    wishes = pl.pallas_call(
        note_kernel,
        out_shape=jax.ShapeDtypeStruct((16, 128), I32),
        in_specs=[VMEM] * 7,
        out_specs=VMEM,
        compiler_params=small,
        name="notes",
    )(table, *[half for line in lines for half in line])
    partner = swap(wishes)
    wishes = wishes + partner
    partner = partner[9:11]

    slots = jax.ShapeDtypeStruct((SIDE * SIDE, BLK, CUT), BF)
    gathered = []
    arrived = []
    for part, (across, _, axis) in enumerate(ROUTES):
        right = [shift(half, axis, 1) for half in lines[part]]
        left = [shift(half, axis, -1) for half in lines[part]]
        far = [shift(right[0], axis, 1), shift(left[1], axis, -1)]
        gathered.append([*lines[part], *right, *far, *left])
    chosen = pl.pallas_call(
        select_kernel,
        out_shape=[slots] * 9,
        in_specs=[SMEM] * 2 + [VMEM] * 24,
        out_specs=[VMEM] * 9,
        compiler_params=pltpu.CompilerParams(vmem_limit_bytes=2 * SELECT_VMEM),
        name="select",
    )(me, wishes, *[a for part in gathered for a in part])
    for part, (across, _, _) in enumerate(ROUTES):
        arrived.append([shift(chosen[3 * part + d - 1], across, d) for d in range(1, SIDE)])
    own_slots = pl.pallas_call(
        own_kernel,
        out_shape=[slots] * PARTS,
        in_specs=[SMEM] * 2 + [VMEM] * 24,
        out_specs=[VMEM] * PARTS,
        compiler_params=small,
        name="own",
    )(me, wishes, *[a for part in gathered for a in part])
    spread = pl.pallas_call(
        spread_kernel,
        out_shape=jax.ShapeDtypeStruct((blocks, PAIRS, 2 * BLK, BLK), BF),
        in_specs=[VMEM] * 2,
        out_specs=VMEM,
        compiler_params=small,
        name="spread",
    )(query_tokens, w_query)
    w_keys, w_values = pl.pallas_call(
        weight_kernel,
        out_shape=[jax.ShapeDtypeStruct((WIDTH, WIDTH), BF)] * 2,
        in_specs=[VMEM],
        out_specs=[VMEM] * 2,
        compiler_params=small,
        name="weights",
    )(w_keyval)
    arrived = [[own_slots[part]] + arrived[part] for part in range(PARTS)]
    items = blocks * -(-2 * CAP // GROUP)
    handed = []
    for part in range(PARTS):
        given = pl.pallas_call(
            lambda *refs: hand_kernel(part, *refs),
            out_shape=jax.ShapeDtypeStruct((blocks * CAP, BLK, CUT), BF),
            in_specs=[SMEM] * 2 + [HBM] * SIDE,
            out_specs=VMEM,
            scratch_shapes=[pltpu.SemaphoreType.DMA],
            name="hand",
        )(me, partner, *arrived[part])
        handed.append(swap(given))
    return pl.pallas_call(
        lambda *refs: attend_kernel(True, True, *refs),
        out_shape=jax.ShapeDtypeStruct(query_tokens.shape, BF),
        in_specs=[SMEM] * 3 + [VMEM] * 4 + [HBM] * 15,
        out_specs=VMEM,
        scratch_shapes=[
            pltpu.SMEM((items,), I32),
            pltpu.SMEM((items,), I32),
            pltpu.SMEM((items * GROUP,), I32),
            pltpu.VMEM((2, ITEM, WIDTH), BF),
            pltpu.VMEM((2, ITEM, WIDTH), BF),
            pltpu.VMEM((2, WIDTH, ITEM), BF),
            pltpu.SemaphoreType.DMA((2,)),
            pltpu.VMEM((blocks, 8, 2 * BLK), F32),
            pltpu.VMEM((blocks, 8, 2 * BLK), F32),
            pltpu.VMEM((blocks, WIDTH, BLK), F32),
        ],
        name="attend",
    )(
        me,
        table,
        counts,
        spread,
        w_keys,
        w_values,
        w_out,
        *[a for part in arrived for a in part],
        *handed,
    )


def solution(mesh):
    placed = (
        P(("pb", "ka"), None),
        P(None, ("pb", "ka"), None),
        P(),
        P(),
        P(),
        P(),
        P(("pb", "ka"), None, None),
        P(("pb", "ka"), None),
    )

    return jax.shard_map(
        on_device, mesh=mesh, in_specs=placed, out_specs=P(("pb", "ka"), None), check_vma=False
    )
```

```python
import jax
import jax.numpy as jnp
from jax import lax
from jax.experimental import pallas as pl
from jax.experimental.pallas import tpu as pltpu
from jax.sharding import PartitionSpec as P


HEADS = 12
HEAD_DIM = 64
BLK = 128
CAP = 6
WIDTH = HEADS * HEAD_DIM
PARTS = 3
CUT = WIDTH // PARTS
SIDE = 4
PAIRS = HEADS // 2
HALVES = 1
SELECT_VMEM = 8 << 20
ROWS = BLK // HALVES
GROUP = 2 * BLK // ROWS
ITEM = GROUP * ROWS
BF = jnp.bfloat16
F32 = jnp.float32
I32 = jnp.int32
STRIDE = (SIDE * SIDE, SIDE, 1)
ROUTES = ((2, 0, 1), (1, 2, 0), (0, 1, 2))
LOG2E = 1.4426950408889634


SMEM = pl.BlockSpec(memory_space=pltpu.SMEM)
VMEM = pl.BlockSpec(memory_space=pltpu.VMEM)
HBM = pl.BlockSpec(memory_space=pltpu.HBM)


def shift(value, axis, step):
    stride = STRIDE[axis]
    pairs = []
    for source in range(SIDE**3):
        at = source // stride % SIDE
        pairs.append((source, source + ((at + step) % SIDE - at) * stride))
    return lax.ppermute(value, "pb", pairs)


def swap(value):
    return lax.ppermute(value, "ka", [(0, 1), (1, 0)])


def table_kernel(blocks, near_ref, count_ref, map_ref, out_ref):
    def clear(i, _):
        for k in range(8):
            out_ref[0, i * 8 + k] = 0
            out_ref[1, i * 8 + k] = -1
        return 0

    lax.fori_loop(0, 16, clear, 0)
    key_blocks = map_ref.shape[1]
    mine = lax.axis_index("pb")
    for slab in range(2):
        for q in range(blocks):
            live = count_ref[q, slab]
            for j in range(CAP):

                @pl.when(j < live)
                def _():
                    entry = near_ref[q, slab, j]
                    one = (entry >= key_blocks).astype(I32)
                    two = (entry >= 2 * key_blocks).astype(I32)
                    contrast = one + two
                    stored = map_ref[contrast, entry - contrast * key_blocks]
                    owner = lax.shift_right_logical(stored, 1)
                    out_ref[0, slab * 64 + owner] = 1 + contrast
                    away = (mine & 48) + 64 - (owner & 48) & 48
                    away = away | ((mine & 12) + 16 - (owner & 12) & 12)
                    away = away | ((mine & 3) + 4 - (owner & 3) & 3)
                    out_ref[1, (slab * blocks + q) * CAP + j] = away


def walk_slots(part, me_ref, table_ref, gathered, outs):
    across, first, second = ROUTES[part]
    for d2 in range(SIDE):
        for d1 in range(SIDE):
            at = [None, None, None]
            at[across] = me_ref[across]
            at[first] = me_ref[first] + 4 - d1 & 3
            at[second] = me_ref[second] + 4 - d2 & 3
            place = me_ref[3] * 64 + at[0] * 16 + at[1] * 4 + at[2]
            line, row = gathered[d2 * 2 + d1 // 2], d1 % 2
            for d, out in outs:
                which = table_ref[0 if d == 0 else 3 * part + d, place]
                begin = pl.multiple_of(jnp.maximum(which - 1, 0) * BLK, BLK)
                out[d2 * 4 + d1] = line[row, pl.ds(begin, BLK), :]


def note_kernel(table_ref, *refs):
    out = refs[-1]
    tall = PARTS * BLK
    source = {first: part for part, (_, first, _) in enumerate(ROUTES)}
    out[...] = jnp.zeros_like(out)
    out[0:1, :] = table_ref[0:1, :]
    for part, (across, _, _) in enumerate(ROUTES):
        for d in range(1, SIDE):
            place = source[across] * SIDE + SIDE - d
            note = refs[place // 2][place % 2, tall : tall + 16, :128]
            row = part * 3 + d
            out[row : row + 1, :] = note.astype(F32).astype(I32)[0:1, :]
    out[10:11, :] = table_ref[1:2, :]


def weight_kernel(w_ref, keys_ref, values_ref):
    keys_ref[...] = w_ref[:, :WIDTH]
    values_ref[...] = jnp.transpose(w_ref[:, WIDTH:])


def select_kernel(me_ref, table_ref, *refs):
    outs = refs[24:33]
    stage, sems = refs[33:]
    sends = [
        pltpu.make_async_copy(stage.at[n], out, sems.at[n]) for n, out in enumerate(outs)
    ]
    for part in range(PARTS):
        for d in range(1, SIDE):
            n = 3 * part + d - 1
            walk_slots(part, me_ref, table_ref, refs[8 * part : 8 * part + 8], [(d, stage.at[n])])
            sends[n].start()
    for send in sends:
        send.wait()


def own_kernel(me_ref, table_ref, *refs):
    for part in range(PARTS):
        walk_slots(part, me_ref, table_ref, refs[8 * part : 8 * part + 8], [(0, refs[24 + part])])


def spread_kernel(xq_ref, wq_ref, spread):
    low = lax.broadcasted_iota(I32, (BLK, BLK), 1) < HEAD_DIM
    zero = jnp.zeros((BLK, BLK), BF)
    for q in range(xq_ref.shape[0] // BLK):
        queries = jnp.dot(
            xq_ref[q * BLK : (q + 1) * BLK, :], wq_ref[...], preferred_element_type=F32
        ).astype(BF)
        for p in range(PAIRS):
            two = queries[:, p * BLK : (p + 1) * BLK]
            spread[q, p, :BLK, :] = jnp.where(low, two, zero)
            spread[q, p, BLK:, :] = jnp.where(low, zero, two)


def fetch_parts(code, arrived, target, sem_of):
    away = (lax.shift_right_logical(code, 4), lax.shift_right_logical(code, 2) & 3, code & 3)
    for part, (across, first, second) in enumerate(ROUTES):
        for d in range(SIDE):

            @pl.when(away[across] == d)
            def _():
                pltpu.make_async_copy(
                    arrived[part][d].at[away[second] * 4 + away[first]],
                    target(part),
                    sem_of(part),
                ).start()


def hand_kernel(part, code_ref, *refs):
    arrived = refs[:SIDE]
    out, sem = refs[SIDE:]
    count = out.shape[0]
    across, first, second = ROUTES[part]
    shifts = (4, 2, 0)

    def start(i, _):
        code = jnp.maximum(code_ref[i], 0)
        away = [lax.shift_right_logical(code, shifts[axis]) & 3 for axis in range(3)]
        place = away[second] * 4 + away[first]

        def bring(d):
            pltpu.make_async_copy(arrived[d].at[place], out.at[i], sem).start()
            return 0

        def either(d):
            return lambda: lax.cond(away[across] == d, lambda: bring(d), lambda: bring(d + 1))

        lax.cond(away[across] < 2, either(0), either(2))
        return 0

    lax.fori_loop(0, count, start, 0)
    pltpu.make_async_copy(out, out, sem).wait()


def attend_kernel(first, last, *refs):
    refs = list(refs)
    me_ref, code_ref, count_ref = refs[:3]
    held = refs[3:7]
    arrived = [refs[7 + 4 * part : 11 + 4 * part] for part in range(PARTS)]
    handed = refs[19:22]
    refs = refs[22:]
    if not first:
        before = refs[:3]
        refs = refs[3:]
    if last:
        out_ref = refs.pop(0)
        peak, total, sums = refs[-3:]
    else:
        peak, total, sums = refs[:3]
        refs = refs[3:]
    item_q, item_n, item_code, tokens, keys, values, sems = refs[:7]
    spread, wk_ref, wvt_ref, wo_ref, load_sems = refs[7:12]
    blocks = spread.shape[0]
    loads = [
        pltpu.make_async_copy(source, target, load_sems.at[i])
        for i, (source, target) in enumerate(zip(held, (spread, wk_ref, wvt_ref, wo_ref)))
    ]
    for i in (1, 2, 0, 3):
        loads[i].start()
    mine = me_ref[3]
    span = blocks * CAP

    def plan_block(q, begun):
        own = count_ref[q, mine]
        live = own + count_ref[q, 1 - mine]

        def plan_item(k, _):
            t = begun + k
            item_q[t] = q
            item_n[t] = live - GROUP * k
            for g in range(GROUP):
                i = jnp.where(GROUP * k + g < live, GROUP * k + g, GROUP * k)
                near = code_ref[1, mine * span + q * CAP + jnp.minimum(i, own - 1)]
                item_code[t * GROUP + g] = jnp.where(i < own, near, 64 + q * CAP + i - own)
            return 0

        items = lax.div(live + GROUP - 1, GROUP)
        lax.fori_loop(0, items, plan_item, 0)
        return begun + items

    steps = lax.fori_loop(0, blocks, plan_block, 0)

    def fetch(t):
        slot = t & 1
        for g in range(GROUP):
            code = item_code[t * GROUP + g]
            rows = pl.ds(g * ROWS, ROWS)

            @pl.when(code < 64)
            def _():
                fetch_parts(
                    code,
                    arrived,
                    lambda part: tokens.at[slot, rows, pl.ds(part * CUT, CUT)],
                    lambda part: sems.at[slot],
                )

            @pl.when(code >= 64)
            def _():
                for part in range(PARTS):
                    pltpu.make_async_copy(
                        handed[part].at[jnp.maximum(code - 64, 0)],
                        tokens.at[slot, rows, pl.ds(part * CUT, CUT)],
                        sems.at[slot],
                    ).start()

    def landed(slot):
        pltpu.make_async_copy(tokens.at[slot], tokens.at[slot], sems.at[slot]).wait()

    def project(slot, chunk):
        part = pl.ds(chunk % 3 * CUT, CUT)
        if chunk < 3:
            keys[slot, :, part] = jnp.dot(
                tokens[slot], wk_ref[:, part], preferred_element_type=F32
            ).astype(BF)
        else:
            values[slot, part, :] = lax.dot_general(
                wvt_ref[part, :],
                tokens[slot],
                (((1,), (1,)), ((), ())),
                preferred_element_type=F32,
            ).astype(BF)

    fetch(0)
    fetch(1)
    if first:
        peak[...] = jnp.full_like(peak, -jnp.inf)
        total[...] = jnp.zeros_like(total)
        sums[...] = jnp.zeros_like(sums)
    else:
        for mine_ref, old_ref in zip((peak, total, sums), before):
            mine_ref[...] = old_ref[...]
    loads[1].wait()
    landed(0)
    for chunk in range(3):
        project(0, chunk)
    loads[2].wait()
    for chunk in range(3, 6):
        project(0, chunk)
    loads[0].wait()

    def step(t, _):
        slot = t & 1
        q = item_q[t]
        live = item_n[t]

        @pl.when(t + 2 < steps)
        def _():
            fetch(t + 2)

        for g in range(1, GROUP):

            @pl.when(live <= g)
            def _():
                values[slot, :, pl.ds(g * ROWS, ROWS)] = jnp.zeros((WIDTH, ROWS), BF)

        @pl.when(t + 1 < steps)
        def _():
            landed(1 - slot)

        scale = HEAD_DIM**-0.5 * LOG2E

        def score(p):
            return lax.dot_general(
                keys[slot, :, p * BLK : (p + 1) * BLK],
                spread[q, p],
                (((1,), (1,)), ((), ())),
                preferred_element_type=F32,
            )

        ahead = score(0)
        waiting = None
        for p in range(PAIRS + 1):
            scores = ahead
            if p + 1 < PAIRS:
                ahead = score(p + 1)
            if p % 2 == 0 and p < PAIRS:
                project(1 - slot, p // 2)
                project(1 - slot, 3 + p // 2)
            if waiting is not None:
                weights, factor = waiting
                top = (p - 1) * BLK
                mid = top + HEAD_DIM
                end = top + BLK
                mixed = jnp.dot(values[slot, top:end, :], weights, preferred_element_type=F32)
                sums[q, top:mid, :] = (
                    sums[q, top:mid, :] * factor[:, :BLK] + mixed[:HEAD_DIM, :BLK]
                )
                sums[q, mid:end, :] = (
                    sums[q, mid:end, :] * factor[:, BLK:] + mixed[HEAD_DIM:, BLK:]
                )
            if p < PAIRS:
                old = peak[q, p : p + 1, :]
                new = jnp.maximum(old, jnp.max(scores, axis=0, keepdims=True))
                expo = jnp.exp2((scores - new) * scale)
                factor = jnp.exp2((old - new) * scale)
                peak[q, p : p + 1, :] = new
                add = total[q, p : p + 1, :] * factor
                for g in range(GROUP):
                    some = jnp.sum(expo[g * ROWS : (g + 1) * ROWS], axis=0, keepdims=True)
                    add = add + (some if g == 0 else jnp.where(g < live, some, 0.0))
                total[q, p : p + 1, :] = add
                waiting = (expo.astype(BF), factor)
        return 0

    lax.fori_loop(0, steps, step, 0)
    loads[3].wait()
    if last:
        for q in range(blocks):
            done = []
            for p in range(PAIRS):
                for h in range(2):
                    top = p * BLK + h * HEAD_DIM
                    done.append(
                        sums[q, top : top + HEAD_DIM, :]
                        / total[q, p : p + 1, h * BLK : (h + 1) * BLK]
                    )
            attended = jnp.transpose(jnp.concatenate(done, axis=0)).astype(BF)
            out_ref[q * BLK : (q + 1) * BLK, :] = jnp.dot(
                attended, wo_ref[...], preferred_element_type=F32
            ).astype(BF)


def on_device(query_tokens, source_tokens, w_query, w_keyval, w_out, slab_map, neighbours, counts):
    blocks = neighbours.shape[0]
    place = lax.axis_index("pb").astype(I32)
    me = jnp.stack(
        [place // 16, place // 4 % 4, place % 4, lax.axis_index("ka").astype(I32)]
    )
    table = pl.pallas_call(
        lambda *refs: table_kernel(blocks, *refs),
        out_shape=jax.ShapeDtypeStruct((2, 128), I32),
        in_specs=[SMEM] * 3,
        out_specs=SMEM,
        name="tables",
    )(neighbours, counts, slab_map)
    note = jnp.pad(table[:1].astype(BF), ((0, 15), (0, CUT - 128)))
    tall = PARTS * BLK
    lines = []
    for part, (_, axis, _) in enumerate(ROUTES):
        own = source_tokens[:, :, part * CUT : (part + 1) * CUT].reshape(tall, CUT)
        own = jnp.concatenate([own, note])
        right, left = shift(own, axis, 1), shift(own, axis, -1)
        told = [own, right, shift(right, axis, 1), left]
        lines.append((jnp.stack(told[:2]), jnp.stack(told[2:])))
    small = pltpu.CompilerParams(vmem_limit_bytes=SELECT_VMEM)
    wishes = pl.pallas_call(
        note_kernel,
        out_shape=jax.ShapeDtypeStruct((16, 128), I32),
        in_specs=[VMEM] * 7,
        out_specs=VMEM,
        compiler_params=small,
        name="notes",
    )(table, *[half for line in lines for half in line])
    partner = swap(wishes)
    wishes = wishes + partner
    codes = lax.dynamic_slice(
        partner[10], (lax.axis_index("ka") * blocks * CAP,), (blocks * CAP,)
    )

    slots = jax.ShapeDtypeStruct((SIDE * SIDE, BLK, CUT), BF)
    gathered = []
    arrived = []
    for part, (across, _, axis) in enumerate(ROUTES):
        right = [shift(half, axis, 1) for half in lines[part]]
        left = [shift(half, axis, -1) for half in lines[part]]
        far = [shift(right[0], axis, 1), shift(left[1], axis, -1)]
        gathered.append([*lines[part], *right, *far, *left])
    chosen = pl.pallas_call(
        select_kernel,
        out_shape=[slots] * 9,
        in_specs=[SMEM] * 2 + [VMEM] * 24,
        out_specs=[HBM] * 9,
        scratch_shapes=[
            pltpu.VMEM((9, SIDE * SIDE, BLK, CUT), BF),
            pltpu.SemaphoreType.DMA((9,)),
        ],
        compiler_params=pltpu.CompilerParams(vmem_limit_bytes=2 * SELECT_VMEM),
        name="select",
    )(me, wishes, *[a for part in gathered for a in part])
    for part, (across, _, _) in enumerate(ROUTES):
        arrived.append([shift(chosen[3 * part + d - 1], across, d) for d in range(1, SIDE)])
    own_slots = pl.pallas_call(
        own_kernel,
        out_shape=[slots] * PARTS,
        in_specs=[SMEM] * 2 + [VMEM] * 24,
        out_specs=[VMEM] * PARTS,
        compiler_params=small,
        name="own",
    )(me, wishes, *[a for part in gathered for a in part])
    spread = pl.pallas_call(
        spread_kernel,
        out_shape=jax.ShapeDtypeStruct((blocks, PAIRS, 2 * BLK, BLK), BF),
        in_specs=[VMEM] * 2,
        out_specs=VMEM,
        compiler_params=small,
        name="spread",
    )(query_tokens, w_query)
    w_keys, w_values = pl.pallas_call(
        weight_kernel,
        out_shape=[jax.ShapeDtypeStruct((WIDTH, WIDTH), BF)] * 2,
        in_specs=[VMEM],
        out_specs=[VMEM] * 2,
        compiler_params=small,
        name="weights",
    )(w_keyval)
    arrived = [[own_slots[part]] + arrived[part] for part in range(PARTS)]
    items = blocks * -(-2 * CAP // GROUP)
    handed = []
    for part in range(PARTS):
        given = pl.pallas_call(
            lambda *refs: hand_kernel(part, *refs),
            out_shape=jax.ShapeDtypeStruct((blocks * CAP, BLK, CUT), BF),
            in_specs=[SMEM] + [HBM] * SIDE,
            out_specs=VMEM,
            scratch_shapes=[pltpu.SemaphoreType.DMA],
            name="hand",
        )(codes, *arrived[part])
        handed.append(swap(given))
    return pl.pallas_call(
        lambda *refs: attend_kernel(True, True, *refs),
        out_shape=jax.ShapeDtypeStruct(query_tokens.shape, BF),
        in_specs=[SMEM] * 3 + [HBM] * 19,
        out_specs=VMEM,
        scratch_shapes=[
            pltpu.SMEM((items,), I32),
            pltpu.SMEM((items,), I32),
            pltpu.SMEM((items * GROUP,), I32),
            pltpu.VMEM((2, ITEM, WIDTH), BF),
            pltpu.VMEM((2, ITEM, WIDTH), BF),
            pltpu.VMEM((2, WIDTH, ITEM), BF),
            pltpu.SemaphoreType.DMA((2,)),
            pltpu.VMEM((blocks, PAIRS, 2 * BLK, BLK), BF),
            pltpu.VMEM((WIDTH, WIDTH), BF),
            pltpu.VMEM((WIDTH, WIDTH), BF),
            pltpu.VMEM((WIDTH, WIDTH), BF),
            pltpu.SemaphoreType.DMA((4,)),
            pltpu.VMEM((blocks, 8, 2 * BLK), F32),
            pltpu.VMEM((blocks, 8, 2 * BLK), F32),
            pltpu.VMEM((blocks, WIDTH, BLK), F32),
        ],
        name="attend",
    )(
        me,
        table,
        counts,
        spread,
        w_keys,
        w_values,
        w_out,
        *[a for part in arrived for a in part],
        *handed,
    )


def solution(mesh):
    placed = (
        P(("pb", "ka"), None),
        P(None, ("pb", "ka"), None),
        P(),
        P(),
        P(),
        P(),
        P(("pb", "ka"), None, None),
        P(("pb", "ka"), None),
    )

    return jax.shard_map(
        on_device, mesh=mesh, in_specs=placed, out_specs=P(("pb", "ka"), None), check_vma=False
    )
```

```python
import jax
import jax.numpy as jnp
from jax import lax
from jax.experimental import pallas as pl
from jax.experimental.pallas import tpu as pltpu
from jax.sharding import PartitionSpec as P


HEADS = 12
HEAD_DIM = 64
BLK = 128
CAP = 6
WIDTH = HEADS * HEAD_DIM
PARTS = 3
CUT = WIDTH // PARTS
SIDE = 4
PAIRS = HEADS // 2
HALVES = 1
SELECT_VMEM = 8 << 20
ROWS = BLK // HALVES
GROUP = 2 * BLK // ROWS
ITEM = GROUP * ROWS
BF = jnp.bfloat16
F32 = jnp.float32
I32 = jnp.int32
STRIDE = (SIDE * SIDE, SIDE, 1)
ROUTES = ((2, 0, 1), (1, 2, 0), (0, 1, 2))
LOG2E = 1.4426950408889634


SMEM = pl.BlockSpec(memory_space=pltpu.SMEM)
VMEM = pl.BlockSpec(memory_space=pltpu.VMEM)
HBM = pl.BlockSpec(memory_space=pltpu.HBM)


def shift(value, axis, step):
    stride = STRIDE[axis]
    pairs = []
    for source in range(SIDE**3):
        at = source // stride % SIDE
        pairs.append((source, source + ((at + step) % SIDE - at) * stride))
    return lax.ppermute(value, "pb", pairs)


def swap(value):
    return lax.ppermute(value, "ka", [(0, 1), (1, 0)])


def table_kernel(blocks, near_ref, count_ref, map_ref, out_ref):
    def clear(i, _):
        for k in range(8):
            out_ref[0, i * 8 + k] = 0
            out_ref[1, i * 8 + k] = -1
        return 0

    lax.fori_loop(0, 16, clear, 0)
    key_blocks = map_ref.shape[1]
    mine = lax.axis_index("pb")
    for slab in range(2):
        for q in range(blocks):
            live = count_ref[q, slab]
            for j in range(CAP):

                @pl.when(j < live)
                def _():
                    entry = near_ref[q, slab, j]
                    one = (entry >= key_blocks).astype(I32)
                    two = (entry >= 2 * key_blocks).astype(I32)
                    contrast = one + two
                    stored = map_ref[contrast, entry - contrast * key_blocks]
                    owner = lax.shift_right_logical(stored, 1)
                    out_ref[0, slab * 64 + owner] = 1 + contrast
                    away = (mine & 48) + 64 - (owner & 48) & 48
                    away = away | ((mine & 12) + 16 - (owner & 12) & 12)
                    away = away | ((mine & 3) + 4 - (owner & 3) & 3)
                    out_ref[1, (slab * blocks + q) * CAP + j] = away


def walk_slots(part, me_ref, table_ref, gathered, outs):
    across, first, second = ROUTES[part]
    for d2 in range(SIDE):
        for d1 in range(SIDE):
            at = [None, None, None]
            at[across] = me_ref[across]
            at[first] = me_ref[first] + 4 - d1 & 3
            at[second] = me_ref[second] + 4 - d2 & 3
            place = me_ref[3] * 64 + at[0] * 16 + at[1] * 4 + at[2]
            line, row = gathered[d2 * 2 + d1 // 2], d1 % 2
            for d, out in outs:
                which = table_ref[0 if d == 0 else 3 * part + d, place]
                begin = pl.multiple_of(jnp.maximum(which - 1, 0) * BLK, BLK)
                out[d2 * 4 + d1] = line[row, pl.ds(begin, BLK), :]


def note_kernel(table_ref, *refs):
    out = refs[-1]
    tall = PARTS * BLK
    source = {first: part for part, (_, first, _) in enumerate(ROUTES)}
    out[...] = jnp.zeros_like(out)
    out[0:1, :] = table_ref[0:1, :]
    for part, (across, _, _) in enumerate(ROUTES):
        for d in range(1, SIDE):
            place = source[across] * SIDE + SIDE - d
            note = refs[place // 2][place % 2, tall : tall + 16, :128]
            row = part * 3 + d
            out[row : row + 1, :] = note.astype(F32).astype(I32)[0:1, :]
    out[10:11, :] = table_ref[1:2, :]


def weight_kernel(w_ref, keys_ref, values_ref):
    keys_ref[...] = w_ref[:, :WIDTH]
    values_ref[...] = jnp.transpose(w_ref[:, WIDTH:])


def select_kernel(me_ref, table_ref, *refs):
    outs = refs[24:33]
    stage, sems = refs[33:]
    sends = [
        pltpu.make_async_copy(stage.at[n], out, sems.at[n]) for n, out in enumerate(outs)
    ]
    for part in range(PARTS):
        for d in range(1, SIDE):
            n = 3 * part + d - 1
            walk_slots(part, me_ref, table_ref, refs[8 * part : 8 * part + 8], [(d, stage.at[n])])
            sends[n].start()
    for send in sends:
        send.wait()


def own_kernel(me_ref, table_ref, *refs):
    for part in range(PARTS):
        walk_slots(part, me_ref, table_ref, refs[8 * part : 8 * part + 8], [(0, refs[24 + part])])


def spread_kernel(xq_ref, wq_ref, spread):
    low = lax.broadcasted_iota(I32, (BLK, BLK), 1) < HEAD_DIM
    zero = jnp.zeros((BLK, BLK), BF)
    for q in range(xq_ref.shape[0] // BLK):
        queries = jnp.dot(
            xq_ref[q * BLK : (q + 1) * BLK, :], wq_ref[...], preferred_element_type=F32
        ).astype(BF)
        for p in range(PAIRS):
            two = queries[:, p * BLK : (p + 1) * BLK]
            spread[q, p, :BLK, :] = jnp.where(low, two, zero)
            spread[q, p, BLK:, :] = jnp.where(low, zero, two)


def fetch_parts(code, arrived, target, sem_of):
    away = (lax.shift_right_logical(code, 4), lax.shift_right_logical(code, 2) & 3, code & 3)
    for part, (across, first, second) in enumerate(ROUTES):
        place = away[second] * 4 + away[first]

        def bring(d):
            pltpu.make_async_copy(arrived[part][d].at[place], target(part), sem_of(part)).start()
            return 0

        def either(d):
            return lambda: lax.cond(away[across] == d, lambda: bring(d), lambda: bring(d + 1))

        lax.cond(away[across] < 2, either(0), either(2))


def hand_kernel(part, code_ref, *refs):
    arrived = refs[:SIDE]
    out, sem = refs[SIDE:]
    count = out.shape[0]
    across, first, second = ROUTES[part]
    shifts = (4, 2, 0)

    def start(i, _):
        code = jnp.maximum(code_ref[i], 0)
        away = [lax.shift_right_logical(code, shifts[axis]) & 3 for axis in range(3)]
        place = away[second] * 4 + away[first]

        def bring(d):
            pltpu.make_async_copy(arrived[d].at[place], out.at[i], sem).start()
            return 0

        def either(d):
            return lambda: lax.cond(away[across] == d, lambda: bring(d), lambda: bring(d + 1))

        lax.cond(away[across] < 2, either(0), either(2))
        return 0

    lax.fori_loop(0, count, start, 0)
    pltpu.make_async_copy(out, out, sem).wait()


def attend_kernel(first, last, *refs):
    refs = list(refs)
    me_ref, code_ref, count_ref = refs[:3]
    held = refs[3:7]
    arrived = [refs[7 + 4 * part : 11 + 4 * part] for part in range(PARTS)]
    handed = refs[19:22]
    refs = refs[22:]
    if not first:
        before = refs[:3]
        refs = refs[3:]
    if last:
        out_ref = refs.pop(0)
        peak, total, sums = refs[-3:]
    else:
        peak, total, sums = refs[:3]
        refs = refs[3:]
    item_q, item_n, item_code, tokens, keys, values, sems = refs[:7]
    spread, wk_ref, wvt_ref, wo_ref, load_sems = refs[7:12]
    blocks = spread.shape[0]
    loads = [
        pltpu.make_async_copy(source, target, load_sems.at[i])
        for i, (source, target) in enumerate(zip(held, (spread, wk_ref, wvt_ref, wo_ref)))
    ]
    for i in (1, 2, 0, 3):
        loads[i].start()
    mine = me_ref[3]
    span = blocks * CAP

    def plan_block(q, begun):
        own = count_ref[q, mine]
        live = own + count_ref[q, 1 - mine]

        def plan_item(k, _):
            t = begun + k
            item_q[t] = q
            item_n[t] = live - GROUP * k
            for g in range(GROUP):
                i = jnp.where(GROUP * k + g < live, GROUP * k + g, GROUP * k)
                near = code_ref[1, mine * span + q * CAP + jnp.minimum(i, own - 1)]
                item_code[t * GROUP + g] = jnp.where(i < own, near, 64 + q * CAP + i - own)
            return 0

        items = lax.div(live + GROUP - 1, GROUP)
        lax.fori_loop(0, items, plan_item, 0)
        return begun + items

    steps = lax.fori_loop(0, blocks, plan_block, 0)

    def fetch(t):
        slot = t & 1
        for g in range(GROUP):
            code = item_code[t * GROUP + g]
            rows = pl.ds(g * ROWS, ROWS)

            @pl.when(code < 64)
            def _():
                fetch_parts(
                    code,
                    arrived,
                    lambda part: tokens.at[slot, rows, pl.ds(part * CUT, CUT)],
                    lambda part: sems.at[slot],
                )

            @pl.when(code >= 64)
            def _():
                for part in range(PARTS):
                    pltpu.make_async_copy(
                        handed[part].at[jnp.maximum(code - 64, 0)],
                        tokens.at[slot, rows, pl.ds(part * CUT, CUT)],
                        sems.at[slot],
                    ).start()

    def landed(slot):
        pltpu.make_async_copy(tokens.at[slot], tokens.at[slot], sems.at[slot]).wait()

    def project(slot, chunk):
        part = pl.ds(chunk % 3 * CUT, CUT)
        if chunk < 3:
            keys[slot, :, part] = jnp.dot(
                tokens[slot], wk_ref[:, part], preferred_element_type=F32
            ).astype(BF)
        else:
            values[slot, part, :] = lax.dot_general(
                wvt_ref[part, :],
                tokens[slot],
                (((1,), (1,)), ((), ())),
                preferred_element_type=F32,
            ).astype(BF)

    fetch(0)
    fetch(1)
    if first:
        peak[...] = jnp.full_like(peak, -jnp.inf)
        total[...] = jnp.zeros_like(total)
        sums[...] = jnp.zeros_like(sums)
    else:
        for mine_ref, old_ref in zip((peak, total, sums), before):
            mine_ref[...] = old_ref[...]
    loads[1].wait()
    landed(0)
    for chunk in range(3):
        project(0, chunk)
    loads[2].wait()
    for chunk in range(3, 6):
        project(0, chunk)
    loads[0].wait()

    def step(t, _):
        slot = t & 1
        q = item_q[t]
        live = item_n[t]

        @pl.when(t + 2 < steps)
        def _():
            fetch(t + 2)

        for g in range(1, GROUP):

            @pl.when(live <= g)
            def _():
                values[slot, :, pl.ds(g * ROWS, ROWS)] = jnp.zeros((WIDTH, ROWS), BF)

        @pl.when(t + 1 < steps)
        def _():
            landed(1 - slot)

        scale = HEAD_DIM**-0.5 * LOG2E

        def score(p):
            return lax.dot_general(
                keys[slot, :, p * BLK : (p + 1) * BLK],
                spread[q, p],
                (((1,), (1,)), ((), ())),
                preferred_element_type=F32,
            )

        ahead = score(0)
        waiting = None
        for p in range(PAIRS + 1):
            scores = ahead
            if p + 1 < PAIRS:
                ahead = score(p + 1)
            if p % 2 == 0 and p < PAIRS:
                project(1 - slot, p // 2)
                project(1 - slot, 3 + p // 2)
            if waiting is not None:
                weights, factor = waiting
                top = (p - 1) * BLK
                mid = top + HEAD_DIM
                end = top + BLK
                mixed = jnp.dot(values[slot, top:end, :], weights, preferred_element_type=F32)
                sums[q, top:mid, :] = (
                    sums[q, top:mid, :] * factor[:, :BLK] + mixed[:HEAD_DIM, :BLK]
                )
                sums[q, mid:end, :] = (
                    sums[q, mid:end, :] * factor[:, BLK:] + mixed[HEAD_DIM:, BLK:]
                )
            if p < PAIRS:
                old = peak[q, p : p + 1, :]
                new = jnp.maximum(old, jnp.max(scores, axis=0, keepdims=True))
                expo = jnp.exp2((scores - new) * scale)
                factor = jnp.exp2((old - new) * scale)
                peak[q, p : p + 1, :] = new
                add = total[q, p : p + 1, :] * factor
                for g in range(GROUP):
                    some = jnp.sum(expo[g * ROWS : (g + 1) * ROWS], axis=0, keepdims=True)
                    add = add + (some if g == 0 else jnp.where(g < live, some, 0.0))
                total[q, p : p + 1, :] = add
                waiting = (expo.astype(BF), factor)
        return 0

    lax.fori_loop(0, steps, step, 0)
    loads[3].wait()
    if last:
        for q in range(blocks):
            done = []
            for p in range(PAIRS):
                for h in range(2):
                    top = p * BLK + h * HEAD_DIM
                    done.append(
                        sums[q, top : top + HEAD_DIM, :]
                        / total[q, p : p + 1, h * BLK : (h + 1) * BLK]
                    )
            attended = jnp.transpose(jnp.concatenate(done, axis=0)).astype(BF)
            out_ref[q * BLK : (q + 1) * BLK, :] = jnp.dot(
                attended, wo_ref[...], preferred_element_type=F32
            ).astype(BF)


def on_device(query_tokens, source_tokens, w_query, w_keyval, w_out, slab_map, neighbours, counts):
    blocks = neighbours.shape[0]
    place = lax.axis_index("pb").astype(I32)
    me = jnp.stack(
        [place // 16, place // 4 % 4, place % 4, lax.axis_index("ka").astype(I32)]
    )
    table = pl.pallas_call(
        lambda *refs: table_kernel(blocks, *refs),
        out_shape=jax.ShapeDtypeStruct((2, 128), I32),
        in_specs=[SMEM] * 3,
        out_specs=SMEM,
        name="tables",
    )(neighbours, counts, slab_map)
    note = jnp.pad(table[:1].astype(BF), ((0, 15), (0, CUT - 128)))
    tall = PARTS * BLK
    lines = []
    for part, (_, axis, _) in enumerate(ROUTES):
        own = source_tokens[:, :, part * CUT : (part + 1) * CUT].reshape(tall, CUT)
        own = jnp.concatenate([own, note])
        right, left = shift(own, axis, 1), shift(own, axis, -1)
        told = [own, right, shift(right, axis, 1), left]
        lines.append((jnp.stack(told[:2]), jnp.stack(told[2:])))
    small = pltpu.CompilerParams(vmem_limit_bytes=SELECT_VMEM)
    wishes = pl.pallas_call(
        note_kernel,
        out_shape=jax.ShapeDtypeStruct((16, 128), I32),
        in_specs=[VMEM] * 7,
        out_specs=VMEM,
        compiler_params=small,
        name="notes",
    )(table, *[half for line in lines for half in line])
    partner = swap(wishes)
    wishes = wishes + partner
    codes = lax.dynamic_slice(
        partner[10], (lax.axis_index("ka") * blocks * CAP,), (blocks * CAP,)
    )

    slots = jax.ShapeDtypeStruct((SIDE * SIDE, BLK, CUT), BF)
    gathered = []
    arrived = []
    for part, (across, _, axis) in enumerate(ROUTES):
        right = [shift(half, axis, 1) for half in lines[part]]
        left = [shift(half, axis, -1) for half in lines[part]]
        far = [shift(right[0], axis, 1), shift(left[1], axis, -1)]
        gathered.append([*lines[part], *right, *far, *left])
    chosen = pl.pallas_call(
        select_kernel,
        out_shape=[slots] * 9,
        in_specs=[SMEM] * 2 + [VMEM] * 24,
        out_specs=[HBM] * 9,
        scratch_shapes=[
            pltpu.VMEM((9, SIDE * SIDE, BLK, CUT), BF),
            pltpu.SemaphoreType.DMA((9,)),
        ],
        compiler_params=pltpu.CompilerParams(vmem_limit_bytes=2 * SELECT_VMEM),
        name="select",
    )(me, wishes, *[a for part in gathered for a in part])
    for part, (across, _, _) in enumerate(ROUTES):
        arrived.append([shift(chosen[3 * part + d - 1], across, d) for d in range(1, SIDE)])
    own_slots = pl.pallas_call(
        own_kernel,
        out_shape=[slots] * PARTS,
        in_specs=[SMEM] * 2 + [VMEM] * 24,
        out_specs=[VMEM] * PARTS,
        compiler_params=small,
        name="own",
    )(me, wishes, *[a for part in gathered for a in part])
    spread = pl.pallas_call(
        spread_kernel,
        out_shape=jax.ShapeDtypeStruct((blocks, PAIRS, 2 * BLK, BLK), BF),
        in_specs=[VMEM] * 2,
        out_specs=VMEM,
        compiler_params=small,
        name="spread",
    )(query_tokens, w_query)
    w_keys, w_values = pl.pallas_call(
        weight_kernel,
        out_shape=[jax.ShapeDtypeStruct((WIDTH, WIDTH), BF)] * 2,
        in_specs=[VMEM],
        out_specs=[VMEM] * 2,
        compiler_params=small,
        name="weights",
    )(w_keyval)
    arrived = [[own_slots[part]] + arrived[part] for part in range(PARTS)]
    items = blocks * -(-2 * CAP // GROUP)
    handed = []
    for part in range(PARTS):
        given = pl.pallas_call(
            lambda *refs: hand_kernel(part, *refs),
            out_shape=jax.ShapeDtypeStruct((blocks * CAP, BLK, CUT), BF),
            in_specs=[SMEM] + [HBM] * SIDE,
            out_specs=VMEM,
            scratch_shapes=[pltpu.SemaphoreType.DMA],
            name="hand",
        )(codes, *arrived[part])
        handed.append(swap(given))
    return pl.pallas_call(
        lambda *refs: attend_kernel(True, True, *refs),
        out_shape=jax.ShapeDtypeStruct(query_tokens.shape, BF),
        in_specs=[SMEM] * 3 + [HBM] * 19,
        out_specs=VMEM,
        scratch_shapes=[
            pltpu.SMEM((items,), I32),
            pltpu.SMEM((items,), I32),
            pltpu.SMEM((items * GROUP,), I32),
            pltpu.VMEM((2, ITEM, WIDTH), BF),
            pltpu.VMEM((2, ITEM, WIDTH), BF),
            pltpu.VMEM((2, WIDTH, ITEM), BF),
            pltpu.SemaphoreType.DMA((2,)),
            pltpu.VMEM((blocks, PAIRS, 2 * BLK, BLK), BF),
            pltpu.VMEM((WIDTH, WIDTH), BF),
            pltpu.VMEM((WIDTH, WIDTH), BF),
            pltpu.VMEM((WIDTH, WIDTH), BF),
            pltpu.SemaphoreType.DMA((4,)),
            pltpu.VMEM((blocks, 8, 2 * BLK), F32),
            pltpu.VMEM((blocks, 8, 2 * BLK), F32),
            pltpu.VMEM((blocks, WIDTH, BLK), F32),
        ],
        name="attend",
    )(
        me,
        table,
        counts,
        spread,
        w_keys,
        w_values,
        w_out,
        *[a for part in arrived for a in part],
        *handed,
    )


def solution(mesh):
    placed = (
        P(("pb", "ka"), None),
        P(None, ("pb", "ka"), None),
        P(),
        P(),
        P(),
        P(),
        P(("pb", "ka"), None, None),
        P(("pb", "ka"), None),
    )

    return jax.shard_map(
        on_device, mesh=mesh, in_specs=placed, out_specs=P(("pb", "ka"), None), check_vma=False
    )
```
